32 devices in a mesh: groups: 2 (over y), section: 2 (over x), band: 4 (over z), chan: 2 (over core).
Axes of the slice: x: 2, y: 2, z: 4, core: 2. Of those that a mesh axis runs over, the one named last changes fastest.
Arguments:
- latent: bfloat16 [16, 128, 640], P(('groups', 'band'), None, ('section', 'chan')), parts along dimension 0, may hold values from -6 to 6
- control_hint: bfloat16 [16, 128, 640], P(('groups', 'band'), None, ('section', 'chan')), parts along dimension 0, may hold values from -6 to 6
- control_weight_one: bfloat16 [3, 3, 640, 640], P(None, None, ('section', 'chan')), may hold values from -0.078125 to 0.078125
- control_bias_one: bfloat16 [640], P(('section', 'chan')), may hold values from -3 to 3
- control_weight_two: bfloat16 [3, 3, 640, 640], P(None, None, ('section', 'chan')), may hold values from -0.078125 to 0.078125
- control_bias_two: bfloat16 [640], P(('section', 'chan')), may hold values from -3 to 3
- main_weight_one: bfloat16 [3, 3, 640, 640], P(None, None, ('section', 'chan')), may hold values from -0.078125 to 0.078125
- main_bias_one: bfloat16 [640], P(('section', 'chan')), may hold values from -3 to 3
- main_weight_two: bfloat16 [3, 3, 640, 640], P(None, None, ('section', 'chan')), may hold values from -0.078125 to 0.078125
- main_bias_two: bfloat16 [640], P(('section', 'chan')), may hold values from -3 to 3
- decoder_weight_one: bfloat16 [3, 3, 640, 1280], P(None, None, ('section', 'chan')), may hold values from -0.0546875 to 0.0546875
- decoder_bias_one: bfloat16 [640], P(('section', 'chan')), may hold values from -3 to 3
- decoder_weight_two: bfloat16 [3, 3, 640, 1280], P(None, None, ('section', 'chan')), may hold values from -0.0546875 to 0.0546875
- decoder_bias_two: bfloat16 [640], P(('section', 'chan')), may hold values from -3 to 3
Outputs:
- decoded: bfloat16 [16, 128, 640], P(('groups', 'band'), None, ('section', 'chan')), parts along dimension 0
The draws below stay inside these ranges and needn't reach their ends.
There are 2 independent parts, one for each index of `groups`. The reference program is written for one: setup_inputs(seed, part) draws one part's arguments, and reference() takes and returns one part's arrays. A program takes and returns all parts, laid end to end along the dimension named above; an argument that names none is the same for every part. Nothing has to cross between parts.
All inputs are finite; a program needn't handle non-finite values.
Results may differ from the reference program's by a relative error of at most 0.015.
Values may be sent and summed in bfloat16 or wider, within the bound.
No kernel may reach another device: no remote copies, remote signals or barrier semaphores. Data moves between devices by JAX's collectives and lax.ppermute only.
A program may use at most 64 MiB of HBM per device.

```python
import jax
import jax.numpy as jnp
from jax import lax

C = 640
WIDTH = 128
HEIGHT = 8
CIN = 1280


def block_levels(stream_key, shape, cuts, least, top_value):
    factor_of = 1.0
    for axis_at, blocks in cuts:
        heights = jax.random.uniform(jax.random.fold_in(jax.random.fold_in(stream_key, 6), axis_at), (blocks,), jnp.float32, least / len(cuts), top_value / len(cuts))
        factor_of = factor_of * jnp.repeat(jnp.exp(heights), shape[axis_at] // blocks).reshape((-1,) + (1,) * (len(shape) - 1 - axis_at))
    return factor_of


def centred(rng, shape, deviation, limit, shards=(), dtype=jnp.bfloat16):
    values = jax.random.normal(rng, shape, jnp.float32) * deviation
    if len(shards) > 0:
        values = block_levels(rng, shape, shards, -0.22, 0.18) * values
    return jnp.clip(values, min=-limit, max=limit).astype(dtype)


def setup_inputs(seed: int = 0, part: int = 0) -> dict:
    key_list = jax.random.split(jax.random.key(seed), 15)
    part_keys = jax.random.split(jax.random.fold_in(key_list[14], part), 15)
    latent = centred(part_keys[0], (HEIGHT, WIDTH, C), 1.0, 6.0, ((0, 4), (2, 4)))
    control_hint = centred(part_keys[1], (HEIGHT, WIDTH, C), 1.0, 6.0, ((0, 4), (2, 4)))
    control_weight_one = centred(key_list[2], (3, 3, C, C), (9 * C) ** -0.5, 0.078125, ((2, 4),))
    control_bias_one = centred(key_list[3], (C,), 0.5, 3.0, ((0, 4),))
    control_weight_two = centred(key_list[4], (3, 3, C, C), (9 * C) ** -0.5, 0.078125, ((2, 4),))
    control_bias_two = centred(key_list[5], (C,), 0.5, 3.0, ((0, 4),))
    main_weight_one = centred(key_list[6], (3, 3, C, C), (9 * C) ** -0.5, 0.078125, ((2, 4),))
    main_bias_one = centred(key_list[7], (C,), 0.5, 3.0, ((0, 4),))
    main_weight_two = centred(key_list[8], (3, 3, C, C), (9 * C) ** -0.5, 0.078125, ((2, 4),))
    main_bias_two = centred(key_list[9], (C,), 0.5, 3.0, ((0, 4),))
    decoder_weight_one = centred(key_list[10], (3, 3, C, CIN), (9 * CIN) ** -0.5, 0.0546875, ((2, 4),))
    decoder_bias_one = centred(key_list[11], (C,), 0.5, 3.0, ((0, 4),))
    decoder_weight_two = centred(key_list[12], (3, 3, C, CIN), (9 * CIN) ** -0.5, 0.0546875, ((2, 4),))
    decoder_bias_two = centred(key_list[13], (C,), 0.5, 3.0, ((0, 4),))
    return {"latent": latent, "control_hint": control_hint, "control_weight_one": control_weight_one, "control_bias_one": control_bias_one, "control_weight_two": control_weight_two, "control_bias_two": control_bias_two, "main_weight_one": main_weight_one, "main_bias_one": main_bias_one, "main_weight_two": main_weight_two, "main_bias_two": main_bias_two, "decoder_weight_one": decoder_weight_one, "decoder_bias_one": decoder_bias_one, "decoder_weight_two": decoder_weight_two, "decoder_bias_two": decoder_bias_two}


def activate(state):
    value = state.astype(jnp.float32)
    return (value * jax.nn.sigmoid(value)).astype(jnp.bfloat16)


def convolve(inputs, weights):
    joined = jnp.concatenate(inputs, axis=2)
    height, breadth, depth = joined.shape
    padded = jnp.pad(joined, ((1, 1), (1, 1), (0, 0)))
    running = jnp.zeros((height * breadth, weights.shape[2]), jnp.float32)
    for row_step in range(3):
        for col_step in range(3):
            window = padded[row_step:row_step + height, col_step:col_step + breadth, :].reshape(height * breadth, depth)
            running = running + lax.dot_general(window, weights[row_step, col_step], (((1,), (1,)), ((), ())), preferred_element_type=jnp.float32)
    return running.reshape(height, breadth, weights.shape[2])


def residual_layer(state, weights, offset, extras):
    activated = activate(state)
    result = convolve((activated,) + extras, weights)
    total = state.astype(jnp.float32) + result + offset.astype(jnp.float32)
    return total.astype(jnp.bfloat16)


def reference(latent, control_hint, control_weight_one, control_bias_one, control_weight_two, control_bias_two, main_weight_one, main_bias_one, main_weight_two, main_bias_two, decoder_weight_one, decoder_bias_one, decoder_weight_two, decoder_bias_two):
    control_input = (latent.astype(jnp.float32) + control_hint.astype(jnp.float32)).astype(jnp.bfloat16)
    control_mid = residual_layer(control_input, control_weight_one, control_bias_one, ())
    control_out = residual_layer(control_mid, control_weight_two, control_bias_two, ())
    main_mid = residual_layer(latent, main_weight_one, main_bias_one, ())
    main_out = residual_layer(main_mid, main_weight_two, main_bias_two, ())
    control_act = activate(control_out)
    decoder_mid = residual_layer(main_out, decoder_weight_one, decoder_bias_one, (control_act,))
    decoded = residual_layer(decoder_mid, decoder_weight_two, decoder_bias_two, (control_act,))
    return decoded
```

```python
import jax
import jax.numpy as jnp
from jax import lax
from jax.sharding import PartitionSpec as P

LAYERS = 4
CHANNEL_AXES = ("section", "chan")


def activate(state):
    value = state.astype(jnp.float32)
    return (value * jax.nn.sigmoid(value)).astype(jnp.bfloat16)


def gather_channels(cells):
    return lax.all_gather(cells, CHANNEL_AXES, axis=cells.ndim - 1, tiled=True)


def convolve(cells, weights):
    return lax.conv_general_dilated(
        cells[None],
        weights,
        (1, 1),
        ((1, 1), (0, 0)),
        dimension_numbers=("NHWC", "HWOI", "NHWC"),
        preferred_element_type=jnp.float32,
    )[0]


def rows_to_columns(cells, halo):
    bands = lax.axis_size("band")
    columns = cells.shape[-2] // bands
    pad = [(0, 0)] * cells.ndim
    pad[-2] = (halo, halo)
    wide = jnp.pad(cells, pad)
    blocks = jnp.stack(
        [
            lax.slice_in_dim(wide, t * columns, (t + 1) * columns + 2 * halo, axis=wide.ndim - 2)
            for t in range(bands)
        ]
    )
    blocks = lax.all_to_all(blocks, "band", 0, 0)
    blocks = jnp.moveaxis(blocks, 0, -4)
    return blocks.reshape(blocks.shape[:-4] + (-1,) + blocks.shape[-2:])


def columns_to_rows(cells):
    bands = lax.axis_size("band")
    rows = cells.shape[0] // bands
    blocks = cells.reshape((bands, rows) + cells.shape[1:])
    blocks = lax.all_to_all(blocks, "band", 0, 0)
    blocks = jnp.moveaxis(blocks, 0, 1)
    return blocks.reshape((rows, -1) + cells.shape[2:])


def per_device(
    latent,
    control_hint,
    control_weight_one,
    control_bias_one,
    control_weight_two,
    control_bias_two,
    main_weight_one,
    main_bias_one,
    main_weight_two,
    main_bias_two,
    decoder_weight_one,
    decoder_bias_one,
    decoder_weight_two,
    decoder_bias_two,
):
    width = latent.shape[1]
    columns = width // lax.axis_size("band")
    first = lax.axis_index("band") * columns

    def masked(cells, halo):
        at = first - halo + jnp.arange(columns + 2 * halo)
        inside = (at >= 0) & (at < width)
        return jnp.where(inside[:, None], cells, jnp.zeros_like(cells))

    def finish(state, result, offset):
        total = state[..., 1:-1, :].astype(jnp.float32) + result + offset.astype(jnp.float32)
        return total.astype(jnp.bfloat16)

    control_input = (latent.astype(jnp.float32) + control_hint.astype(jnp.float32)).astype(
        jnp.bfloat16
    )
    both = rows_to_columns(jnp.stack([control_input, latent]), LAYERS)
    weights = ((control_weight_one, main_weight_one), (control_weight_two, main_weight_two))
    offsets = ((control_bias_one, main_bias_one), (control_bias_two, main_bias_two))
    for step in range(2):
        halo = LAYERS - step
        wide = gather_channels(masked(activate(both), halo))
        both = jnp.stack(
            [
                finish(both[i], convolve(wide[i], weights[step][i]), offsets[step][i])
                for i in range(2)
            ]
        )
    wide = gather_channels(masked(activate(both), 2))
    skip = wide[0]
    joined = jnp.concatenate([wide[1], skip], axis=2)
    state = finish(both[1], convolve(joined, decoder_weight_one), decoder_bias_one)
    wide = gather_channels(masked(activate(state), 1))
    joined = jnp.concatenate([wide, skip[:, 1:-1]], axis=2)
    state = finish(state, convolve(joined, decoder_weight_two), decoder_bias_two)
    return columns_to_rows(state)


def solution(mesh):
    image = P(("groups", "band"), None, CHANNEL_AXES)
    kernel = P(None, None, CHANNEL_AXES, None)
    bias = P(CHANNEL_AXES)
    return jax.shard_map(
        per_device,
        mesh=mesh,
        in_specs=(image, image) + (kernel, bias) * 6,
        out_specs=image,
        check_vma=False,
    )
```

```python
import functools

import jax
import jax.numpy as jnp
from jax import lax
from jax.experimental import pallas as pl
from jax.experimental.pallas import tpu as pltpu
from jax.sharding import PartitionSpec as P

LAYERS = 4
CHANNEL_AXES = ("section", "chan")
F32 = jnp.float32
BF16 = jnp.bfloat16
TRANSPOSED = (((1,), (1,)), ((), ()))


def silu(value):
    return value * jax.nn.sigmoid(value)


def exchange(cells, axis, distance):
    count = lax.axis_size(axis)
    return lax.ppermute(cells, axis, [(i, i ^ distance) for i in range(count)])


def channel_place():
    return lax.axis_index("section") * lax.axis_size("chan") + lax.axis_index("chan")


def channel_count():
    return lax.axis_size("section") * lax.axis_size("chan")


def whole(count):
    return [pl.BlockSpec(memory_space=pltpu.VMEM)] * count


def call(kernel, outs, *args, scratch=(), flops=0):
    many = isinstance(outs, (tuple, list))
    moved = sum(a.size * a.dtype.itemsize for a in args)
    moved += sum(o.size * o.dtype.itemsize for o in (outs if many else [outs]))
    return pl.pallas_call(
        kernel,
        out_shape=outs,
        in_specs=whole(len(args)),
        out_specs=whole(len(outs)) if many else whole(1)[0],
        scratch_shapes=list(scratch),
        compiler_params=pltpu.CompilerParams(vmem_limit_bytes=20 << 20),
        cost_estimate=pl.CostEstimate(flops=flops, bytes_accessed=moved, transcendentals=0),
    )(*args)


def sds(shape, dtype=BF16):
    return jax.ShapeDtypeStruct(shape, dtype)


class Sizes:
    def __init__(self, latent):
        self.bands = lax.axis_size("band")
        self.rows, self.width, self.per = latent.shape
        self.columns = self.width // self.bands
        self.wide = self.columns + 2 * LAYERS
        self.height = self.rows * self.bands
        self.cells = self.height * self.wide
        self.shards = channel_count()
        self.depth = self.shards * self.per


def masked_silu(z, state):
    value = silu(state).reshape(-1, z.wide, z.per)
    at = lax.broadcasted_iota(jnp.int32, value.shape, 1)
    at = at + (lax.axis_index("band") * z.columns - LAYERS)
    value = jnp.where((at >= 0) & (at < z.width), value, 0.0)
    return value.reshape(-1, z.per)


def split_kernel(z, latent_ref, hint_ref, *refs):
    outs, spread = refs[:-1], refs[-1]
    latent = latent_ref[...].astype(F32)
    control = (latent + hint_ref[...].astype(F32)).astype(BF16).astype(F32)
    edge = jnp.zeros((2, z.rows, LAYERS, z.per), F32)
    spread[:, :, :LAYERS] = edge
    spread[:, :, LAYERS + z.width :] = edge
    spread[0, :, LAYERS : LAYERS + z.width] = control
    spread[1, :, LAYERS : LAYERS + z.width] = latent
    band = lax.axis_index("band")
    for k, out in enumerate(outs):
        start = pl.multiple_of((band ^ k) * z.columns, 8)
        block = spread[:, :, pl.ds(start, z.wide)]
        out[...] = block.reshape(2, z.rows * z.wide, z.per).astype(BF16)


def join_kernel(z, *refs):
    blocks, (state_ref, act_ref) = refs[:-2], refs[-2:]
    band = lax.axis_index("band")
    size = z.rows * z.wide
    for k, block in enumerate(blocks):
        start = pl.multiple_of((band ^ k) * size, 16)
        for t in range(2):
            cells = block[t]
            state_ref[t, pl.ds(start, size)] = cells
            act_ref[t, pl.ds(start, size)] = masked_silu(z, cells.astype(F32)).astype(BF16)


def in_order(pieces):
    place = channel_place()
    step = 1
    while step < len(pieces):
        flip = (place & step) != 0
        pieces = [
            jnp.where(flip, pieces[j ^ step], pieces[j]) for j in range(len(pieces))
        ]
        step *= 2
    return pieces


def lay_out(z, a_ref, pieces, at=0):
    for j, piece in enumerate(in_order(pieces)):
        a_ref[:, at + j * z.per : at + (j + 1) * z.per] = piece


def convolve(z, cells, weight, left, right):
    n = z.cells
    left[8 : 8 + n] = lax.dot_general(cells, weight(0), TRANSPOSED, preferred_element_type=F32)
    right[8 : 8 + n] = lax.dot_general(cells, weight(2), TRANSPOSED, preferred_element_type=F32)
    middle = lax.dot_general(cells, weight(1), TRANSPOSED, preferred_element_type=F32)
    total = middle + left[7 : 7 + n] + right[9 : 9 + n]
    row = jnp.zeros((z.wide, z.per), F32)
    above = jnp.concatenate([row, total[: n - z.wide, : z.per]], 0)
    below = jnp.concatenate([total[z.wide :, 2 * z.per :], row], 0)
    return total[:, z.per : 2 * z.per] + above + below


def taps(z, w_ref, start, depth):
    def weight(j):
        return w_ref[:, j, :, start : start + depth].reshape(3 * z.per, depth)

    return weight


def clear_edges(z, left, right):
    left[0:8] = jnp.zeros((8, 3 * z.per), F32)
    right[8 + z.cells : 16 + z.cells] = jnp.zeros((8, 3 * z.per), F32)


def pair_kernel(z, *refs):
    n = z.shards
    blocks, refs = refs[:n], refs[n:]
    state_ref, w0, b0, w1, b1, new_ref, act_ref, a_ref, left, right = refs
    clear_edges(z, left, right)
    for t, (w_ref, b_ref) in enumerate(((w0, b0), (w1, b1))):
        lay_out(z, a_ref, [block[t] for block in blocks])
        result = convolve(z, a_ref[...], taps(z, w_ref, 0, z.depth), left, right)
        total = state_ref[t].astype(F32) + result + b_ref[...].astype(F32)
        new = total.astype(BF16)
        new_ref[t] = new
        act_ref[t] = masked_silu(z, new.astype(F32)).astype(BF16)


def decode_kernel(z, *refs):
    n = z.shards
    blocks, refs = refs[:n], refs[n:]
    state_ref, w_ref, b_ref, new_ref, act_ref, skip_ref, a_ref, left, right = refs
    clear_edges(z, left, right)
    lay_out(z, a_ref, [block[1] for block in blocks])
    lay_out(z, a_ref, [block[0] for block in blocks], z.depth)
    skip_ref[...] = a_ref[:, z.depth :]
    result = convolve(z, a_ref[...], taps(z, w_ref, 0, 2 * z.depth), left, right)
    total = state_ref[1].astype(F32) + result + b_ref[...].astype(F32)
    new = total.astype(BF16)
    new_ref[...] = new
    act_ref[...] = masked_silu(z, new.astype(F32)).astype(BF16)


def skip_kernel(z, skip_ref, w_ref, out_ref, left, right):
    clear_edges(z, left, right)
    out_ref[...] = convolve(z, skip_ref[...], taps(z, w_ref, z.depth, z.depth), left, right)


def last_kernel(z, *refs):
    n = z.shards
    blocks, refs = refs[:n], refs[n:]
    state_ref, skip_ref, w_ref, b_ref = refs[:4]
    outs, (a_ref, left, right, image) = refs[4 : 4 + z.bands], refs[4 + z.bands :]
    clear_edges(z, left, right)
    lay_out(z, a_ref, [block[...] for block in blocks])
    result = convolve(z, a_ref[...], taps(z, w_ref, 0, z.depth), left, right)
    total = state_ref[...].astype(F32) + (result + skip_ref[...]) + b_ref[...].astype(F32)
    image[...] = total.reshape(z.height, z.wide, z.per)
    band = lax.axis_index("band")
    for k, out in enumerate(outs):
        rows = image[pl.ds((band ^ k) * z.rows, z.rows), LAYERS : LAYERS + z.columns]
        out[...] = rows.astype(BF16)


def rows_kernel(z, *refs):
    blocks, (out_ref, image) = refs[:-2], refs[-2:]
    band = lax.axis_index("band")
    for k, block in enumerate(blocks):
        start = pl.multiple_of((band ^ k) * z.columns, 8)
        image[:, pl.ds(start, z.columns)] = block[...].astype(F32)
    out_ref[...] = image[...].astype(BF16)


def over_bands(blocks):
    return [blocks[0]] + [exchange(b, "band", k) for k, b in enumerate(blocks) if k]


def gather(cells):
    chips = [cells] + [exchange(cells, "section", k) for k in range(1, lax.axis_size("section"))]
    cores = range(1, lax.axis_size("chan"))
    pieces = []
    for chip in chips:
        pieces += [chip] + [exchange(chip, "chan", k) for k in cores]
    return pieces


def per_device(latent, control_hint, cw1, cb1, cw2, cb2, mw1, mb1, mw2, mb2, dw1, db1, dw2, db2):
    z = Sizes(latent)
    cb1, cb2, mb1, mb2, db1, db2 = [b.reshape(1, -1) for b in (cb1, cb2, mb1, mb2, db1, db2)]
    kernel = lambda f: functools.partial(f, z)
    edges = [pltpu.VMEM((z.cells + 16, 3 * z.per), F32)] * 2
    work = lambda parts: [pltpu.VMEM((z.cells, parts * z.depth), BF16)] + edges
    unit = 2 * 9 * z.cells * z.per * z.depth

    blocks = call(
        kernel(split_kernel),
        [sds((2, z.rows * z.wide, z.per))] * z.bands,
        latent,
        control_hint,
        scratch=[pltpu.VMEM((2, z.rows, z.width + 2 * LAYERS, z.per), F32)],
    )
    pair = sds((2, z.cells, z.per))
    single = sds((z.cells, z.per))
    state, act = call(kernel(join_kernel), [pair, pair], *over_bands(blocks))
    for weights in ((cw1, cb1, mw1, mb1), (cw2, cb2, mw2, mb2)):
        state, act = call(
            kernel(pair_kernel),
            [pair, pair],
            *gather(act),
            state,
            *weights,
            scratch=work(1),
            flops=2 * unit,
        )
    state, act, skip = call(
        kernel(decode_kernel),
        [single, single, sds((z.cells, z.depth))],
        *gather(act),
        state,
        dw1,
        db1,
        scratch=work(2),
        flops=2 * unit,
    )
    part = call(
        kernel(skip_kernel), sds((z.cells, z.per), F32), skip, dw2, scratch=edges, flops=unit
    )
    blocks = call(
        kernel(last_kernel),
        [sds((z.rows, z.columns, z.per))] * z.bands,
        *gather(act),
        state,
        part,
        dw2,
        db2,
        scratch=work(1) + [pltpu.VMEM((z.height, z.wide, z.per), F32)],
        flops=unit,
    )
    return call(
        kernel(rows_kernel),
        sds((z.rows, z.width, z.per)),
        *over_bands(blocks),
        scratch=[pltpu.VMEM((z.rows, z.width, z.per), F32)],
    )


def solution(mesh):
    image = P(("groups", "band"), None, CHANNEL_AXES)
    kernel = P(None, None, CHANNEL_AXES, None)
    bias = P(CHANNEL_AXES)
    return jax.shard_map(
        per_device,
        mesh=mesh,
        in_specs=(image, image) + (kernel, bias) * 6,
        out_specs=image,
        check_vma=False,
    )
```

```python
import functools

import jax
import jax.numpy as jnp
from jax import lax
from jax.experimental import pallas as pl
from jax.experimental.pallas import tpu as pltpu
from jax.sharding import PartitionSpec as P


LAYERS = 4
LANES = 128
CHANNEL_AXES = ("section", "chan")
F32 = jnp.float32
BF16 = jnp.bfloat16
TRANSPOSED = (((1,), (1,)), ((), ()))


def silu(value):
    return value * jax.nn.sigmoid(value)


def exchange(cells, axis, distance):
    count = lax.axis_size(axis)
    return lax.ppermute(cells, axis, [(i, i ^ distance) for i in range(count)])


def channel_place():
    return lax.axis_index("section") * lax.axis_size("chan") + lax.axis_index("chan")


def channel_count():
    return lax.axis_size("section") * lax.axis_size("chan")


def whole(count):
    return [pl.BlockSpec(memory_space=pltpu.VMEM)] * count


def call(kernel, outs, *args, scratch=(), flops=0):
    many = isinstance(outs, (tuple, list))
    moved = sum(a.size * a.dtype.itemsize for a in args)
    moved += sum(o.size * o.dtype.itemsize for o in (outs if many else [outs]))
    return pl.pallas_call(
        kernel,
        out_shape=outs,
        in_specs=whole(len(args)),
        out_specs=whole(len(outs)) if many else whole(1)[0],
        scratch_shapes=list(scratch),
        compiler_params=pltpu.CompilerParams(vmem_limit_bytes=20 << 20),
        cost_estimate=pl.CostEstimate(flops=flops, bytes_accessed=moved, transcendentals=0),
    )(*args)


def sds(shape, dtype=BF16):
    return jax.ShapeDtypeStruct(shape, dtype)


class Sizes:
    def __init__(self, latent):
        self.bands = lax.axis_size("band")
        self.rows, self.width, self.per = latent.shape
        self.columns = self.width // self.bands
        self.wide = self.columns + 2 * LAYERS
        self.height = self.rows * self.bands
        self.cells = self.height * self.wide
        self.shards = channel_count()
        self.rest = self.per % LANES
        self.groups = LANES // self.rest if self.rest and LANES % self.rest == 0 else 0
        if self.per < LANES:
            self.groups = 0
        self.depth = self.shards * self.per


    def dense(self, cells):
        return self.groups and cells % (8 * self.groups) == 0

    def packed(self, cells):
        if not self.dense(cells):
            return (cells, self.per)
        return (cells * (self.per // LANES) + cells // self.groups, LANES)


def pack(z, ref, value):
    cells = value.shape[0]
    if not z.dense(cells):
        ref[...] = value.astype(BF16)
        return
    full = z.per // LANES
    for g in range(full):
        ref[g * cells : (g + 1) * cells] = value[:, g * LANES : (g + 1) * LANES].astype(BF16)
    part = cells // z.groups
    rest = [value[g * part : (g + 1) * part, full * LANES :] for g in range(z.groups)]
    ref[full * cells :] = jnp.concatenate(rest, axis=1).astype(BF16)


def unpack(z, cells, message, put):
    if not z.dense(cells):
        put(0, 0, message)
        return
    full = z.per // LANES
    for g in range(full):
        put(0, g * LANES, message[g * cells : (g + 1) * cells])
    part = cells // z.groups
    rest = message[full * cells :]
    for g in range(z.groups):
        put(g * part, full * LANES, rest[:, g * z.rest : (g + 1) * z.rest])


def masked_silu(z, state):
    value = silu(state).reshape(-1, z.wide, z.per)
    at = lax.broadcasted_iota(jnp.int32, value.shape, 1)
    at = at + (lax.axis_index("band") * z.columns - LAYERS)
    value = jnp.where((at >= 0) & (at < z.width), value, 0.0)
    return value.reshape(-1, z.per)


def fetch(sources, targets, sems):
    copies = [
        pltpu.make_async_copy(source, target, sems.at[i])
        for i, (source, target) in enumerate(zip(sources, targets))
    ]
    for copy in copies:
        copy.start()
    for copy in copies:
        copy.wait()


def split_kernel(z, latent_hbm, hint_hbm, *refs):
    outs, (latent_ref, hint_ref, spread, sems) = refs[:-4], refs[-4:]
    fetch((latent_hbm, hint_hbm), (latent_ref, hint_ref), sems)
    latent = latent_ref[...].astype(F32)
    control = (latent + hint_ref[...].astype(F32)).astype(BF16).astype(F32)
    edge = jnp.zeros((2, z.rows, LAYERS, z.per), F32)
    spread[:, :, :LAYERS] = edge
    spread[:, :, LAYERS + z.width :] = edge
    spread[0, :, LAYERS : LAYERS + z.width] = control
    spread[1, :, LAYERS : LAYERS + z.width] = latent
    band = lax.axis_index("band")
    for k, out in enumerate(outs):
        start = pl.multiple_of((band ^ k) * z.columns, 8)
        pack(z, out, spread[:, :, pl.ds(start, z.wide)].reshape(-1, z.per))


def in_hbm(array):
    return pltpu.with_memory_space_constraint(array, pltpu.HBM)


def load_kernel(count, *refs):
    fetch(refs[:count], refs[count : 2 * count], refs[2 * count])


def load(*weights):
    count = len(weights)
    return pl.pallas_call(
        functools.partial(load_kernel, count),
        out_shape=[sds(w.shape) for w in weights],
        in_specs=[pl.BlockSpec(memory_space=pltpu.HBM)] * count,
        out_specs=whole(count),
        scratch_shapes=[pltpu.SemaphoreType.DMA((count,))],
        compiler_params=pltpu.CompilerParams(vmem_limit_bytes=1 << 20),
        cost_estimate=pl.CostEstimate(
            flops=0, bytes_accessed=2 * sum(w.size for w in weights), transcendentals=0
        ),
    )(*[in_hbm(w) for w in weights])


def join_kernel(z, *refs):
    blocks, (state_ref, act_ref, image, block_image) = refs[:-4], refs[-4:]
    band = lax.axis_index("band")
    size = z.rows * z.wide

    def put(row, lane, piece):
        rows, lanes = piece.shape
        block_image[row : row + rows, lane : lane + lanes] = piece

    for k, block in enumerate(blocks):
        start = pl.multiple_of((band ^ k) * size, 8)
        unpack(z, 2 * size, block[...].astype(F32), put)
        for t in range(2):
            image[t, pl.ds(start, size)] = block_image[t * size : (t + 1) * size]
    for t in range(2):
        value = image[t]
        state_ref[t] = value.astype(BF16)
        pack(z, act_ref.at[t], masked_silu(z, value))


def in_order(pieces):
    place = channel_place()
    step = 1
    while step < len(pieces):
        flip = (place & step) != 0
        pieces = [
            jnp.where(flip, pieces[j ^ step], pieces[j]) for j in range(len(pieces))
        ]
        step *= 2
    return pieces


def lay_out(z, a_ref, messages, at=0):
    for j, message in enumerate(in_order(messages)):

        def put(row, lane, piece):
            rows, lanes = piece.shape
            lane = at + j * z.per + lane
            a_ref[row : row + rows, lane : lane + lanes] = piece

        unpack(z, z.cells, message, put)


def convolve(z, cells, weight, left, right):
    n = z.cells
    left[8 : 8 + n] = lax.dot_general(cells, weight(0), TRANSPOSED, preferred_element_type=F32)
    right[8 : 8 + n] = lax.dot_general(cells, weight(2), TRANSPOSED, preferred_element_type=F32)
    middle = lax.dot_general(cells, weight(1), TRANSPOSED, preferred_element_type=F32)
    total = middle + left[7 : 7 + n] + right[9 : 9 + n]
    row = jnp.zeros((z.wide, z.per), F32)
    above = jnp.concatenate([row, total[: n - z.wide, : z.per]], 0)
    below = jnp.concatenate([total[z.wide :, 2 * z.per :], row], 0)
    return total[:, z.per : 2 * z.per] + above + below


def taps(z, w_ref, start, depth):
    def weight(j):
        return w_ref[:, j, :, start : start + depth].reshape(3 * z.per, depth)

    return weight


def clear_edges(z, left, right):
    left[0:8] = jnp.zeros((8, 3 * z.per), F32)
    right[8 + z.cells : 16 + z.cells] = jnp.zeros((8, 3 * z.per), F32)


def finish(z, state, result, bias, new_ref, act_ref):
    new = (state.astype(F32) + result + bias).astype(BF16)
    new_ref[...] = new
    pack(z, act_ref, masked_silu(z, new.astype(F32)))


def bias_of(ref):
    return ref[...].astype(F32).reshape(1, -1)


def layer_kernel(z, *refs):
    n = z.shards
    blocks, refs = refs[:n], refs[n:]
    state_ref, w0, b0, w1, b1, new_ref, act_ref, a_ref, left, right = refs
    clear_edges(z, left, right)
    for t, (w_ref, b_ref) in enumerate(((w0, b0), (w1, b1))):
        lay_out(z, a_ref, [block[t] for block in blocks])
        result = convolve(z, a_ref[...], taps(z, w_ref, 0, z.depth), left, right)
        finish(z, state_ref[t], result, bias_of(b_ref), new_ref.at[t], act_ref.at[t])


def decode_kernel(z, *refs):
    n = z.shards
    blocks, refs = refs[:n], refs[n:]
    state_ref, w_ref, b_ref, new_ref, act_ref, skip_ref, a_ref, left, right = refs
    clear_edges(z, left, right)
    lay_out(z, a_ref, [block[1] for block in blocks])
    lay_out(z, a_ref, [block[0] for block in blocks], z.depth)
    skip_ref[...] = a_ref[:, z.depth :]
    result = convolve(z, a_ref[...], taps(z, w_ref, 0, 2 * z.depth), left, right)
    finish(z, state_ref[1], result, bias_of(b_ref), new_ref, act_ref)


def skip_kernel(z, skip_ref, w_ref, out_ref, left, right):
    clear_edges(z, left, right)
    out_ref[...] = convolve(z, skip_ref[...], taps(z, w_ref, z.depth, z.depth), left, right)


def last_kernel(z, *refs):
    n = z.shards
    blocks, refs = refs[:n], refs[n:]
    state_ref, skip_ref, w_ref, b_ref = refs[:4]
    outs, (a_ref, left, right, image) = refs[4 : 4 + z.bands], refs[4 + z.bands :]
    clear_edges(z, left, right)
    lay_out(z, a_ref, [block[...] for block in blocks])
    result = convolve(z, a_ref[...], taps(z, w_ref, 0, z.depth), left, right)
    total = state_ref[...].astype(F32) + (result + skip_ref[...])
    total = total + bias_of(b_ref)
    image[...] = total.reshape(z.height, z.wide, z.per)
    band = lax.axis_index("band")
    for k, out in enumerate(outs):
        rows = image[pl.ds((band ^ k) * z.rows, z.rows), LAYERS : LAYERS + z.columns]
        out[...] = rows.astype(BF16)


def rows_kernel(z, *refs):
    blocks, (out_ref, image) = refs[:-2], refs[-2:]
    band = lax.axis_index("band")
    for k, block in enumerate(blocks):
        start = pl.multiple_of((band ^ k) * z.columns, 8)
        image[:, pl.ds(start, z.columns)] = block[...].astype(F32)
    out_ref[...] = image[...].astype(BF16)


def over_bands(blocks):
    moved = [blocks[0]]
    for k, block in enumerate(blocks):
        if k:
            moved.append(exchange(block, "band", k))
    return moved


def gather(cells):
    chips = [cells]
    for k in range(1, lax.axis_size("section")):
        chips.append(exchange(cells, "section", k))
    pieces = []
    for chip in chips:
        pieces.append(chip)
        for k in range(1, lax.axis_size("chan")):
            pieces.append(exchange(chip, "chan", k))
    return pieces


def per_device(latent, control_hint, cw1, cb1, cw2, cb2, mw1, mb1, mw2, mb2, dw1, db1, dw2, db2):
    z = Sizes(latent)
    kernel = lambda f, *a: functools.partial(f, z, *a)
    edges = [pltpu.VMEM((z.cells + 16, 3 * z.per), F32)] * 2
    work = lambda parts: [pltpu.VMEM((z.cells, parts * z.depth), BF16)] + edges
    unit = 2 * 9 * z.cells * z.per * z.depth
    single = sds((z.cells, z.per))
    pair = sds((2, z.cells, z.per))
    message = z.packed(z.cells)

    raw = (z.rows, z.width, z.per)
    blocks = pl.pallas_call(
        kernel(split_kernel),
        out_shape=[sds(z.packed(2 * z.rows * z.wide))] * z.bands,
        in_specs=[pl.BlockSpec(memory_space=pltpu.HBM)] * 2,
        out_specs=whole(z.bands),
        scratch_shapes=[pltpu.VMEM(raw, BF16)] * 2
        + [
            pltpu.VMEM((2, z.rows, z.width + 2 * LAYERS, z.per), F32),
            pltpu.SemaphoreType.DMA((2,)),
        ],
        compiler_params=pltpu.CompilerParams(vmem_limit_bytes=4 << 20),
    )(in_hbm(latent), in_hbm(control_hint))
    blocks = over_bands(blocks)
    cw1, mw1, cw2, mw2 = load(cw1, mw1, cw2, mw2)
    (dw1,) = load(dw1)
    (dw2,) = load(dw2)
    state, act = call(
        kernel(join_kernel),
        [pair, sds((2,) + message)],
        *blocks,
        scratch=[
            pltpu.VMEM((2, z.cells, z.per), F32),
            pltpu.VMEM((2 * z.rows * z.wide, z.per), F32),
        ],
    )
    for weights in ((cw1, cb1, mw1, mb1), (cw2, cb2, mw2, mb2)):
        state, act = call(
            kernel(layer_kernel),
            [pair, sds((2,) + message)],
            *gather(act),
            state,
            *weights,
            scratch=work(1),
            flops=2 * unit,
        )
    state, act, skip = call(
        kernel(decode_kernel),
        [single, sds(message), sds((z.cells, z.depth))],
        *gather(act),
        state,
        dw1,
        db1,
        scratch=work(2),
        flops=2 * unit,
    )
    part = call(
        kernel(skip_kernel), sds((z.cells, z.per), F32), skip, dw2, scratch=edges, flops=unit
    )
    blocks = call(
        kernel(last_kernel),
        [sds((z.rows, z.columns, z.per))] * z.bands,
        *gather(act),
        state,
        part,
        dw2,
        db2,
        scratch=work(1) + [pltpu.VMEM((z.height, z.wide, z.per), F32)],
        flops=unit,
    )
    return call(
        kernel(rows_kernel),
        sds(raw),
        *over_bands(blocks),
        scratch=[pltpu.VMEM(raw, F32)],
    )


def solution(mesh):
    image = P(("groups", "band"), None, CHANNEL_AXES)
    kernel = P(None, None, CHANNEL_AXES, None)
    bias = P(CHANNEL_AXES)

    return jax.shard_map(
        per_device,
        mesh=mesh,
        in_specs=(image, image) + (kernel, bias) * 6,
        out_specs=image,
        check_vma=False,
    )
```

```python
import functools

import jax
import jax.numpy as jnp
from jax import lax
from jax.experimental import pallas as pl
from jax.experimental.pallas import tpu as pltpu
from jax.sharding import PartitionSpec as P


LAYERS = 4
LANES = 128
CHANNEL_AXES = ("section", "chan")
F32 = jnp.float32
BF16 = jnp.bfloat16
TRANSPOSED = (((1,), (1,)), ((), ()))


def silu(value):
    return value * jax.nn.sigmoid(value)


def exchange(cells, axis, distance):
    count = lax.axis_size(axis)
    return lax.ppermute(cells, axis, [(i, i ^ distance) for i in range(count)])


def channel_place():
    return lax.axis_index("section") * lax.axis_size("chan") + lax.axis_index("chan")


def channel_count():
    return lax.axis_size("section") * lax.axis_size("chan")


def whole(count):
    return [pl.BlockSpec(memory_space=pltpu.VMEM)] * count


def call(kernel, outs, *args, scratch=(), flops=0):
    many = isinstance(outs, (tuple, list))
    moved = sum(a.size * a.dtype.itemsize for a in args)
    moved += sum(o.size * o.dtype.itemsize for o in (outs if many else [outs]))
    return pl.pallas_call(
        kernel,
        out_shape=outs,
        in_specs=whole(len(args)),
        out_specs=whole(len(outs)) if many else whole(1)[0],
        scratch_shapes=list(scratch),
        compiler_params=pltpu.CompilerParams(vmem_limit_bytes=20 << 20),
        cost_estimate=pl.CostEstimate(flops=flops, bytes_accessed=moved, transcendentals=0),
    )(*args)


def sds(shape, dtype=BF16):
    return jax.ShapeDtypeStruct(shape, dtype)


class Sizes:
    def __init__(self, latent):
        self.bands = lax.axis_size("band")
        self.rows, self.width, self.per = latent.shape
        self.columns = self.width // self.bands
        self.wide = self.columns + 2 * LAYERS
        self.height = self.rows * self.bands
        self.cells = self.height * self.wide
        self.shards = channel_count()
        self.rest = self.per % LANES
        self.groups = LANES // self.rest if self.rest and LANES % self.rest == 0 else 0
        if self.per < LANES:
            self.groups = 0
        self.depth = self.shards * self.per


    def dense(self, cells):
        return self.groups and cells % (8 * self.groups) == 0

    def packed(self, cells):
        if not self.dense(cells):
            return (cells, self.per)
        return (cells * (self.per // LANES) + cells // self.groups, LANES)


def pack(z, ref, value):
    cells = value.shape[0]
    if not z.dense(cells):
        ref[...] = value.astype(BF16)
        return
    full = z.per // LANES
    for g in range(full):
        ref[g * cells : (g + 1) * cells] = value[:, g * LANES : (g + 1) * LANES].astype(BF16)
    part = cells // z.groups
    rest = [value[g * part : (g + 1) * part, full * LANES :] for g in range(z.groups)]
    ref[full * cells :] = jnp.concatenate(rest, axis=1).astype(BF16)


def unpack(z, cells, message, put):
    if not z.dense(cells):
        put(0, 0, message)
        return
    full = z.per // LANES
    for g in range(full):
        put(0, g * LANES, message[g * cells : (g + 1) * cells])
    part = cells // z.groups
    rest = message[full * cells :]
    for g in range(z.groups):
        put(g * part, full * LANES, rest[:, g * z.rest : (g + 1) * z.rest])


def masked_silu(z, state):
    value = silu(state).reshape(-1, z.wide, z.per)
    at = lax.broadcasted_iota(jnp.int32, value.shape, 1)
    at = at + (lax.axis_index("band") * z.columns - LAYERS)
    value = jnp.where((at >= 0) & (at < z.width), value, 0.0)
    return value.reshape(-1, z.per)


def fetch(sources, targets, sems):
    copies = [
        pltpu.make_async_copy(source, target, sems.at[i])
        for i, (source, target) in enumerate(zip(sources, targets))
    ]
    for copy in copies:
        copy.start()
    for copy in copies:
        copy.wait()


def split_kernel(z, latent_hbm, hint_hbm, *refs):
    outs, (latent_ref, hint_ref, spread, sems) = refs[:-4], refs[-4:]
    fetch((latent_hbm, hint_hbm), (latent_ref, hint_ref), sems)
    latent = latent_ref[...].astype(F32)
    control = (latent + hint_ref[...].astype(F32)).astype(BF16).astype(F32)
    edge = jnp.zeros((2, z.rows, LAYERS, z.per), F32)
    spread[:, :, :LAYERS] = edge
    spread[:, :, LAYERS + z.width :] = edge
    for row in range(z.rows):
        spread[0, row, LAYERS : LAYERS + z.width] = control[row].T
        spread[1, row, LAYERS : LAYERS + z.width] = latent[row].T
    band = lax.axis_index("band")
    for k, out in enumerate(outs):
        start = pl.multiple_of((band ^ k) * z.columns, 8)
        pack(z, out, spread[:, :, pl.ds(start, z.wide)].reshape(-1, z.per))


def in_hbm(array):
    return pltpu.with_memory_space_constraint(array, pltpu.HBM)


def load_kernel(count, *refs):
    fetch(refs[:count], refs[count : 2 * count], refs[2 * count])


def load(*weights):
    count = len(weights)
    return pl.pallas_call(
        functools.partial(load_kernel, count),
        out_shape=[sds(w.shape) for w in weights],
        in_specs=[pl.BlockSpec(memory_space=pltpu.HBM)] * count,
        out_specs=whole(count),
        scratch_shapes=[pltpu.SemaphoreType.DMA((count,))],
        compiler_params=pltpu.CompilerParams(vmem_limit_bytes=1 << 20),
        cost_estimate=pl.CostEstimate(
            flops=0, bytes_accessed=2 * sum(w.size for w in weights), transcendentals=0
        ),
    )(*[in_hbm(w) for w in weights])


def join_kernel(z, *refs):
    blocks, (state_ref, act_ref, image, block_image) = refs[:-4], refs[-4:]
    band = lax.axis_index("band")
    size = z.rows * z.wide

    def put(row, lane, piece):
        rows, lanes = piece.shape
        block_image[row : row + rows, lane : lane + lanes] = piece

    for k, block in enumerate(blocks):
        start = pl.multiple_of((band ^ k) * size, 8)
        unpack(z, 2 * size, block[...].astype(F32), put)
        for t in range(2):
            image[t, pl.ds(start, size)] = block_image[t * size : (t + 1) * size]
    for t in range(2):
        value = image[t]
        state_ref[t] = value.astype(BF16)
        pack(z, act_ref.at[t], masked_silu(z, value))


def in_order(pieces):
    place = channel_place()
    step = 1
    while step < len(pieces):
        flip = (place & step) != 0
        pieces = [
            jnp.where(flip, pieces[j ^ step], pieces[j]) for j in range(len(pieces))
        ]
        step *= 2
    return pieces


def lay_out(z, a_ref, messages, at=0):
    for j, message in enumerate(in_order(messages)):

        def put(row, lane, piece):
            rows, lanes = piece.shape
            lane = at + j * z.per + lane
            a_ref[row : row + rows, lane : lane + lanes] = piece

        unpack(z, z.cells, message, put)


def convolve(z, cells, weight, left, right):
    n = z.cells
    left[8 : 8 + n] = lax.dot_general(cells, weight(0), TRANSPOSED, preferred_element_type=F32)
    right[8 : 8 + n] = lax.dot_general(cells, weight(2), TRANSPOSED, preferred_element_type=F32)
    middle = lax.dot_general(cells, weight(1), TRANSPOSED, preferred_element_type=F32)
    total = middle + left[7 : 7 + n] + right[9 : 9 + n]
    row = jnp.zeros((z.wide, z.per), F32)
    above = jnp.concatenate([row, total[: n - z.wide, : z.per]], 0)
    below = jnp.concatenate([total[z.wide :, 2 * z.per :], row], 0)
    return total[:, z.per : 2 * z.per] + above + below


def taps(z, w_ref, start, depth):
    def weight(j):
        return w_ref[:, j, :, start : start + depth].reshape(3 * z.per, depth)

    return weight


def clear_edges(z, left, right):
    left[0:8] = jnp.zeros((8, 3 * z.per), F32)
    right[8 + z.cells : 16 + z.cells] = jnp.zeros((8, 3 * z.per), F32)


def finish(z, state, result, bias, new_ref, act_ref):
    new = (state.astype(F32) + result + bias).astype(BF16)
    new_ref[...] = new
    pack(z, act_ref, masked_silu(z, new.astype(F32)))


def bias_of(ref):
    return ref[...].astype(F32).reshape(1, -1)


def layer_kernel(z, *refs):
    n = z.shards
    blocks, refs = refs[:n], refs[n:]
    state_ref, w0, b0, w1, b1, new_ref, act_ref, a_ref, left, right = refs
    clear_edges(z, left, right)
    for t, (w_ref, b_ref) in enumerate(((w0, b0), (w1, b1))):
        lay_out(z, a_ref, [block[t] for block in blocks])
        result = convolve(z, a_ref[...], taps(z, w_ref, 0, z.depth), left, right)
        finish(z, state_ref[t], result, bias_of(b_ref), new_ref.at[t], act_ref.at[t])


def decode_kernel(z, *refs):
    n = z.shards
    blocks, refs = refs[:n], refs[n:]
    state_ref, w_ref, b_ref, new_ref, act_ref, skip_ref, a_ref, left, right = refs
    clear_edges(z, left, right)
    lay_out(z, a_ref, [block[1] for block in blocks])
    lay_out(z, a_ref, [block[0] for block in blocks], z.depth)
    skip_ref[...] = a_ref[:, z.depth :]
    result = convolve(z, a_ref[...], taps(z, w_ref, 0, 2 * z.depth), left, right)
    finish(z, state_ref[1], result, bias_of(b_ref), new_ref, act_ref)


def skip_kernel(z, skip_ref, w_ref, out_ref, left, right):
    clear_edges(z, left, right)
    out_ref[...] = convolve(z, skip_ref[...], taps(z, w_ref, z.depth, z.depth), left, right)


def last_kernel(z, *refs):
    n = z.shards
    blocks, refs = refs[:n], refs[n:]
    state_ref, skip_ref, w_ref, b_ref = refs[:4]
    outs, (a_ref, left, right, image) = refs[4 : 4 + z.bands], refs[4 + z.bands :]
    clear_edges(z, left, right)
    lay_out(z, a_ref, [block[...] for block in blocks])
    result = convolve(z, a_ref[...], taps(z, w_ref, 0, z.depth), left, right)
    total = state_ref[...].astype(F32) + (result + skip_ref[...])
    total = total + bias_of(b_ref)
    image[...] = total.reshape(z.height, z.wide, z.per)
    band = lax.axis_index("band")
    for k, out in enumerate(outs):
        rows = image[pl.ds((band ^ k) * z.rows, z.rows), LAYERS : LAYERS + z.columns]
        pack(z, out, rows.reshape(-1, z.per))


def rows_kernel(z, *refs):
    blocks, (out_ref, image, block_image) = refs[:-3], refs[-3:]
    band = lax.axis_index("band")

    def put(row, lane, piece):
        rows, lanes = piece.shape
        block_image[row : row + rows, lane : lane + lanes] = piece

    for k, block in enumerate(blocks):
        start = pl.multiple_of((band ^ k) * z.columns, 8)
        unpack(z, z.rows * z.columns, block[...].astype(F32), put)
        for row in range(z.rows):
            image[row, pl.ds(start, z.columns)] = block_image[
                row * z.columns : (row + 1) * z.columns
            ]
    for row in range(z.rows):
        out_ref[row] = image[row].T.astype(BF16)


def over_bands(blocks):
    moved = [blocks[0]]
    for k, block in enumerate(blocks):
        if k:
            moved.append(exchange(block, "band", k))
    return moved


def gather(cells):
    chips = [cells]
    for k in range(1, lax.axis_size("section")):
        chips.append(exchange(cells, "section", k))
    pieces = []
    for chip in chips:
        pieces.append(chip)
        for k in range(1, lax.axis_size("chan")):
            pieces.append(exchange(chip, "chan", k))
    return pieces


def per_device(latent, control_hint, cw1, cb1, cw2, cb2, mw1, mb1, mw2, mb2, dw1, db1, dw2, db2):
    z = Sizes(latent)
    kernel = lambda f, *a: functools.partial(f, z, *a)
    edges = [pltpu.VMEM((z.cells + 16, 3 * z.per), F32)] * 2
    work = lambda parts: [pltpu.VMEM((z.cells, parts * z.depth), BF16)] + edges
    unit = 2 * 9 * z.cells * z.per * z.depth
    single = sds((z.cells, z.per))
    pair = sds((2, z.cells, z.per))
    message = z.packed(z.cells)

    raw = (z.rows, z.per, z.width)
    blocks = pl.pallas_call(
        kernel(split_kernel),
        out_shape=[sds(z.packed(2 * z.rows * z.wide))] * z.bands,
        in_specs=[pl.BlockSpec(memory_space=pltpu.HBM)] * 2,
        out_specs=whole(z.bands),
        scratch_shapes=[pltpu.VMEM(raw, BF16)] * 2
        + [
            pltpu.VMEM((2, z.rows, z.width + 2 * LAYERS, z.per), F32),
            pltpu.SemaphoreType.DMA((2,)),
        ],
        compiler_params=pltpu.CompilerParams(vmem_limit_bytes=4 << 20),
    )(in_hbm(latent.swapaxes(1, 2)), in_hbm(control_hint.swapaxes(1, 2)))
    blocks = over_bands(blocks)
    cw1, mw1 = load(cw1, mw1)
    cw2, mw2 = load(cw2, mw2)
    (dw1,) = load(dw1)
    (dw2,) = load(dw2)
    state, act = call(
        kernel(join_kernel),
        [pair, sds((2,) + message)],
        *blocks,
        scratch=[
            pltpu.VMEM((2, z.cells, z.per), F32),
            pltpu.VMEM((2 * z.rows * z.wide, z.per), F32),
        ],
    )
    for weights in ((cw1, cb1, mw1, mb1), (cw2, cb2, mw2, mb2)):
        state, act = call(
            kernel(layer_kernel),
            [pair, sds((2,) + message)],
            *gather(act),
            state,
            *weights,
            scratch=work(1),
            flops=2 * unit,
        )
    state, act, skip = call(
        kernel(decode_kernel),
        [single, sds(message), sds((z.cells, z.depth))],
        *gather(act),
        state,
        dw1,
        db1,
        scratch=work(2),
        flops=2 * unit,
    )
    part = call(
        kernel(skip_kernel), sds((z.cells, z.per), F32), skip, dw2, scratch=edges, flops=unit
    )
    blocks = call(
        kernel(last_kernel),
        [sds(z.packed(z.rows * z.columns))] * z.bands,
        *gather(act),
        state,
        part,
        dw2,
        db2,
        scratch=work(1) + [pltpu.VMEM((z.height, z.wide, z.per), F32)],
        flops=unit,
    )
    out = call(
        kernel(rows_kernel),
        sds(raw),
        *over_bands(blocks),
        scratch=[
            pltpu.VMEM((z.rows, z.width, z.per), F32),
            pltpu.VMEM((z.rows * z.columns, z.per), F32),
        ],
    )
    return out.swapaxes(1, 2)


def solution(mesh):
    image = P(("groups", "band"), None, CHANNEL_AXES)
    kernel = P(None, None, CHANNEL_AXES, None)
    bias = P(CHANNEL_AXES)

    return jax.shard_map(
        per_device,
        mesh=mesh,
        in_specs=(image, image) + (kernel, bias) * 6,
        out_specs=image,
        check_vma=False,
    )
```

```python
import functools

import jax
import jax.numpy as jnp
from jax import lax
from jax.experimental import pallas as pl
from jax.experimental.pallas import tpu as pltpu
from jax.sharding import PartitionSpec as P


LAYERS = 4
LANES = 128
CHANNEL_AXES = ("section", "chan")
F32 = jnp.float32
BF16 = jnp.bfloat16
TRANSPOSED = (((1,), (1,)), ((), ()))


def silu(value):
    return value * jax.nn.sigmoid(value)


def exchange(cells, axis, distance):
    count = lax.axis_size(axis)
    return lax.ppermute(cells, axis, [(i, i ^ distance) for i in range(count)])


def channel_place():
    return lax.axis_index("section") * lax.axis_size("chan") + lax.axis_index("chan")


def channel_count():
    return lax.axis_size("section") * lax.axis_size("chan")


def whole(count):
    return [pl.BlockSpec(memory_space=pltpu.VMEM)] * count


def call(kernel, outs, *args, scratch=(), flops=0):
    many = isinstance(outs, (tuple, list))
    moved = sum(a.size * a.dtype.itemsize for a in args)
    moved += sum(o.size * o.dtype.itemsize for o in (outs if many else [outs]))
    return pl.pallas_call(
        kernel,
        out_shape=outs,
        in_specs=whole(len(args)),
        out_specs=whole(len(outs)) if many else whole(1)[0],
        scratch_shapes=list(scratch),
        compiler_params=pltpu.CompilerParams(vmem_limit_bytes=20 << 20),
        cost_estimate=pl.CostEstimate(flops=flops, bytes_accessed=moved, transcendentals=0),
    )(*args)


def sds(shape, dtype=BF16):
    return jax.ShapeDtypeStruct(shape, dtype)


class Sizes:
    def __init__(self, latent):
        self.bands = lax.axis_size("band")
        self.rows, self.width, self.per = latent.shape
        self.columns = self.width // self.bands
        self.wide = self.columns + 2 * LAYERS
        self.height = self.rows * self.bands
        self.cells = self.height * self.wide
        self.held = self.cells + 2 * self.height
        self.shards = channel_count()
        self.rest = self.per % LANES
        self.groups = LANES // self.rest if self.rest and LANES % self.rest == 0 else 0
        if self.per < LANES:
            self.groups = 0
        self.depth = self.shards * self.per


    def dense(self, cells):
        return self.groups and cells % (8 * self.groups) == 0

    def packed(self, cells):
        if not self.dense(cells):
            return (cells, self.per)
        return (cells * (self.per // LANES) + cells // self.groups, LANES)


def pack(z, ref, value):
    cells = value.shape[0]
    if not z.dense(cells):
        ref[...] = value.astype(BF16)
        return
    full = z.per // LANES
    for g in range(full):
        ref[g * cells : (g + 1) * cells] = value[:, g * LANES : (g + 1) * LANES].astype(BF16)
    part = cells // z.groups
    rest = [value[g * part : (g + 1) * part, full * LANES :] for g in range(z.groups)]
    ref[full * cells :] = jnp.concatenate(rest, axis=1).astype(BF16)


def unpack(z, cells, message, put):
    if not z.dense(cells):
        put(0, 0, message)
        return
    full = z.per // LANES
    for g in range(full):
        put(0, g * LANES, message[g * cells : (g + 1) * cells])
    part = cells // z.groups
    rest = message[full * cells :]
    for g in range(z.groups):
        put(g * part, full * LANES, rest[:, g * z.rest : (g + 1) * z.rest])


def masked_silu(z, state):
    value = silu(state).reshape(z.wide, z.height, z.per)
    at = lax.broadcasted_iota(jnp.int32, value.shape, 0)
    at = at + (lax.axis_index("band") * z.columns - LAYERS)
    value = jnp.where((at >= 0) & (at < z.width), value, 0.0)
    return value.reshape(-1, z.per)


def fetch(sources, targets, sems):
    copies = [
        pltpu.make_async_copy(source, target, sems.at[i])
        for i, (source, target) in enumerate(zip(sources, targets))
    ]
    for copy in copies:
        copy.start()
    for copy in copies:
        copy.wait()


def split_kernel(z, latent_hbm, hint_hbm, *refs):
    outs, (latent_ref, hint_ref, spread, sems) = refs[:-4], refs[-4:]
    fetch((latent_hbm, hint_hbm), (latent_ref, hint_ref), sems)
    latent = latent_ref[...].astype(F32)
    control = (latent + hint_ref[...].astype(F32)).astype(BF16).astype(F32)
    edge = jnp.zeros((2, z.rows, LAYERS, z.per), F32)
    spread[:, :, :LAYERS] = edge
    spread[:, :, LAYERS + z.width :] = edge
    for row in range(z.rows):
        spread[0, row, LAYERS : LAYERS + z.width] = control[row].T
        spread[1, row, LAYERS : LAYERS + z.width] = latent[row].T
    band = lax.axis_index("band")
    for k, out in enumerate(outs):
        start = pl.multiple_of((band ^ k) * z.columns, 8)
        pack(z, out, spread[:, :, pl.ds(start, z.wide)].reshape(-1, z.per))


def in_hbm(array):
    return pltpu.with_memory_space_constraint(array, pltpu.HBM)


def load_kernel(count, *refs):
    fetch(refs[:count], refs[count : 2 * count], refs[2 * count])


def load(*weights):
    count = len(weights)
    return pl.pallas_call(
        functools.partial(load_kernel, count),
        out_shape=[sds(w.shape) for w in weights],
        in_specs=[pl.BlockSpec(memory_space=pltpu.HBM)] * count,
        out_specs=whole(count),
        scratch_shapes=[pltpu.SemaphoreType.DMA((count,))],
        compiler_params=pltpu.CompilerParams(vmem_limit_bytes=1 << 20),
        cost_estimate=pl.CostEstimate(
            flops=0, bytes_accessed=2 * sum(w.size for w in weights), transcendentals=0
        ),
    )(*[in_hbm(w) for w in weights])


def lane_groups(z):
    return [(at, min(LANES, z.per - at)) for at in range(0, z.per, LANES)]


def join_kernel(z, *refs):
    blocks, (state_ref, act_ref, image, block_image) = refs[:-4], refs[-4:]
    band = lax.axis_index("band")
    size = z.rows * z.wide

    def put(row, lane, piece):
        rows, lanes = piece.shape
        group, lane = lane // LANES, lane % LANES
        block_image[group, row : row + rows, lane : lane + lanes] = piece

    for k, block in enumerate(blocks):
        unpack(z, 2 * size, block[...].astype(F32), put)
        for t in range(2):
            for row in range(z.rows):
                to = pl.ds((band ^ k) * z.rows + row, z.wide, stride=z.height)
                at = t * size + row * z.wide
                for g in range(len(lane_groups(z))):
                    image[t, g, to] = block_image[g, at : at + z.wide]
    for t in range(2):
        parts = [image[t, g][:, :n] for g, (_, n) in enumerate(lane_groups(z))]
        value = jnp.concatenate(parts, axis=1)
        state_ref[t] = value.astype(BF16)
        pack(z, act_ref.at[t], masked_silu(z, value))


def in_order(pieces):
    place = channel_place()
    step = 1
    while step < len(pieces):
        flip = (place & step) != 0
        pieces = [
            jnp.where(flip, pieces[j ^ step], pieces[j]) for j in range(len(pieces))
        ]
        step *= 2
    return pieces


def lay_out(z, a_ref, messages, at=0):
    for j, message in enumerate(in_order(messages)):

        def put(row, lane, piece):
            rows, lanes = piece.shape
            lane = at + j * z.per + lane
            row = row + z.height
            a_ref[row : row + rows, lane : lane + lanes] = piece

        unpack(z, z.cells, message, put)


def convolve(z, cells, weight):
    moved = jnp.concatenate([cells(j) for j in range(3)], axis=1)
    weights = jnp.concatenate([weight(j) for j in range(3)], axis=1)
    total = lax.dot_general(moved, weights, TRANSPOSED, preferred_element_type=F32)
    above, middle, below = [
        total[:, i * z.per : (i + 1) * z.per].reshape(z.wide, z.height, z.per) for i in range(3)
    ]
    row = lax.broadcasted_iota(jnp.int32, middle.shape, 1)
    above = jnp.where(row == 0, 0.0, pltpu.roll(above, 1, 1))
    below = jnp.where(row == z.height - 1, 0.0, pltpu.roll(below, z.height - 1, 1))
    return (middle + above + below).reshape(-1, z.per)


def moves(z, a_ref):
    return lambda j: a_ref[j * z.height : j * z.height + z.cells]


def taps(z, w_ref, start, depth):
    def weight(j):
        return w_ref[:, j, :, start : start + depth].reshape(3 * z.per, depth)

    return weight


def clear_edges(z, a_ref):
    edge = jnp.zeros((z.height, a_ref.shape[1]), BF16)
    a_ref[: z.height] = edge
    a_ref[z.height + z.cells :] = edge


def finish(z, state, result, bias, new_ref, act_ref):
    new = (state.astype(F32) + result + bias).astype(BF16)
    new_ref[...] = new
    pack(z, act_ref, masked_silu(z, new.astype(F32)))


def bias_of(ref):
    return ref[...].astype(F32).reshape(1, -1)


def layer_kernel(z, *refs):
    n = z.shards
    blocks, refs = refs[:n], refs[n:]
    state_ref, w0, b0, w1, b1, new_ref, act_ref, a_ref = refs
    for t, (w_ref, b_ref) in enumerate(((w0, b0), (w1, b1))):
        clear_edges(z, a_ref.at[t])
        lay_out(z, a_ref.at[t], [block[t] for block in blocks])
        result = convolve(z, moves(z, a_ref.at[t]), taps(z, w_ref, 0, z.depth))
        finish(z, state_ref[t], result, bias_of(b_ref), new_ref.at[t], act_ref.at[t])


def decode_kernel(z, *refs):
    n = z.shards
    blocks, refs = refs[:n], refs[n:]
    state_ref, w_ref, b_ref, new_ref, act_ref, skip_ref, a_ref = refs
    clear_edges(z, a_ref)
    lay_out(z, a_ref, [block[1] for block in blocks])
    lay_out(z, a_ref, [block[0] for block in blocks], z.depth)
    skip_ref[...] = a_ref[:, z.depth :]
    result = convolve(z, moves(z, a_ref), taps(z, w_ref, 0, 2 * z.depth))
    finish(z, state_ref[1], result, bias_of(b_ref), new_ref, act_ref)


def skip_kernel(z, skip_ref, w_ref, out_ref):
    out_ref[...] = convolve(z, moves(z, skip_ref), taps(z, w_ref, z.depth, z.depth))


def last_kernel(z, *refs):
    n = z.shards
    blocks, refs = refs[:n], refs[n:]
    state_ref, skip_ref, w_ref, b_ref = refs[:4]
    outs, (a_ref, image) = refs[4 : 4 + z.bands], refs[4 + z.bands :]
    clear_edges(z, a_ref)
    lay_out(z, a_ref, [block[...] for block in blocks])
    result = convolve(z, moves(z, a_ref), taps(z, w_ref, 0, z.depth))
    total = state_ref[...].astype(F32) + (result + skip_ref[...])
    total = total + bias_of(b_ref)
    groups = lane_groups(z)
    for g, (lane, n) in enumerate(groups):
        image[g, :, :n] = total[:, lane : lane + n]
    band = lax.axis_index("band")
    for k, out in enumerate(outs):
        rows = []
        for row in range(z.rows):
            first = LAYERS * z.height + (band ^ k) * z.rows + row
            at = pl.ds(first, z.columns, stride=z.height)
            rows.append(
                jnp.concatenate([image[g, at][:, :n] for g, (_, n) in enumerate(groups)], axis=1)
            )
        pack(z, out, jnp.concatenate(rows, axis=0))


def rows_kernel(z, *refs):
    blocks, (out_ref, image, block_image) = refs[:-3], refs[-3:]
    band = lax.axis_index("band")

    def put(row, lane, piece):
        rows, lanes = piece.shape
        block_image[row : row + rows, lane : lane + lanes] = piece

    for k, block in enumerate(blocks):
        start = pl.multiple_of((band ^ k) * z.columns, 8)
        unpack(z, z.rows * z.columns, block[...].astype(F32), put)
        for row in range(z.rows):
            image[row, pl.ds(start, z.columns)] = block_image[
                row * z.columns : (row + 1) * z.columns
            ]
    for row in range(z.rows):
        out_ref[row] = image[row].T.astype(BF16)


def over_bands(blocks):
    moved = [blocks[0]]
    for k, block in enumerate(blocks):
        if k:
            moved.append(exchange(block, "band", k))
    return moved


def gather(cells):
    chips = [cells]
    for k in range(1, lax.axis_size("section")):
        chips.append(exchange(cells, "section", k))
    pieces = []
    for chip in chips:
        pieces.append(chip)
        for k in range(1, lax.axis_size("chan")):
            pieces.append(exchange(chip, "chan", k))
    return pieces


def per_device(latent, control_hint, cw1, cb1, cw2, cb2, mw1, mb1, mw2, mb2, dw1, db1, dw2, db2):
    z = Sizes(latent)
    kernel = lambda f, *a: functools.partial(f, z, *a)
    held = lambda *parts: [pltpu.VMEM(parts[:-1] + (z.held, parts[-1] * z.depth), BF16)]
    groups = len(lane_groups(z))
    unit = 2 * 9 * z.cells * z.per * z.depth
    single = sds((z.cells, z.per))
    pair = sds((2, z.cells, z.per))
    message = z.packed(z.cells)

    raw = (z.rows, z.per, z.width)
    blocks = pl.pallas_call(
        kernel(split_kernel),
        out_shape=[sds(z.packed(2 * z.rows * z.wide))] * z.bands,
        in_specs=[pl.BlockSpec(memory_space=pltpu.HBM)] * 2,
        out_specs=whole(z.bands),
        scratch_shapes=[pltpu.VMEM(raw, BF16)] * 2
        + [
            pltpu.VMEM((2, z.rows, z.width + 2 * LAYERS, z.per), F32),
            pltpu.SemaphoreType.DMA((2,)),
        ],
        compiler_params=pltpu.CompilerParams(vmem_limit_bytes=4 << 20),
    )(in_hbm(latent.swapaxes(1, 2)), in_hbm(control_hint.swapaxes(1, 2)))
    blocks = over_bands(blocks)
    cw1, mw1 = load(cw1, mw1)
    cw2, mw2 = load(cw2, mw2)
    (dw1,) = load(dw1)
    (dw2,) = load(dw2)
    state, act = call(
        kernel(join_kernel),
        [pair, sds((2,) + message)],
        *blocks,
        scratch=[
            pltpu.VMEM((2, groups, z.cells, LANES), F32),
            pltpu.VMEM((groups, 2 * z.rows * z.wide, LANES), F32),
        ],
    )
    for weights in ((cw1, cb1, mw1, mb1), (cw2, cb2, mw2, mb2)):
        state, act = call(
            kernel(layer_kernel),
            [pair, sds((2,) + message)],
            *gather(act),
            state,
            *weights,
            scratch=held(2, 1),
            flops=2 * unit,
        )
    state, act, skip = call(
        kernel(decode_kernel),
        [single, sds(message), sds((z.held, z.depth))],
        *gather(act),
        state,
        dw1,
        db1,
        scratch=held(2),
        flops=2 * unit,
    )
    part = call(kernel(skip_kernel), sds((z.cells, z.per), F32), skip, dw2, flops=unit)
    blocks = call(
        kernel(last_kernel),
        [sds(z.packed(z.rows * z.columns))] * z.bands,
        *gather(act),
        state,
        part,
        dw2,
        db2,
        scratch=held(1) + [pltpu.VMEM((groups, z.cells, LANES), F32)],
        flops=unit,
    )
    out = call(
        kernel(rows_kernel),
        sds(raw),
        *over_bands(blocks),
        scratch=[
            pltpu.VMEM((z.rows, z.width, z.per), F32),
            pltpu.VMEM((z.rows * z.columns, z.per), F32),
        ],
    )
    return out.swapaxes(1, 2)


def solution(mesh):
    image = P(("groups", "band"), None, CHANNEL_AXES)
    kernel = P(None, None, CHANNEL_AXES, None)
    bias = P(CHANNEL_AXES)

    return jax.shard_map(
        per_device,
        mesh=mesh,
        in_specs=(image, image) + (kernel, bias) * 6,
        out_specs=image,
        check_vma=False,
    )
```

```python
import functools

import jax
import jax.numpy as jnp
from jax import lax
from jax.experimental import pallas as pl
from jax.experimental.pallas import tpu as pltpu
from jax.sharding import PartitionSpec as P


LAYERS = 4
LANES = 128
CHANNEL_AXES = ("section", "chan")
F32 = jnp.float32
BF16 = jnp.bfloat16
TRANSPOSED = (((1,), (1,)), ((), ()))


def silu(value):
    return value * jax.nn.sigmoid(value)


def exchange(cells, axis, distance):
    count = lax.axis_size(axis)
    return lax.ppermute(cells, axis, [(i, i ^ distance) for i in range(count)])


def channel_place():
    return lax.axis_index("section") * lax.axis_size("chan") + lax.axis_index("chan")


def channel_count():
    return lax.axis_size("section") * lax.axis_size("chan")


def whole(count):
    return [pl.BlockSpec(memory_space=pltpu.VMEM)] * count


def call(kernel, outs, *args, scratch=(), flops=0):
    many = isinstance(outs, (tuple, list))
    moved = sum(a.size * a.dtype.itemsize for a in args)
    moved += sum(o.size * o.dtype.itemsize for o in (outs if many else [outs]))
    return pl.pallas_call(
        kernel,
        out_shape=outs,
        in_specs=whole(len(args)),
        out_specs=whole(len(outs)) if many else whole(1)[0],
        scratch_shapes=list(scratch),
        compiler_params=pltpu.CompilerParams(vmem_limit_bytes=20 << 20),
        cost_estimate=pl.CostEstimate(flops=flops, bytes_accessed=moved, transcendentals=0),
    )(*args)


def sds(shape, dtype=BF16):
    return jax.ShapeDtypeStruct(shape, dtype)


class Sizes:
    def __init__(self, latent):
        self.bands = lax.axis_size("band")
        self.rows, self.width, self.per = latent.shape
        self.columns = self.width // self.bands
        self.wide = self.columns + 2 * LAYERS
        self.height = self.rows * self.bands
        self.cells = self.height * self.wide
        self.held = self.cells + 2 * self.height
        self.shards = channel_count()
        self.rest = self.per % LANES
        self.groups = LANES // self.rest if self.rest and LANES % self.rest == 0 else 0
        if self.per < LANES:
            self.groups = 0
        self.depth = self.shards * self.per


    def dense(self, cells):
        return self.groups and cells % (8 * self.groups) == 0

    def packed(self, cells):
        if not self.dense(cells):
            return (cells, self.per)
        return (cells * (self.per // LANES) + cells // self.groups, LANES)


def pack(z, ref, value):
    cells = value.shape[0]
    if not z.dense(cells):
        ref[...] = value.astype(BF16)
        return
    full = z.per // LANES
    for g in range(full):
        ref[g * cells : (g + 1) * cells] = value[:, g * LANES : (g + 1) * LANES].astype(BF16)
    part = cells // z.groups
    rest = [value[g * part : (g + 1) * part, full * LANES :] for g in range(z.groups)]
    ref[full * cells :] = jnp.concatenate(rest, axis=1).astype(BF16)


def unpack(z, cells, message, put):
    if not z.dense(cells):
        put(0, 0, message)
        return
    full = z.per // LANES
    for g in range(full):
        put(0, g * LANES, message[g * cells : (g + 1) * cells])
    part = cells // z.groups
    rest = message[full * cells :]
    for g in range(z.groups):
        put(g * part, full * LANES, rest[:, g * z.rest : (g + 1) * z.rest])


def masked_silu(z, state):
    value = silu(state).reshape(z.wide, z.height, z.per)
    at = lax.broadcasted_iota(jnp.int32, value.shape, 0)
    at = at + (lax.axis_index("band") * z.columns - LAYERS)
    value = jnp.where((at >= 0) & (at < z.width), value, 0.0)
    return value.reshape(-1, z.per)


def fetch(sources, targets, sems):
    copies = [
        pltpu.make_async_copy(source, target, sems.at[i])
        for i, (source, target) in enumerate(zip(sources, targets))
    ]
    for copy in copies:
        copy.start()
    for copy in copies:
        copy.wait()


def split_kernel(z, latent_hbm, hint_hbm, *refs):
    outs, (latent_ref, hint_ref, spread, sems) = refs[:-4], refs[-4:]
    fetch((latent_hbm, hint_hbm), (latent_ref, hint_ref), sems)
    latent = latent_ref[...].astype(F32)
    control = (latent + hint_ref[...].astype(F32)).astype(BF16).astype(F32)
    edge = jnp.zeros((2, z.rows, LAYERS, z.per), F32)
    spread[:, :, :LAYERS] = edge
    spread[:, :, LAYERS + z.width :] = edge
    for row in range(z.rows):
        spread[0, row, LAYERS : LAYERS + z.width] = control[row].T
        spread[1, row, LAYERS : LAYERS + z.width] = latent[row].T
    band = lax.axis_index("band")
    for k, out in enumerate(outs):
        start = pl.multiple_of((band ^ k) * z.columns, 8)
        pack(z, out, spread[:, :, pl.ds(start, z.wide)].reshape(-1, z.per))


def in_hbm(array):
    return pltpu.with_memory_space_constraint(array, pltpu.HBM)


def load_kernel(count, *refs):
    fetch(refs[:count], refs[count : 2 * count], refs[2 * count])


def load(*weights):
    count = len(weights)
    return pl.pallas_call(
        functools.partial(load_kernel, count),
        out_shape=[sds(w.shape) for w in weights],
        in_specs=[pl.BlockSpec(memory_space=pltpu.HBM)] * count,
        out_specs=whole(count),
        scratch_shapes=[pltpu.SemaphoreType.DMA((count,))],
        compiler_params=pltpu.CompilerParams(vmem_limit_bytes=1 << 20),
        cost_estimate=pl.CostEstimate(
            flops=0, bytes_accessed=2 * sum(w.size for w in weights), transcendentals=0
        ),
    )(*[in_hbm(w) for w in weights])


def lane_groups(z):
    return [(at, min(LANES, z.per - at)) for at in range(0, z.per, LANES)]


def join_kernel(z, *refs):
    blocks, (state_ref, act_ref, image, block_image) = refs[:-4], refs[-4:]
    band = lax.axis_index("band")
    size = z.rows * z.wide

    def put(row, lane, piece):
        rows, lanes = piece.shape
        group, lane = lane // LANES, lane % LANES
        block_image[group, row : row + rows, lane : lane + lanes] = piece

    for k, block in enumerate(blocks):
        unpack(z, 2 * size, block[...].astype(F32), put)
        for t in range(2):
            for row in range(z.rows):
                to = pl.ds((band ^ k) * z.rows + row, z.wide, stride=z.height)
                at = t * size + row * z.wide
                for g in range(len(lane_groups(z))):
                    image[t, g, to] = block_image[g, at : at + z.wide]
    for t in range(2):
        parts = [image[t, g][:, :n] for g, (_, n) in enumerate(lane_groups(z))]
        value = jnp.concatenate(parts, axis=1)
        state_ref[t] = value.astype(BF16)
        pack(z, act_ref.at[t], masked_silu(z, value))


def in_order(pieces):
    place = channel_place()
    step = 1
    while step < len(pieces):
        flip = (place & step) != 0
        pieces = [
            jnp.where(flip, pieces[j ^ step], pieces[j]) for j in range(len(pieces))
        ]
        step *= 2
    return pieces


def lay_out(z, a_ref, messages, at=0):
    for j, message in enumerate(in_order(messages)):

        def put(row, lane, piece):
            rows, lanes = piece.shape
            lane = at + j * z.per + lane
            row = row + z.height
            a_ref[row : row + rows, lane : lane + lanes] = piece

        unpack(z, z.cells, message, put)


def up(z, value):
    value = value.reshape(z.wide, z.height, -1)
    row = lax.broadcasted_iota(jnp.int32, value.shape, 1)
    return jnp.where(row == 0, 0.0, pltpu.roll(value, 1, 1)).reshape(z.cells, -1)


def down(z, value):
    value = value.reshape(z.wide, z.height, -1)
    row = lax.broadcasted_iota(jnp.int32, value.shape, 1)
    last = z.height - 1
    return jnp.where(row == last, 0.0, pltpu.roll(value, last, 1)).reshape(z.cells, -1)


def convolve(z, cells, weight):
    moved = jnp.concatenate([cells(j) for j in range(3)], axis=1)
    weights = jnp.concatenate([weight(j) for j in range(3)], axis=1)
    total = lax.dot_general(moved, weights, TRANSPOSED, preferred_element_type=F32)
    full = z.per - z.rest
    parts = []
    if full:
        above, middle, below = [total[:, i * full : (i + 1) * full] for i in range(3)]
        parts.append(middle + up(z, above) + down(z, below))
    if z.rest:
        middle, above, below = [
            total[:, 3 * full + i * z.rest : 3 * full + (i + 1) * z.rest] for i in range(3)
        ]
        parts.append(middle + up(z, above) + down(z, below))
    return jnp.concatenate(parts, axis=1) if len(parts) > 1 else parts[0]


def moves(z, a_ref):
    return lambda j: a_ref[j * z.height : j * z.height + z.cells]


def taps(z, w_ref, start, depth):
    full = z.per - z.rest

    def weight(j):
        rows = [w_ref[i, j, :full, start : start + depth] for i in range(3) if full]
        if z.rest:
            rows += [w_ref[i, j, full:, start : start + depth] for i in (1, 0, 2)]
        return jnp.concatenate(rows, axis=0)

    return weight


def clear_edges(z, a_ref):
    edge = jnp.zeros((z.height, a_ref.shape[1]), BF16)
    a_ref[: z.height] = edge
    a_ref[z.height + z.cells :] = edge


def finish(z, state, result, bias, new_ref, act_ref):
    new = (state.astype(F32) + result + bias).astype(BF16)
    new_ref[...] = new
    pack(z, act_ref, masked_silu(z, new.astype(F32)))


def bias_of(ref):
    return ref[...].astype(F32).reshape(1, -1)


def layer_kernel(z, *refs):
    n = z.shards
    blocks, refs = refs[:n], refs[n:]
    state_ref, w0, b0, w1, b1, new_ref, act_ref, a_ref = refs
    for t, (w_ref, b_ref) in enumerate(((w0, b0), (w1, b1))):
        clear_edges(z, a_ref.at[t])
        lay_out(z, a_ref.at[t], [block[t] for block in blocks])
        result = convolve(z, moves(z, a_ref.at[t]), taps(z, w_ref, 0, z.depth))
        finish(z, state_ref[t], result, bias_of(b_ref), new_ref.at[t], act_ref.at[t])


def decode_kernel(z, *refs):
    n = z.shards
    blocks, refs = refs[:n], refs[n:]
    state_ref, w_ref, b_ref, new_ref, act_ref, skip_ref, a_ref = refs
    clear_edges(z, a_ref)
    lay_out(z, a_ref, [block[1] for block in blocks])
    lay_out(z, a_ref, [block[0] for block in blocks], z.depth)
    skip_ref[...] = a_ref[:, z.depth :]
    result = convolve(z, moves(z, a_ref), taps(z, w_ref, 0, 2 * z.depth))
    finish(z, state_ref[1], result, bias_of(b_ref), new_ref, act_ref)


def skip_kernel(z, skip_ref, w_ref, out_ref):
    out_ref[...] = convolve(z, moves(z, skip_ref), taps(z, w_ref, z.depth, z.depth))


def last_kernel(z, *refs):
    n = z.shards
    blocks, refs = refs[:n], refs[n:]
    state_ref, skip_ref, w_ref, b_ref = refs[:4]
    outs, (a_ref, image) = refs[4 : 4 + z.bands], refs[4 + z.bands :]
    clear_edges(z, a_ref)
    lay_out(z, a_ref, [block[...] for block in blocks])
    result = convolve(z, moves(z, a_ref), taps(z, w_ref, 0, z.depth))
    total = state_ref[...].astype(F32) + (result + skip_ref[...])
    total = total + bias_of(b_ref)
    groups = lane_groups(z)
    for g, (lane, n) in enumerate(groups):
        image[g, :, :n] = total[:, lane : lane + n]
    band = lax.axis_index("band")
    for k, out in enumerate(outs):
        rows = []
        for row in range(z.rows):
            first = LAYERS * z.height + (band ^ k) * z.rows + row
            at = pl.ds(first, z.columns, stride=z.height)
            rows.append(
                jnp.concatenate([image[g, at][:, :n] for g, (_, n) in enumerate(groups)], axis=1)
            )
        pack(z, out, jnp.concatenate(rows, axis=0))


def rows_kernel(z, *refs):
    blocks, (out_ref, image, block_image) = refs[:-3], refs[-3:]
    band = lax.axis_index("band")

    def put(row, lane, piece):
        rows, lanes = piece.shape
        block_image[row : row + rows, lane : lane + lanes] = piece

    for k, block in enumerate(blocks):
        start = pl.multiple_of((band ^ k) * z.columns, 8)
        unpack(z, z.rows * z.columns, block[...].astype(F32), put)
        for row in range(z.rows):
            image[row, pl.ds(start, z.columns)] = block_image[
                row * z.columns : (row + 1) * z.columns
            ]
    for row in range(z.rows):
        out_ref[row] = image[row].T.astype(BF16)


def over_bands(blocks):
    moved = [blocks[0]]
    for k, block in enumerate(blocks):
        if k:
            moved.append(exchange(block, "band", k))
    return moved


def gather(cells):
    chips = [cells]
    for k in range(1, lax.axis_size("section")):
        chips.append(exchange(cells, "section", k))
    pieces = []
    for chip in chips:
        pieces.append(chip)
        for k in range(1, lax.axis_size("chan")):
            pieces.append(exchange(chip, "chan", k))
    return pieces


def per_device(latent, control_hint, cw1, cb1, cw2, cb2, mw1, mb1, mw2, mb2, dw1, db1, dw2, db2):
    z = Sizes(latent)
    kernel = lambda f, *a: functools.partial(f, z, *a)
    held = lambda *parts: [pltpu.VMEM(parts[:-1] + (z.held, parts[-1] * z.depth), BF16)]
    groups = len(lane_groups(z))
    unit = 2 * 9 * z.cells * z.per * z.depth
    single = sds((z.cells, z.per))
    pair = sds((2, z.cells, z.per))
    message = z.packed(z.cells)

    raw = (z.rows, z.per, z.width)
    blocks = pl.pallas_call(
        kernel(split_kernel),
        out_shape=[sds(z.packed(2 * z.rows * z.wide))] * z.bands,
        in_specs=[pl.BlockSpec(memory_space=pltpu.HBM)] * 2,
        out_specs=whole(z.bands),
        scratch_shapes=[pltpu.VMEM(raw, BF16)] * 2
        + [
            pltpu.VMEM((2, z.rows, z.width + 2 * LAYERS, z.per), F32),
            pltpu.SemaphoreType.DMA((2,)),
        ],
        compiler_params=pltpu.CompilerParams(vmem_limit_bytes=4 << 20),
    )(in_hbm(latent.swapaxes(1, 2)), in_hbm(control_hint.swapaxes(1, 2)))
    blocks = over_bands(blocks)
    cw1, mw1 = load(cw1, mw1)
    cw2, mw2 = load(cw2, mw2)
    (dw1,) = load(dw1)
    (dw2,) = load(dw2)
    state, act = call(
        kernel(join_kernel),
        [pair, sds((2,) + message)],
        *blocks,
        scratch=[
            pltpu.VMEM((2, groups, z.cells, LANES), F32),
            pltpu.VMEM((groups, 2 * z.rows * z.wide, LANES), F32),
        ],
    )
    for weights in ((cw1, cb1, mw1, mb1), (cw2, cb2, mw2, mb2)):
        state, act = call(
            kernel(layer_kernel),
            [pair, sds((2,) + message)],
            *gather(act),
            state,
            *weights,
            scratch=held(2, 1),
            flops=2 * unit,
        )
    state, act, skip = call(
        kernel(decode_kernel),
        [single, sds(message), sds((z.held, z.depth))],
        *gather(act),
        state,
        dw1,
        db1,
        scratch=held(2),
        flops=2 * unit,
    )
    part = call(
        kernel(skip_kernel), sds((z.cells, z.per), F32), skip, dw2, flops=unit
    )
    blocks = call(
        kernel(last_kernel),
        [sds(z.packed(z.rows * z.columns))] * z.bands,
        *gather(act),
        state,
        part,
        dw2,
        db2,
        scratch=held(1) + [pltpu.VMEM((groups, z.cells, LANES), F32)],
        flops=unit,
    )
    out = call(
        kernel(rows_kernel),
        sds(raw),
        *over_bands(blocks),
        scratch=[
            pltpu.VMEM((z.rows, z.width, z.per), F32),
            pltpu.VMEM((z.rows * z.columns, z.per), F32),
        ],
    )
    return out.swapaxes(1, 2)


def solution(mesh):
    image = P(("groups", "band"), None, CHANNEL_AXES)
    kernel = P(None, None, CHANNEL_AXES, None)
    bias = P(CHANNEL_AXES)

    return jax.shard_map(
        per_device,
        mesh=mesh,
        in_specs=(image, image) + (kernel, bias) * 6,
        out_specs=image,
        check_vma=False,
    )
```

```python
import functools

import jax
import jax.numpy as jnp
from jax import lax
from jax.experimental import pallas as pl
from jax.experimental.pallas import tpu as pltpu
from jax.sharding import PartitionSpec as P


LAYERS = 4
LANES = 128
CHANNEL_AXES = ("section", "chan")
F32 = jnp.float32
BF16 = jnp.bfloat16
TRANSPOSED = (((1,), (1,)), ((), ()))


def silu(value):
    return value * jax.nn.sigmoid(value)


def exchange(cells, axis, distance):
    count = lax.axis_size(axis)
    return lax.ppermute(cells, axis, [(i, i ^ distance) for i in range(count)])


def channel_place():
    return lax.axis_index("section") * lax.axis_size("chan") + lax.axis_index("chan")


def channel_count():
    return lax.axis_size("section") * lax.axis_size("chan")


def whole(count):
    return [pl.BlockSpec(memory_space=pltpu.VMEM)] * count


def call(kernel, outs, *args, scratch=(), flops=0):
    many = isinstance(outs, (tuple, list))
    moved = sum(a.size * a.dtype.itemsize for a in args)
    moved += sum(o.size * o.dtype.itemsize for o in (outs if many else [outs]))
    return pl.pallas_call(
        kernel,
        out_shape=outs,
        in_specs=whole(len(args)),
        out_specs=whole(len(outs)) if many else whole(1)[0],
        scratch_shapes=list(scratch),
        compiler_params=pltpu.CompilerParams(vmem_limit_bytes=20 << 20),
        cost_estimate=pl.CostEstimate(flops=flops, bytes_accessed=moved, transcendentals=0),
    )(*args)


def sds(shape, dtype=BF16):
    return jax.ShapeDtypeStruct(shape, dtype)


class Sizes:
    def __init__(self, latent):
        self.bands = lax.axis_size("band")
        self.rows, self.width, self.per = latent.shape
        self.columns = self.width // self.bands
        self.wide = self.columns + 2 * LAYERS
        self.height = self.rows * self.bands
        self.cells = self.height * self.wide
        self.held = self.cells + 2 * self.height
        self.shards = channel_count()
        self.depth = self.shards * self.per
        self.rest = self.per % LANES
        self.groups = LANES // self.rest if self.rest and LANES % self.rest == 0 else 0
        if self.per < LANES:
            self.groups = 0
        self.span = LANES
        while not self.fits():
            self.span += LANES

    def fits(self):
        last = self.depth - self.span
        self.starts = [min(j * self.per // LANES * LANES, last) for j in range(self.shards)]
        self.offsets = [j * self.per - start for j, start in enumerate(self.starts)]
        return all(offset + self.per <= self.span for offset in self.offsets)


    def part(self, cells):
        return -(-cells // (8 * self.groups)) * 8

    def packed(self, cells):
        if not self.groups:
            return (cells, self.per)
        return (cells * (self.per // LANES) + self.part(cells), LANES)

    def kept(self, trim):
        return self.cells - 2 * trim * self.height


def pack(z, ref, value):
    cells = value.shape[0]
    if not z.groups:
        ref[...] = value.astype(BF16)
        return
    full = z.per // LANES
    for g in range(full):
        ref[g * cells : (g + 1) * cells] = value[:, g * LANES : (g + 1) * LANES].astype(BF16)
    part = z.part(cells)
    rest = [value[g * part : (g + 1) * part, full * LANES :] for g in range(z.groups)]
    short = part - rest[-1].shape[0]
    if short:
        rest[-1] = jnp.concatenate([rest[-1], jnp.zeros((short, z.rest), F32)], axis=0)
    ref[full * cells :] = jnp.concatenate(rest, axis=1).astype(BF16)


def unpack(z, cells, message, put):
    if not z.groups:
        put(0, 0, message)
        return
    full = z.per // LANES
    for g in range(full):
        put(0, g * LANES, message[g * cells : (g + 1) * cells])
    part = z.part(cells)
    rest = message[full * cells :]
    for g in range(z.groups):
        rows = min(part, cells - g * part)
        put(g * part, full * LANES, rest[:rows, g * z.rest : (g + 1) * z.rest])


def masked_silu(z, state):
    value = silu(state).reshape(z.wide, z.height, z.per)
    at = lax.broadcasted_iota(jnp.int32, value.shape, 0)
    at = at + (lax.axis_index("band") * z.columns - LAYERS)
    value = jnp.where((at >= 0) & (at < z.width), value, 0.0)
    return value.reshape(-1, z.per)


def fetch(sources, targets, sems):
    copies = [
        pltpu.make_async_copy(source, target, sems.at[i])
        for i, (source, target) in enumerate(zip(sources, targets))
    ]
    for copy in copies:
        copy.start()
    for copy in copies:
        copy.wait()


def split_kernel(z, latent_hbm, hint_hbm, *refs):
    outs, (latent_ref, hint_ref, spread, sems) = refs[:-4], refs[-4:]
    fetch((latent_hbm, hint_hbm), (latent_ref, hint_ref), sems)
    latent = latent_ref[...].astype(F32)
    control = (latent + hint_ref[...].astype(F32)).astype(BF16).astype(F32)
    edge = jnp.zeros((2, z.rows, LAYERS, z.per), F32)
    spread[:, :, :LAYERS] = edge
    spread[:, :, LAYERS + z.width :] = edge
    for row in range(z.rows):
        spread[0, row, LAYERS : LAYERS + z.width] = control[row].T
        spread[1, row, LAYERS : LAYERS + z.width] = latent[row].T
    band = lax.axis_index("band")
    for k, out in enumerate(outs):
        start = pl.multiple_of((band ^ k) * z.columns, 8)
        pack(z, out, spread[:, :, pl.ds(start, z.wide)].reshape(-1, z.per))


def in_hbm(array):
    return pltpu.with_memory_space_constraint(array, pltpu.HBM)


def load_kernel(count, *refs):
    fetch(refs[:count], refs[count : 2 * count], refs[2 * count])


def load(*weights):
    count = len(weights)
    return pl.pallas_call(
        functools.partial(load_kernel, count),
        out_shape=[sds(w.shape) for w in weights],
        in_specs=[pl.BlockSpec(memory_space=pltpu.HBM)] * count,
        out_specs=whole(count),
        scratch_shapes=[pltpu.SemaphoreType.DMA((count,))],
        compiler_params=pltpu.CompilerParams(vmem_limit_bytes=1 << 20),
        cost_estimate=pl.CostEstimate(
            flops=0, bytes_accessed=2 * sum(w.size for w in weights), transcendentals=0
        ),
    )(*[in_hbm(w) for w in weights])


def lane_groups(z):
    return [(at, min(LANES, z.per - at)) for at in range(0, z.per, LANES)]


def join_kernel(z, *refs):
    blocks, (state_ref, act_ref, image, block_image) = refs[:-4], refs[-4:]
    band = lax.axis_index("band")
    size = z.rows * z.wide

    def put(row, lane, piece):
        rows, lanes = piece.shape
        group, lane = lane // LANES, lane % LANES
        block_image[group, row : row + rows, lane : lane + lanes] = piece

    for k, block in enumerate(blocks):
        unpack(z, 2 * size, block[...].astype(F32), put)
        for t in range(2):
            for row in range(z.rows):
                to = pl.ds((band ^ k) * z.rows + row, z.wide, stride=z.height)
                at = t * size + row * z.wide
                for g in range(len(lane_groups(z))):
                    image[t, g, to] = block_image[g, at : at + z.wide]
    for t in range(2):
        parts = [image[t, g][:, :n] for g, (_, n) in enumerate(lane_groups(z))]
        value = jnp.concatenate(parts, axis=1)
        state_ref[t] = value.astype(BF16)
        pack(z, act_ref.at[t], masked_silu(z, value))


def in_order(pieces):
    place = channel_place()
    step = 1
    while step < len(pieces):
        flip = (place & step) != 0
        pieces = [
            jnp.where(flip, pieces[j ^ step], pieces[j]) for j in range(len(pieces))
        ]
        step *= 2
    return pieces


def lay_out(z, trim, a_ref, messages):
    first = (1 + trim) * z.height
    a_ref[:first] = jnp.zeros((first, a_ref.shape[1]), BF16)
    a_ref[z.held - first :] = jnp.zeros((first, a_ref.shape[1]), BF16)
    for j, message in enumerate(in_order(messages)):

        def put(row, lane, piece):
            rows, lanes = piece.shape
            lane = j * z.per + lane
            row = row + first
            a_ref[row : row + rows, lane : lane + lanes] = piece

        unpack(z, z.kept(trim), message, put)


def place(z, trim, a_ref, at, message, distance):
    first = (1 + trim) * z.height
    owner = channel_place() ^ distance
    start = offset = jnp.int32(0)
    for j in range(z.shards):
        start = jnp.where(owner == j, z.starts[j], start)
        offset = jnp.where(owner == j, z.offsets[j], offset)
    for known in sorted(set(z.offsets)):

        @pl.when(offset == known)
        def _():
            def put(row, lane, piece):
                rows, lanes = piece.shape
                lane = at + known + lane
                row = row + first
                a_ref[row : row + rows, lane : lane + lanes] = piece

            unpack(z, z.kept(trim), message, put)

    return start


def accumulate(z, trim, distances, sources, w_ref, a_ref):
    a_ref[...] = jnp.zeros(a_ref.shape, BF16)
    slices = []
    for base, messages in sources:
        for distance, message in zip(distances, messages):
            start = place(z, trim, a_ref, len(slices) * z.span, message, distance)
            slices.append(pl.ds(pl.multiple_of(base + start, LANES), z.span))
    return convolve(z, moves(z, a_ref), taps(z, w_ref, slices))


def up(z, value):
    value = value.reshape(z.wide, z.height, -1)
    row = lax.broadcasted_iota(jnp.int32, value.shape, 1)
    return jnp.where(row == 0, 0.0, pltpu.roll(value, 1, 1)).reshape(z.cells, -1)


def down(z, value):
    value = value.reshape(z.wide, z.height, -1)
    row = lax.broadcasted_iota(jnp.int32, value.shape, 1)
    last = z.height - 1
    return jnp.where(row == last, 0.0, pltpu.roll(value, last, 1)).reshape(z.cells, -1)


def convolve(z, cells, weight):
    moved = jnp.concatenate([cells(j) for j in range(3)], axis=1)
    weights = jnp.concatenate([weight(j) for j in range(3)], axis=1)
    total = lax.dot_general(moved, weights, TRANSPOSED, preferred_element_type=F32)
    full = z.per - z.rest
    parts = []
    if full:
        above, middle, below = [total[:, i * full : (i + 1) * full] for i in range(3)]
        parts.append(middle + up(z, above) + down(z, below))
    if z.rest:
        middle, above, below = [
            total[:, 3 * full + i * z.rest : 3 * full + (i + 1) * z.rest] for i in range(3)
        ]
        parts.append(middle + up(z, above) + down(z, below))
    return jnp.concatenate(parts, axis=1) if len(parts) > 1 else parts[0]


def moves(z, a_ref):
    return lambda j: a_ref[j * z.height : j * z.height + z.cells]


def taps(z, w_ref, slices):
    full = z.per - z.rest

    def rows(j, at):
        rows = [w_ref[i, j, :full, at] for i in range(3) if full]
        if z.rest:
            rows += [w_ref[i, j, full:, at] for i in (1, 0, 2)]
        return jnp.concatenate(rows, axis=0)

    return lambda j: jnp.concatenate([rows(j, at) for at in slices], axis=1)


def finish(z, trim, state, result, bias, new_ref, act_ref):
    new = (state.astype(F32) + result + bias).astype(BF16)
    new_ref[...] = new
    edge = trim * z.height
    pack(z, act_ref, masked_silu(z, new.astype(F32))[edge : z.cells - edge])


def bias_of(ref):
    return ref[...].astype(F32).reshape(1, -1)


def pair_kernel(z, trim, distances, add, end, *refs):
    n = len(distances)
    blocks, refs = refs[:n], refs[n:]
    sums, refs = refs[:add], refs[add:]
    w0, w1, *refs = refs
    if end:
        state_ref, b0, b1, new_ref, act_ref, a_ref = refs
    else:
        out_ref, a_ref = refs
    for t, w_ref in enumerate((w0, w1)):
        sources = [(0, [block[t] for block in blocks])]
        total = accumulate(z, trim, distances, sources, w_ref, a_ref.at[t])
        for other in sums:
            total = total + other[t]
        if end:
            bias = bias_of((b0, b1)[t])
            finish(z, trim + 1, state_ref[t], total, bias, new_ref.at[t], act_ref.at[t])
        else:
            out_ref[t] = total


def decode_kernel(z, trim, distances, add, end, *refs):
    n = len(distances)
    blocks, refs = refs[:n], refs[n:]
    sums, refs = refs[:add], refs[add:]
    w_ref, *refs = refs
    a_ref = refs.pop()
    sources = [(0, [block[1] for block in blocks]), (z.depth, [block[0] for block in blocks])]
    total = accumulate(z, trim, distances, sources, w_ref, a_ref)
    for other in sums:
        total = total + other[...]
    if end:
        state_ref, b_ref, new_ref, act_ref = refs
        finish(z, trim + 1, state_ref[1], total, bias_of(b_ref), new_ref, act_ref)
    else:
        refs[0][...] = total


def skip_kernel(z, trim, *refs):
    blocks, (w_ref, out_ref, a_ref) = refs[: z.shards], refs[z.shards :]
    lay_out(z, trim, a_ref, [block[0] for block in blocks])
    weights = taps(z, w_ref, [slice(z.depth, 2 * z.depth)])
    out_ref[...] = convolve(z, moves(z, a_ref), weights)


def last_kernel(z, trim, distances, add, end, *refs):
    n = len(distances)
    blocks, refs = refs[:n], refs[n:]
    sums, refs = refs[:add], refs[add:]
    w_ref, *refs = refs
    a_ref = refs.pop()
    sources = [(0, [block[...] for block in blocks])]
    total = accumulate(z, trim, distances, sources, w_ref, a_ref)
    for other in sums:
        total = total + other[...]
    if not end:
        refs[0][...] = total
        return
    image = refs.pop()
    state_ref, b_ref, *outs = refs
    total = state_ref[...].astype(F32) + total + bias_of(b_ref)
    groups = lane_groups(z)
    for g, (lane, n) in enumerate(groups):
        image[g, :, :n] = total[:, lane : lane + n]
    band = lax.axis_index("band")
    for k, out in enumerate(outs):
        rows = []
        for row in range(z.rows):
            first = LAYERS * z.height + (band ^ k) * z.rows + row
            at = pl.ds(first, z.columns, stride=z.height)
            rows.append(
                jnp.concatenate([image[g, at][:, :n] for g, (_, n) in enumerate(groups)], axis=1)
            )
        pack(z, out, jnp.concatenate(rows, axis=0))


def rows_kernel(z, *refs):
    blocks, (out_ref, image, block_image) = refs[:-3], refs[-3:]
    band = lax.axis_index("band")

    def put(row, lane, piece):
        rows, lanes = piece.shape
        block_image[row : row + rows, lane : lane + lanes] = piece

    for k, block in enumerate(blocks):
        start = pl.multiple_of((band ^ k) * z.columns, 8)
        unpack(z, z.rows * z.columns, block[...].astype(F32), put)
        for row in range(z.rows):
            image[row, pl.ds(start, z.columns)] = block_image[
                row * z.columns : (row + 1) * z.columns
            ]
    for row in range(z.rows):
        out_ref[row] = image[row].T.astype(BF16)


def over_bands(blocks):
    moved = [blocks[0]]
    for k, block in enumerate(blocks):
        if k:
            moved.append(exchange(block, "band", k))
    return moved


def gather(cells):
    cores = lax.axis_size("chan")
    near, far = [cells], []
    for k in range(1, cores):
        near.append(exchange(cells, "chan", k))
    chips = []
    for k in range(1, lax.axis_size("section")):
        chips.append(exchange(cells, "section", k))
    for chip in chips:
        for k in range(1, cores):
            far.append(exchange(chip, "chan", k))
    names = (
        tuple(range(cores)),
        tuple(at * cores for at in range(1, len(chips) + 1)),
        tuple(at * cores + k for at in range(1, len(chips) + 1) for k in range(1, cores)),
    )
    return list(zip(names, (near, chips, far)))


def per_device(latent, control_hint, cw1, cb1, cw2, cb2, mw1, mb1, mw2, mb2, dw1, db1, dw2, db2):
    z = Sizes(latent)
    kernel = lambda f, *a: functools.partial(f, z, *a)
    groups = len(lane_groups(z))
    single = sds((z.cells, z.per))
    pair = sds((2, z.cells, z.per))
    total = sds((z.cells, z.per), F32)
    totals = sds((2, z.cells, z.per), F32)
    message = lambda trim: z.packed(z.kept(trim))

    raw = (z.rows, z.per, z.width)
    blocks = pl.pallas_call(
        kernel(split_kernel),
        out_shape=[sds(z.packed(2 * z.rows * z.wide))] * z.bands,
        in_specs=[pl.BlockSpec(memory_space=pltpu.HBM)] * 2,
        out_specs=whole(z.bands),
        scratch_shapes=[pltpu.VMEM(raw, BF16)] * 2
        + [
            pltpu.VMEM((2, z.rows, z.width + 2 * LAYERS, z.per), F32),
            pltpu.SemaphoreType.DMA((2,)),
        ],
        compiler_params=pltpu.CompilerParams(vmem_limit_bytes=4 << 20),
    )(in_hbm(latent.swapaxes(1, 2)), in_hbm(control_hint.swapaxes(1, 2)))
    blocks = over_bands(blocks)
    cw1, mw1 = load(cw1, mw1)
    cw2, mw2 = load(cw2, mw2)
    (dw1,) = load(dw1)
    (dw2,) = load(dw2)
    state, act = call(
        kernel(join_kernel),
        [pair, sds((2,) + message(0))],
        *blocks,
        scratch=[
            pltpu.VMEM((2, groups, z.cells, LANES), F32),
            pltpu.VMEM((groups, 2 * z.rows * z.wide, LANES), F32),
        ],
    )

    def layer(step, body, received, weights, rest, partial_out, outs, sums=(), extra=(), wide=1):
        received = [(names, pieces) for names, pieces in received if names]
        for at, (names, pieces) in enumerate(received):
            end = at == len(received) - 1
            shape = (z.held, len(names) * z.span * wide)
            if len(weights) > 1:
                shape = (len(weights),) + shape
            result = call(
                kernel(body, step, names, len(sums), end),
                outs if end else partial_out,
                *pieces,
                *sums,
                *weights,
                *(rest if end else ()),
                scratch=(list(extra) if end else []) + [pltpu.VMEM(shape, BF16)],
                flops=2 * 9 * z.cells * z.per * z.per * len(names) * len(weights) * wide,
            )
            sums = (result,)
        return result

    for step, (cw, cb, mw, mb) in enumerate(((cw1, cb1, mw1, mb1), (cw2, cb2, mw2, mb2))):
        received = gather(act)
        outs = [pair, sds((2,) + message(step + 1))]
        rest = (state, cb, mb)
        state, act = layer(step, pair_kernel, received, (cw, mw), rest, totals, outs)
    received = gather(act)
    skips = {d: p for names, pieces in received for d, p in zip(names, pieces)}
    outs = [single, sds(message(3))]
    state, act = layer(2, decode_kernel, received, (dw1,), (state, db1), total, outs, wide=2)
    part = call(
        kernel(skip_kernel, 2),
        total,
        *[skips[d] for d in range(z.shards)],
        dw2,
        scratch=[pltpu.VMEM((z.held, z.depth), BF16)],
        flops=2 * 9 * z.cells * z.per * z.depth,
    )
    blocks = layer(
        3,
        last_kernel,
        gather(act),
        (dw2,),
        (state, db2),
        total,
        [sds(z.packed(z.rows * z.columns))] * z.bands,
        sums=(part,),
        extra=[pltpu.VMEM((groups, z.cells, LANES), F32)],
    )
    out = call(
        kernel(rows_kernel),
        sds(raw),
        *over_bands(blocks),
        scratch=[
            pltpu.VMEM((z.rows, z.width, z.per), F32),
            pltpu.VMEM((z.rows * z.columns, z.per), F32),
        ],
    )
    return out.swapaxes(1, 2)


def solution(mesh):
    image = P(("groups", "band"), None, CHANNEL_AXES)
    kernel = P(None, None, CHANNEL_AXES, None)
    bias = P(CHANNEL_AXES)

    return jax.shard_map(
        per_device,
        mesh=mesh,
        in_specs=(image, image) + (kernel, bias) * 6,
        out_specs=image,
        check_vma=False,
    )
```

```python
import functools

import jax
import jax.numpy as jnp
from jax import lax
from jax.experimental import pallas as pl
from jax.experimental.pallas import tpu as pltpu
from jax.sharding import PartitionSpec as P


LAYERS = 4
LANES = 128
CHANNEL_AXES = ("section", "chan")
F32 = jnp.float32
BF16 = jnp.bfloat16
TRANSPOSED = (((1,), (1,)), ((), ()))


def silu(value):
    return value * jax.nn.sigmoid(value)


def exchange(cells, axis, distance):
    count = lax.axis_size(axis)
    return lax.ppermute(cells, axis, [(i, i ^ distance) for i in range(count)])


def channel_place():
    return lax.axis_index("section") * lax.axis_size("chan") + lax.axis_index("chan")


def channel_count():
    return lax.axis_size("section") * lax.axis_size("chan")


def whole(count):
    return [pl.BlockSpec(memory_space=pltpu.VMEM)] * count


def call(kernel, outs, *args, scratch=(), flops=0):
    many = isinstance(outs, (tuple, list))
    moved = sum(a.size * a.dtype.itemsize for a in args)
    moved += sum(o.size * o.dtype.itemsize for o in (outs if many else [outs]))
    return pl.pallas_call(
        kernel,
        out_shape=outs,
        in_specs=whole(len(args)),
        out_specs=whole(len(outs)) if many else whole(1)[0],
        scratch_shapes=list(scratch),
        compiler_params=pltpu.CompilerParams(vmem_limit_bytes=20 << 20),
        cost_estimate=pl.CostEstimate(flops=flops, bytes_accessed=moved, transcendentals=0),
    )(*args)


def sds(shape, dtype=BF16):
    return jax.ShapeDtypeStruct(shape, dtype)


class Sizes:
    def __init__(self, latent):
        self.bands = lax.axis_size("band")
        self.rows, self.width, self.per = latent.shape
        self.columns = self.width // self.bands
        self.wide = self.columns + 2 * LAYERS
        self.height = self.rows * self.bands
        self.cells = self.height * self.wide
        self.held = self.cells + 2 * self.height
        self.shards = channel_count()
        self.depth = self.shards * self.per
        self.rest = self.per % LANES
        self.groups = LANES // self.rest if self.rest and LANES % self.rest == 0 else 0
        if self.per < LANES:
            self.groups = 0
        self.span = LANES
        while not self.fits():
            self.span += LANES

    def fits(self):
        last = self.depth - self.span
        self.starts = [min(j * self.per // LANES * LANES, last) for j in range(self.shards)]
        self.offsets = [j * self.per - start for j, start in enumerate(self.starts)]
        return all(offset + self.per <= self.span for offset in self.offsets)


    def rolled(self):
        return (
            self.groups > 0
            and self.per // LANES == 1
            and self.span == 2 * LANES
            and all(o % self.rest == 0 and o + self.rest <= LANES for o in self.offsets)
        )

    def part(self, cells):
        return -(-cells // (8 * self.groups)) * 8

    def packed(self, cells):
        if not self.groups:
            return (cells, self.per)
        return (cells * (self.per // LANES) + self.part(cells), LANES)

    def kept(self, trim):
        return self.cells - 2 * trim * self.height


def pick(values, owner):
    chosen = jnp.int32(values[0])
    for j, value in enumerate(values):
        chosen = jnp.where(owner == j, value, chosen)
    return chosen


def pack(z, ref, value, roll=False):
    cells = value.shape[0]
    if not z.groups:
        ref[...] = value.astype(BF16)
        return
    turn = lambda lanes: lanes
    if roll and z.rolled():
        offset = pick(z.offsets, channel_place())
        turn = lambda lanes: pltpu.roll(lanes, offset, 1)
    full = z.per // LANES
    for g in range(full):
        lanes = turn(value[:, g * LANES : (g + 1) * LANES])
        ref[g * cells : (g + 1) * cells] = lanes.astype(BF16)
    part = z.part(cells)
    rest = [value[g * part : (g + 1) * part, full * LANES :] for g in range(z.groups)]
    short = part - rest[-1].shape[0]
    if short:
        rest[-1] = jnp.concatenate([rest[-1], jnp.zeros((short, z.rest), F32)], axis=0)
    ref[full * cells :] = turn(jnp.concatenate(rest, axis=1)).astype(BF16)


def unpack(z, cells, message, put):
    if not z.groups:
        put(0, 0, message)
        return
    full = z.per // LANES
    for g in range(full):
        put(0, g * LANES, message[g * cells : (g + 1) * cells])
    part = z.part(cells)
    rest = message[full * cells :]
    for g in range(z.groups):
        rows = min(part, cells - g * part)
        put(g * part, full * LANES, rest[:rows, g * z.rest : (g + 1) * z.rest])


def masked_silu(z, state):
    value = silu(state).reshape(z.wide, z.height, z.per)
    at = lax.broadcasted_iota(jnp.int32, value.shape, 0)
    at = at + (lax.axis_index("band") * z.columns - LAYERS)
    value = jnp.where((at >= 0) & (at < z.width), value, 0.0)
    return value.reshape(-1, z.per)


def fetch(sources, targets, sems):
    copies = [
        pltpu.make_async_copy(source, target, sems.at[i])
        for i, (source, target) in enumerate(zip(sources, targets))
    ]
    for copy in copies:
        copy.start()
    for copy in copies:
        copy.wait()


def split_kernel(z, latent_hbm, hint_hbm, *refs):
    outs, (latent_ref, hint_ref, spread, sems) = refs[:-4], refs[-4:]
    fetch((latent_hbm, hint_hbm), (latent_ref, hint_ref), sems)
    latent = latent_ref[...].astype(F32)
    control = (latent + hint_ref[...].astype(F32)).astype(BF16).astype(F32)
    edge = jnp.zeros((2, z.rows, LAYERS, z.per), F32)
    spread[:, :, :LAYERS] = edge
    spread[:, :, LAYERS + z.width :] = edge
    for row in range(z.rows):
        spread[0, row, LAYERS : LAYERS + z.width] = control[row].T
        spread[1, row, LAYERS : LAYERS + z.width] = latent[row].T
    band = lax.axis_index("band")
    for k, out in enumerate(outs):
        start = pl.multiple_of((band ^ k) * z.columns, 8)
        pack(z, out, spread[:, :, pl.ds(start, z.wide)].reshape(-1, z.per))


def in_hbm(array):
    return pltpu.with_memory_space_constraint(array, pltpu.HBM)


def load_kernel(count, *refs):
    fetch(refs[:count], refs[count : 2 * count], refs[2 * count])


def load(*weights):
    count = len(weights)
    return pl.pallas_call(
        functools.partial(load_kernel, count),
        out_shape=[sds(w.shape) for w in weights],
        in_specs=[pl.BlockSpec(memory_space=pltpu.HBM)] * count,
        out_specs=whole(count),
        scratch_shapes=[pltpu.SemaphoreType.DMA((count,))],
        compiler_params=pltpu.CompilerParams(vmem_limit_bytes=1 << 20),
        cost_estimate=pl.CostEstimate(
            flops=0, bytes_accessed=2 * sum(w.size for w in weights), transcendentals=0
        ),
    )(*[in_hbm(w) for w in weights])


def lane_groups(z):
    return [(at, min(LANES, z.per - at)) for at in range(0, z.per, LANES)]


def join_kernel(z, *refs):
    blocks, (state_ref, act_ref, image, block_image) = refs[:-4], refs[-4:]
    band = lax.axis_index("band")
    size = z.rows * z.wide

    def put(row, lane, piece):
        rows, lanes = piece.shape
        group, lane = lane // LANES, lane % LANES
        block_image[group, row : row + rows, lane : lane + lanes] = piece

    for k, block in enumerate(blocks):
        unpack(z, 2 * size, block[...].astype(F32), put)
        for t in range(2):
            for row in range(z.rows):
                to = pl.ds((band ^ k) * z.rows + row, z.wide, stride=z.height)
                at = t * size + row * z.wide
                for g in range(len(lane_groups(z))):
                    image[t, g, to] = block_image[g, at : at + z.wide]
    for t in range(2):
        parts = [image[t, g][:, :n] for g, (_, n) in enumerate(lane_groups(z))]
        value = jnp.concatenate(parts, axis=1)
        state_ref[t] = value.astype(BF16)
        pack(z, act_ref.at[t], masked_silu(z, value), roll=True)


def place(z, trim, a_ref, at, message, distance):
    first = (1 + trim) * z.height
    owner = channel_place() ^ distance
    offset = pick(z.offsets, owner)
    cells = z.kept(trim)
    if z.rolled():
        main = message[:cells].astype(F32)
        rest = message[cells:].astype(F32)
        part = z.part(cells)
        turned = [rest] + [
            pltpu.roll(rest, LANES - g * z.rest, 1)[: min(part, cells - g * part)]
            for g in range(1, z.groups)
        ]
        rest = jnp.concatenate(turned, axis=0)
        lane = lax.broadcasted_iota(jnp.int32, main.shape, 1)
        low = jnp.where(lane >= offset, main, 0.0)
        high = jnp.where(lane < offset, main, jnp.where(lane < offset + z.rest, rest, 0.0))
        a_ref[first : first + cells, at : at + LANES] = low.astype(BF16)
        a_ref[first : first + cells, at + LANES : at + 2 * LANES] = high.astype(BF16)
    else:
        for known in sorted(set(z.offsets)):

            @pl.when(offset == known)
            def _():
                def put(row, lane, piece):
                    rows, lanes = piece.shape
                    lane = at + known + lane
                    row = row + first
                    a_ref[row : row + rows, lane : lane + lanes] = piece

                unpack(z, cells, message, put)

    return pick(z.starts, owner)


def clear(z, trim, a_ref):
    if z.rolled():
        first = (1 + trim) * z.height
        edge = jnp.zeros((first, a_ref.shape[1]), BF16)
        a_ref[:first] = edge
        a_ref[z.held - first :] = edge
    else:
        a_ref[...] = jnp.zeros(a_ref.shape, BF16)


def accumulate(z, trim, distances, sources, w_ref, a_ref):
    clear(z, trim, a_ref)
    slices = []
    for base, messages in sources:
        for distance, message in zip(distances, messages):
            start = place(z, trim, a_ref, len(slices) * z.span, message, distance)
            slices.append(pl.ds(pl.multiple_of(base + start, LANES), z.span))
    return convolve(z, moves(z, a_ref), taps(z, w_ref, slices))


def up(z, value):
    value = value.reshape(z.wide, z.height, -1)
    row = lax.broadcasted_iota(jnp.int32, value.shape, 1)
    return jnp.where(row == 0, 0.0, pltpu.roll(value, 1, 1)).reshape(z.cells, -1)


def down(z, value):
    value = value.reshape(z.wide, z.height, -1)
    row = lax.broadcasted_iota(jnp.int32, value.shape, 1)
    last = z.height - 1
    return jnp.where(row == last, 0.0, pltpu.roll(value, last, 1)).reshape(z.cells, -1)


def convolve(z, cells, weight):
    moved = jnp.concatenate([cells(j) for j in range(3)], axis=1)
    weights = jnp.concatenate([weight(j) for j in range(3)], axis=1)
    total = lax.dot_general(moved, weights, TRANSPOSED, preferred_element_type=F32)
    full = z.per - z.rest
    parts = []
    if full:
        above, middle, below = [total[:, i * full : (i + 1) * full] for i in range(3)]
        parts.append(middle + up(z, above) + down(z, below))
    if z.rest:
        middle, above, below = [
            total[:, 3 * full + i * z.rest : 3 * full + (i + 1) * z.rest] for i in range(3)
        ]
        parts.append(middle + up(z, above) + down(z, below))
    return jnp.concatenate(parts, axis=1) if len(parts) > 1 else parts[0]


def moves(z, a_ref):
    return lambda j: a_ref[j * z.height : j * z.height + z.cells]


def taps(z, w_ref, slices):
    full = z.per - z.rest

    def rows(j, at):
        rows = [w_ref[i, j, :full, at] for i in range(3) if full]
        if z.rest:
            rows += [w_ref[i, j, full:, at] for i in (1, 0, 2)]
        return jnp.concatenate(rows, axis=0)

    return lambda j: jnp.concatenate([rows(j, at) for at in slices], axis=1)


def finish(z, trim, state, result, bias, new_ref, act_ref):
    new = (state.astype(F32) + result + bias).astype(BF16)
    new_ref[...] = new
    edge = trim * z.height
    act = masked_silu(z, new.astype(F32))[edge : z.cells - edge]
    pack(z, act_ref, act, roll=True)


def bias_of(ref):
    return ref[...].astype(F32).reshape(1, -1)


def pair_kernel(z, trim, distances, add, end, *refs):
    n = len(distances)
    blocks, refs = refs[:n], refs[n:]
    sums, refs = refs[:add], refs[add:]
    w0, w1, *refs = refs
    if end:
        state_ref, b0, b1, new_ref, act_ref, a_ref = refs
    else:
        out_ref, a_ref = refs
    for t, w_ref in enumerate((w0, w1)):
        sources = [(0, [block[t] for block in blocks])]
        total = accumulate(z, trim, distances, sources, w_ref, a_ref.at[t])
        for other in sums:
            total = total + other[t]
        if end:
            bias = bias_of((b0, b1)[t])
            finish(z, trim + 1, state_ref[t], total, bias, new_ref.at[t], act_ref.at[t])
        else:
            out_ref[t] = total


def decode_kernel(z, trim, distances, add, end, *refs):
    n = len(distances)
    blocks, refs = refs[:n], refs[n:]
    sums, refs = refs[:add], refs[add:]
    w_ref, *refs = refs
    a_ref = refs.pop()
    sources = [(0, [block[1] for block in blocks]), (z.depth, [block[0] for block in blocks])]
    total = accumulate(z, trim, distances, sources, w_ref, a_ref)
    for other in sums:
        total = total + other[...]
    if end:
        state_ref, b_ref, new_ref, act_ref = refs
        finish(z, trim + 1, state_ref[1], total, bias_of(b_ref), new_ref, act_ref)
    else:
        refs[0][...] = total


def skip_kernel(z, trim, *refs):
    blocks, (w_ref, out_ref, a_ref) = refs[: z.shards], refs[z.shards :]
    sources = [(z.depth, [block[0] for block in blocks])]
    out_ref[...] = accumulate(z, trim, range(z.shards), sources, w_ref, a_ref)


def last_kernel(z, trim, distances, add, end, *refs):
    n = len(distances)
    blocks, refs = refs[:n], refs[n:]
    sums, refs = refs[:add], refs[add:]
    w_ref, *refs = refs
    a_ref = refs.pop()
    sources = [(0, [block[...] for block in blocks])]
    total = accumulate(z, trim, distances, sources, w_ref, a_ref)
    for other in sums:
        total = total + other[...]
    if not end:
        refs[0][...] = total
        return
    image = refs.pop()
    state_ref, b_ref, *outs = refs
    total = state_ref[...].astype(F32) + total + bias_of(b_ref)
    groups = lane_groups(z)
    for g, (lane, n) in enumerate(groups):
        image[g, :, :n] = total[:, lane : lane + n]
    band = lax.axis_index("band")
    for k, out in enumerate(outs):
        rows = []
        for row in range(z.rows):
            first = LAYERS * z.height + (band ^ k) * z.rows + row
            at = pl.ds(first, z.columns, stride=z.height)
            rows.append(
                jnp.concatenate([image[g, at][:, :n] for g, (_, n) in enumerate(groups)], axis=1)
            )
        pack(z, out, jnp.concatenate(rows, axis=0))


def rows_kernel(z, *refs):
    blocks, (out_ref, image, block_image) = refs[:-3], refs[-3:]
    band = lax.axis_index("band")

    def put(row, lane, piece):
        rows, lanes = piece.shape
        block_image[row : row + rows, lane : lane + lanes] = piece

    for k, block in enumerate(blocks):
        start = pl.multiple_of((band ^ k) * z.columns, 8)
        unpack(z, z.rows * z.columns, block[...].astype(F32), put)
        for row in range(z.rows):
            image[row, pl.ds(start, z.columns)] = block_image[
                row * z.columns : (row + 1) * z.columns
            ]
    for row in range(z.rows):
        out_ref[row] = image[row].T.astype(BF16)


def over_bands(blocks):
    moved = [blocks[0]]
    for k, block in enumerate(blocks):
        if k:
            moved.append(exchange(block, "band", k))
    return moved


def gather(cells):
    cores = lax.axis_size("chan")
    near, far = [cells], []
    for k in range(1, cores):
        near.append(exchange(cells, "chan", k))
    chips = []
    for k in range(1, lax.axis_size("section")):
        chips.append(exchange(cells, "section", k))
    for chip in chips:
        for k in range(1, cores):
            far.append(exchange(chip, "chan", k))
    names = (
        tuple(range(cores)),
        tuple(at * cores for at in range(1, len(chips) + 1)),
        tuple(at * cores + k for at in range(1, len(chips) + 1) for k in range(1, cores)),
    )
    return list(zip(names, (near, chips, far)))


def per_device(latent, control_hint, cw1, cb1, cw2, cb2, mw1, mb1, mw2, mb2, dw1, db1, dw2, db2):
    z = Sizes(latent)
    kernel = lambda f, *a: functools.partial(f, z, *a)
    groups = len(lane_groups(z))
    single = sds((z.cells, z.per))
    pair = sds((2, z.cells, z.per))
    total = sds((z.cells, z.per), F32)
    totals = sds((2, z.cells, z.per), F32)
    message = lambda trim: z.packed(z.kept(trim))

    raw = (z.rows, z.per, z.width)
    blocks = pl.pallas_call(
        kernel(split_kernel),
        out_shape=[sds(z.packed(2 * z.rows * z.wide))] * z.bands,
        in_specs=[pl.BlockSpec(memory_space=pltpu.HBM)] * 2,
        out_specs=whole(z.bands),
        scratch_shapes=[pltpu.VMEM(raw, BF16)] * 2
        + [
            pltpu.VMEM((2, z.rows, z.width + 2 * LAYERS, z.per), F32),
            pltpu.SemaphoreType.DMA((2,)),
        ],
        compiler_params=pltpu.CompilerParams(vmem_limit_bytes=4 << 20),
    )(in_hbm(latent.swapaxes(1, 2)), in_hbm(control_hint.swapaxes(1, 2)))
    blocks = over_bands(blocks)
    cw1, mw1 = load(cw1, mw1)
    cw2, mw2 = load(cw2, mw2)
    (dw1,) = load(dw1)
    (dw2,) = load(dw2)
    state, act = call(
        kernel(join_kernel),
        [pair, sds((2,) + message(0))],
        *blocks,
        scratch=[
            pltpu.VMEM((2, groups, z.cells, LANES), F32),
            pltpu.VMEM((groups, 2 * z.rows * z.wide, LANES), F32),
        ],
    )

    def layer(step, body, received, weights, rest, partial_out, outs, sums=(), extra=(), wide=1):
        received = [(names, pieces) for names, pieces in received if names]
        for at, (names, pieces) in enumerate(received):
            end = at == len(received) - 1
            shape = (z.held, len(names) * z.span * wide)
            if len(weights) > 1:
                shape = (len(weights),) + shape
            result = call(
                kernel(body, step, names, len(sums), end),
                outs if end else partial_out,
                *pieces,
                *sums,
                *weights,
                *(rest if end else ()),
                scratch=(list(extra) if end else []) + [pltpu.VMEM(shape, BF16)],
                flops=2 * 9 * z.cells * z.per * z.per * len(names) * len(weights) * wide,
            )
            sums = (result,)
        return result

    for step, (cw, cb, mw, mb) in enumerate(((cw1, cb1, mw1, mb1), (cw2, cb2, mw2, mb2))):
        received = gather(act)
        outs = [pair, sds((2,) + message(step + 1))]
        rest = (state, cb, mb)
        state, act = layer(step, pair_kernel, received, (cw, mw), rest, totals, outs)
    received = gather(act)
    skips = {d: p for names, pieces in received for d, p in zip(names, pieces)}
    outs = [single, sds(message(3))]
    state, act = layer(2, decode_kernel, received, (dw1,), (state, db1), total, outs, wide=2)
    part = call(
        kernel(skip_kernel, 2),
        total,
        *[skips[d] for d in range(z.shards)],
        dw2,
        scratch=[pltpu.VMEM((z.held, z.shards * z.span), BF16)],
        flops=2 * 9 * z.cells * z.per * z.depth,
    )
    blocks = layer(
        3,
        last_kernel,
        gather(act),
        (dw2,),
        (state, db2),
        total,
        [sds(z.packed(z.rows * z.columns))] * z.bands,
        sums=(part,),
        extra=[pltpu.VMEM((groups, z.cells, LANES), F32)],
    )
    out = call(
        kernel(rows_kernel),
        sds(raw),
        *over_bands(blocks),
        scratch=[
            pltpu.VMEM((z.rows, z.width, z.per), F32),
            pltpu.VMEM((z.rows * z.columns, z.per), F32),
        ],
    )
    return out.swapaxes(1, 2)


def solution(mesh):
    image = P(("groups", "band"), None, CHANNEL_AXES)
    kernel = P(None, None, CHANNEL_AXES, None)
    bias = P(CHANNEL_AXES)

    return jax.shard_map(
        per_device,
        mesh=mesh,
        in_specs=(image, image) + (kernel, bias) * 6,
        out_specs=image,
        check_vma=False,
    )
```

```python
import functools

import jax
import jax.numpy as jnp
from jax import lax
from jax.experimental import pallas as pl
from jax.experimental.pallas import tpu as pltpu
from jax.sharding import PartitionSpec as P


LAYERS = 4
LANES = 128
CHANNEL_AXES = ("section", "chan")
F32 = jnp.float32
BF16 = jnp.bfloat16
TRANSPOSED = (((1,), (1,)), ((), ()))


def silu(value):
    return value * jax.nn.sigmoid(value)


def exchange(cells, axis, distance):
    count = lax.axis_size(axis)
    return lax.ppermute(cells, axis, [(i, i ^ distance) for i in range(count)])


def channel_place():
    return lax.axis_index("section") * lax.axis_size("chan") + lax.axis_index("chan")


def channel_count():
    return lax.axis_size("section") * lax.axis_size("chan")


def whole(count):
    return [pl.BlockSpec(memory_space=pltpu.VMEM)] * count


def call(kernel, outs, *args, scratch=(), flops=0):
    many = isinstance(outs, (tuple, list))
    moved = sum(a.size * a.dtype.itemsize for a in args)
    moved += sum(o.size * o.dtype.itemsize for o in (outs if many else [outs]))
    return pl.pallas_call(
        kernel,
        out_shape=outs,
        in_specs=whole(len(args)),
        out_specs=whole(len(outs)) if many else whole(1)[0],
        scratch_shapes=list(scratch),
        compiler_params=pltpu.CompilerParams(vmem_limit_bytes=20 << 20),
        cost_estimate=pl.CostEstimate(flops=flops, bytes_accessed=moved, transcendentals=0),
    )(*args)


def sds(shape, dtype=BF16):
    return jax.ShapeDtypeStruct(shape, dtype)


class Sizes:
    def __init__(self, latent):
        self.bands = lax.axis_size("band")
        self.rows, self.width, self.per = latent.shape
        self.columns = self.width // self.bands
        self.wide = self.columns + 2 * LAYERS
        self.height = self.rows * self.bands
        self.cells = self.height * self.wide
        self.held = self.cells + 2 * self.height
        self.shards = channel_count()
        self.depth = self.shards * self.per
        self.rest = self.per % LANES
        self.groups = LANES // self.rest if self.rest and LANES % self.rest == 0 else 0
        if self.per < LANES:
            self.groups = 0
        self.span = LANES
        while not self.fits():
            self.span += LANES

    def fits(self):
        last = self.depth - self.span
        self.starts = [min(j * self.per // LANES * LANES, last) for j in range(self.shards)]
        self.offsets = [j * self.per - start for j, start in enumerate(self.starts)]
        return all(offset + self.per <= self.span for offset in self.offsets)


    def rolled(self):
        return (
            self.groups > 0
            and self.per // LANES == 1
            and self.span == 2 * LANES
            and all(o % self.rest == 0 and o + self.rest <= LANES for o in self.offsets)
        )

    def part(self, cells):
        return -(-cells // (8 * self.groups)) * 8

    def packed(self, cells):
        if not self.groups:
            return (cells, self.per)
        return (cells * (self.per // LANES) + self.part(cells), LANES)

    def kept(self, trim):
        return self.cells - 2 * trim * self.height


def pick(values, owner):
    chosen = jnp.int32(values[0])
    for j, value in enumerate(values):
        chosen = jnp.where(owner == j, value, chosen)
    return chosen


def pack(z, ref, value, roll=False):
    cells = value.shape[0]
    if not z.groups:
        ref[...] = value.astype(BF16)
        return
    turn = lambda lanes: lanes
    if roll and z.rolled():
        offset = pick(z.offsets, channel_place())
        turn = lambda lanes: pltpu.roll(lanes, offset, 1)
    full = z.per // LANES
    for g in range(full):
        lanes = turn(value[:, g * LANES : (g + 1) * LANES])
        ref[g * cells : (g + 1) * cells] = lanes.astype(BF16)
    part = z.part(cells)
    rest = [value[g * part : (g + 1) * part, full * LANES :] for g in range(z.groups)]
    short = part - rest[-1].shape[0]
    if short:
        rest[-1] = jnp.concatenate([rest[-1], jnp.zeros((short, z.rest), F32)], axis=0)
    ref[full * cells :] = turn(jnp.concatenate(rest, axis=1)).astype(BF16)


def unpack(z, cells, message, put):
    if not z.groups:
        put(0, 0, message)
        return
    full = z.per // LANES
    for g in range(full):
        put(0, g * LANES, message[g * cells : (g + 1) * cells])
    part = z.part(cells)
    rest = message[full * cells :]
    for g in range(z.groups):
        rows = min(part, cells - g * part)
        put(g * part, full * LANES, rest[:rows, g * z.rest : (g + 1) * z.rest])


def masked_silu(z, state):
    value = silu(state).reshape(z.wide, z.height, z.per)
    at = lax.broadcasted_iota(jnp.int32, value.shape, 0)
    at = at + (lax.axis_index("band") * z.columns - LAYERS)
    value = jnp.where((at >= 0) & (at < z.width), value, 0.0)
    return value.reshape(-1, z.per)


def fetch(sources, targets, sems):
    copies = [
        pltpu.make_async_copy(source, target, sems.at[i])
        for i, (source, target) in enumerate(zip(sources, targets))
    ]
    for copy in copies:
        copy.start()
    for copy in copies:
        copy.wait()


def split_kernel(z, latent_hbm, hint_hbm, *refs):
    outs, (latent_ref, hint_ref, spread, sems) = refs[:-4], refs[-4:]
    fetch((latent_hbm, hint_hbm), (latent_ref, hint_ref), sems)
    latent = latent_ref[...].astype(F32)
    control = (latent + hint_ref[...].astype(F32)).astype(BF16).astype(F32)
    edge = jnp.zeros((2, z.rows, LAYERS, z.per), F32)
    spread[:, :, :LAYERS] = edge
    spread[:, :, LAYERS + z.width :] = edge
    for row in range(z.rows):
        spread[0, row, LAYERS : LAYERS + z.width] = control[row].T
        spread[1, row, LAYERS : LAYERS + z.width] = latent[row].T
    band = lax.axis_index("band")
    for k, out in enumerate(outs):
        start = pl.multiple_of((band ^ k) * z.columns, 8)
        pack(z, out, spread[:, :, pl.ds(start, z.wide)].reshape(-1, z.per))


def in_hbm(array):
    return pltpu.with_memory_space_constraint(array, pltpu.HBM)


def load_kernel(count, *refs):
    fetch(refs[:count], refs[count : 2 * count], refs[2 * count])


def load(*weights):
    count = len(weights)
    return pl.pallas_call(
        functools.partial(load_kernel, count),
        out_shape=[sds(w.shape) for w in weights],
        in_specs=[pl.BlockSpec(memory_space=pltpu.HBM)] * count,
        out_specs=whole(count),
        scratch_shapes=[pltpu.SemaphoreType.DMA((count,))],
        compiler_params=pltpu.CompilerParams(vmem_limit_bytes=1 << 20),
        cost_estimate=pl.CostEstimate(
            flops=0, bytes_accessed=2 * sum(w.size for w in weights), transcendentals=0
        ),
    )(*[in_hbm(w) for w in weights])


def lane_groups(z):
    return [(at, min(LANES, z.per - at)) for at in range(0, z.per, LANES)]


def join_kernel(z, *refs):
    blocks, (*states, act_zero, act_one, image, block_image) = refs[: z.bands], refs[z.bands :]
    acts = (act_zero, act_one)
    band = lax.axis_index("band")
    size = z.rows * z.wide

    def put(row, lane, piece):
        rows, lanes = piece.shape
        group, lane = lane // LANES, lane % LANES
        block_image[group, row : row + rows, lane : lane + lanes] = piece

    for k, block in enumerate(blocks):
        unpack(z, 2 * size, block[...].astype(F32), put)
        for t in range(2):
            for row in range(z.rows):
                to = pl.ds((band ^ k) * z.rows + row, z.wide, stride=z.height)
                at = t * size + row * z.wide
                for g in range(len(lane_groups(z))):
                    image[t, g, to] = block_image[g, at : at + z.wide]
    for t in range(2):
        parts = [image[t, g][:, :n] for g, (_, n) in enumerate(lane_groups(z))]
        value = jnp.concatenate(parts, axis=1)
        states[t][...] = value.astype(BF16)
        pack(z, acts[t], masked_silu(z, value), roll=True)


def place(z, trim, a_ref, at, message, distance):
    first = (1 + trim) * z.height
    owner = channel_place() ^ distance
    offset = pick(z.offsets, owner)
    cells = z.kept(trim)
    if z.rolled():
        main = message[:cells].astype(F32)
        rest = message[cells:].astype(F32)
        part = z.part(cells)
        turned = [rest] + [
            pltpu.roll(rest, LANES - g * z.rest, 1)[: min(part, cells - g * part)]
            for g in range(1, z.groups)
        ]
        rest = jnp.concatenate(turned, axis=0)
        lane = lax.broadcasted_iota(jnp.int32, main.shape, 1)
        low = jnp.where(lane >= offset, main, 0.0)
        high = jnp.where(lane < offset, main, jnp.where(lane < offset + z.rest, rest, 0.0))
        a_ref[first : first + cells, at : at + LANES] = low.astype(BF16)
        a_ref[first : first + cells, at + LANES : at + 2 * LANES] = high.astype(BF16)
    else:
        for known in sorted(set(z.offsets)):

            @pl.when(offset == known)
            def _():
                def put(row, lane, piece):
                    rows, lanes = piece.shape
                    lane = at + known + lane
                    row = row + first
                    a_ref[row : row + rows, lane : lane + lanes] = piece

                unpack(z, cells, message, put)

    return pick(z.starts, owner)


def clear(z, trim, a_ref):
    if z.rolled():
        first = (1 + trim) * z.height
        edge = jnp.zeros((first, a_ref.shape[1]), BF16)
        a_ref[:first] = edge
        a_ref[z.held - first :] = edge
    else:
        a_ref[...] = jnp.zeros(a_ref.shape, BF16)


def accumulate(z, trim, distances, sources, w_ref, a_ref):
    clear(z, trim, a_ref)
    slices = []
    for base, messages in sources:
        for distance, message in zip(distances, messages):
            start = place(z, trim, a_ref, len(slices) * z.span, message, distance)
            slices.append(pl.ds(pl.multiple_of(base + start, LANES), z.span))
    return convolve(z, moves(z, a_ref), taps(z, w_ref, slices))


def up(z, value):
    value = value.reshape(z.wide, z.height, -1)
    row = lax.broadcasted_iota(jnp.int32, value.shape, 1)
    return jnp.where(row == 0, 0.0, pltpu.roll(value, 1, 1)).reshape(z.cells, -1)


def down(z, value):
    value = value.reshape(z.wide, z.height, -1)
    row = lax.broadcasted_iota(jnp.int32, value.shape, 1)
    last = z.height - 1
    return jnp.where(row == last, 0.0, pltpu.roll(value, last, 1)).reshape(z.cells, -1)


def convolve(z, cells, weight):
    moved = jnp.concatenate([cells(j) for j in range(3)], axis=1)
    weights = jnp.concatenate([weight(j) for j in range(3)], axis=1)
    total = lax.dot_general(moved, weights, TRANSPOSED, preferred_element_type=F32)
    full = z.per - z.rest
    parts = []
    if full:
        above, middle, below = [total[:, i * full : (i + 1) * full] for i in range(3)]
        parts.append(middle + up(z, above) + down(z, below))
    if z.rest:
        middle, above, below = [
            total[:, 3 * full + i * z.rest : 3 * full + (i + 1) * z.rest] for i in range(3)
        ]
        parts.append(middle + up(z, above) + down(z, below))
    return jnp.concatenate(parts, axis=1) if len(parts) > 1 else parts[0]


def moves(z, a_ref):
    return lambda j: a_ref[j * z.height : j * z.height + z.cells]


def taps(z, w_ref, slices):
    full = z.per - z.rest

    def rows(j, at):
        rows = [w_ref[i, j, :full, at] for i in range(3) if full]
        if z.rest:
            rows += [w_ref[i, j, full:, at] for i in (1, 0, 2)]
        return jnp.concatenate(rows, axis=0)

    return lambda j: jnp.concatenate([rows(j, at) for at in slices], axis=1)


def finish(z, trim, state, result, bias, new_ref, act_ref):
    new = (state.astype(F32) + result + bias).astype(BF16)
    new_ref[...] = new
    edge = trim * z.height
    act = masked_silu(z, new.astype(F32))[edge : z.cells - edge]
    pack(z, act_ref, act, roll=True)


def bias_of(ref):
    return ref[...].astype(F32).reshape(1, -1)


def block_kernel(z, trim, base, distances, add, end, *refs):
    n = len(distances)
    blocks, refs = refs[:n], refs[n:]
    sums, refs = refs[:add], refs[add:]
    w_ref, *refs = refs
    a_ref = refs.pop()
    sources = [(base, [block[...] for block in blocks])]
    total = accumulate(z, trim, distances, sources, w_ref, a_ref)
    for other in sums:
        total = total + other[...]
    if end:
        end(z, trim, total, *refs)
    else:
        refs[0][...] = total


def close_layer(z, trim, total, state_ref, b_ref, new_ref, act_ref):
    finish(z, trim + 1, state_ref[...], total, bias_of(b_ref), new_ref, act_ref)


def close_image(z, trim, total, *refs):
    state_ref, b_ref, *outs, image = refs
    total = state_ref[...].astype(F32) + total + bias_of(b_ref)
    groups = lane_groups(z)
    for g, (lane, n) in enumerate(groups):
        image[g, :, :n] = total[:, lane : lane + n]
    band = lax.axis_index("band")
    for k, out in enumerate(outs):
        rows = []
        for row in range(z.rows):
            first = LAYERS * z.height + (band ^ k) * z.rows + row
            at = pl.ds(first, z.columns, stride=z.height)
            rows.append(
                jnp.concatenate([image[g, at][:, :n] for g, (_, n) in enumerate(groups)], axis=1)
            )
        pack(z, out, jnp.concatenate(rows, axis=0))


def rows_kernel(z, *refs):
    blocks, (out_ref, image, block_image) = refs[:-3], refs[-3:]
    band = lax.axis_index("band")

    def put(row, lane, piece):
        rows, lanes = piece.shape
        block_image[row : row + rows, lane : lane + lanes] = piece

    for k, block in enumerate(blocks):
        start = pl.multiple_of((band ^ k) * z.columns, 8)
        unpack(z, z.rows * z.columns, block[...].astype(F32), put)
        for row in range(z.rows):
            image[row, pl.ds(start, z.columns)] = block_image[
                row * z.columns : (row + 1) * z.columns
            ]
    for row in range(z.rows):
        out_ref[row] = image[row].T.astype(BF16)


def over_bands(blocks):
    moved = [blocks[0]]
    for k, block in enumerate(blocks):
        if k:
            moved.append(exchange(block, "band", k))
    return moved


def gather(cells):
    cores = lax.axis_size("chan")
    near, far = [cells], []
    for k in range(1, cores):
        near.append(exchange(cells, "chan", k))
    chips = []
    for k in range(1, lax.axis_size("section")):
        chips.append(exchange(cells, "section", k))
    for chip in chips:
        for k in range(1, cores):
            far.append(exchange(chip, "chan", k))
    names = (
        tuple(range(cores)),
        tuple(at * cores for at in range(1, len(chips) + 1)),
        tuple(at * cores + k for at in range(1, len(chips) + 1) for k in range(1, cores)),
    )
    return list(zip(names, (near, chips, far)))


def per_device(latent, control_hint, cw1, cb1, cw2, cb2, mw1, mb1, mw2, mb2, dw1, db1, dw2, db2):
    z = Sizes(latent)
    kernel = lambda f, *a: functools.partial(f, z, *a)
    groups = len(lane_groups(z))
    single = sds((z.cells, z.per))
    total = sds((z.cells, z.per), F32)
    message = lambda trim: z.packed(z.kept(trim))

    raw = (z.rows, z.per, z.width)
    blocks = pl.pallas_call(
        kernel(split_kernel),
        out_shape=[sds(z.packed(2 * z.rows * z.wide))] * z.bands,
        in_specs=[pl.BlockSpec(memory_space=pltpu.HBM)] * 2,
        out_specs=whole(z.bands),
        scratch_shapes=[pltpu.VMEM(raw, BF16)] * 2
        + [
            pltpu.VMEM((2, z.rows, z.width + 2 * LAYERS, z.per), F32),
            pltpu.SemaphoreType.DMA((2,)),
        ],
        compiler_params=pltpu.CompilerParams(vmem_limit_bytes=4 << 20),
    )(in_hbm(latent.swapaxes(1, 2)), in_hbm(control_hint.swapaxes(1, 2)))
    blocks = over_bands(blocks)
    cw1, mw1, cw2, mw2 = load(cw1, mw1, cw2, mw2)
    *states, control, main = call(
        kernel(join_kernel),
        [single, single, sds(message(0)), sds(message(0))],
        *blocks,
        scratch=[
            pltpu.VMEM((2, groups, z.cells, LANES), F32),
            pltpu.VMEM((groups, 2 * z.rows * z.wide, LANES), F32),
        ],
    )

    def convolution(step, received, w, base, outs, end=None, rest=(), sums=(), extra=()):
        received = [(names, pieces) for names, pieces in received if names]
        for at, (names, pieces) in enumerate(received):
            ends = at == len(received) - 1
            result = call(
                kernel(block_kernel, step, base, names, len(sums), end if ends else None),
                outs if ends else total,
                *pieces,
                *sums,
                w,
                *(rest if ends else ()),
                scratch=(list(extra) if ends else [])
                + [pltpu.VMEM((z.held, len(names) * z.span), BF16)],
                flops=2 * 9 * z.cells * z.per * z.per * len(names),
            )
            sums = (result,)
        return result

    for step, (cw, cb, mw, mb) in enumerate(((cw1, cb1, mw1, mb1), (cw2, cb2, mw2, mb2))):
        outs = [single, sds(message(step + 1))]
        received = gather(control)
        rest = (states[0], cb)
        states[0], control = convolution(step, received, cw, 0, outs, close_layer, rest)
        received = gather(main)
        rest = (states[1], mb)
        states[1], main = convolution(step, received, mw, 0, outs, close_layer, rest)
    skip = gather(control)
    near, *others = skip
    merged = tuple(sum((list(part) for part in parts), []) for parts in zip(*others))
    first = convolution(2, [near, merged], dw1, z.depth, total)
    outs = [single, sds(message(3))]
    rest = (states[1], db1)
    state, act = convolution(2, gather(main), dw1, 0, outs, close_layer, rest, sums=(first,))
    every = tuple(sum((list(part) for part in parts), []) for parts in zip(*skip))
    part = convolution(2, [every], dw2, z.depth, total)
    blocks = convolution(
        3,
        gather(act),
        dw2,
        0,
        [sds(z.packed(z.rows * z.columns))] * z.bands,
        close_image,
        (state, db2),
        sums=(part,),
        extra=[pltpu.VMEM((groups, z.cells, LANES), F32)],
    )
    out = call(
        kernel(rows_kernel),
        sds(raw),
        *over_bands(blocks),
        scratch=[
            pltpu.VMEM((z.rows, z.width, z.per), F32),
            pltpu.VMEM((z.rows * z.columns, z.per), F32),
        ],
    )
    return out.swapaxes(1, 2)


def solution(mesh):
    image = P(("groups", "band"), None, CHANNEL_AXES)
    kernel = P(None, None, CHANNEL_AXES, None)
    bias = P(CHANNEL_AXES)

    return jax.shard_map(
        per_device,
        mesh=mesh,
        in_specs=(image, image) + (kernel, bias) * 6,
        out_specs=image,
        check_vma=False,
    )
```

```python
import functools

import jax
import jax.numpy as jnp
from jax import lax
from jax.experimental import pallas as pl
from jax.experimental.pallas import tpu as pltpu
from jax.sharding import PartitionSpec as P


LAYERS = 4
LANES = 128
CHANNEL_AXES = ("section", "chan")
F32 = jnp.float32
BF16 = jnp.bfloat16
TRANSPOSED = (((1,), (1,)), ((), ()))


def silu(value):
    return value * jax.nn.sigmoid(value)


def exchange(cells, axis, distance):
    count = lax.axis_size(axis)
    return lax.ppermute(cells, axis, [(i, i ^ distance) for i in range(count)])


def channel_place():
    return lax.axis_index("section") * lax.axis_size("chan") + lax.axis_index("chan")


def channel_count():
    return lax.axis_size("section") * lax.axis_size("chan")


def whole(count):
    return [pl.BlockSpec(memory_space=pltpu.VMEM)] * count


def call(kernel, outs, *args, scratch=(), flops=0):
    many = isinstance(outs, (tuple, list))
    moved = sum(a.size * a.dtype.itemsize for a in args)
    moved += sum(o.size * o.dtype.itemsize for o in (outs if many else [outs]))
    return pl.pallas_call(
        kernel,
        out_shape=outs,
        in_specs=whole(len(args)),
        out_specs=whole(len(outs)) if many else whole(1)[0],
        scratch_shapes=list(scratch),
        compiler_params=pltpu.CompilerParams(vmem_limit_bytes=20 << 20),
        cost_estimate=pl.CostEstimate(flops=flops, bytes_accessed=moved, transcendentals=0),
    )(*args)


def sds(shape, dtype=BF16):
    return jax.ShapeDtypeStruct(shape, dtype)


class Sizes:
    def __init__(self, latent):
        self.bands = lax.axis_size("band")
        self.rows, self.width, self.per = latent.shape
        self.columns = self.width // self.bands
        self.wide = self.columns + 2 * LAYERS
        self.height = self.rows * self.bands
        self.cells = self.height * self.wide
        self.held = self.cells + 2 * self.height
        self.shards = channel_count()
        self.depth = self.shards * self.per
        self.rest = self.per % LANES
        self.groups = LANES // self.rest if self.rest and LANES % self.rest == 0 else 0
        if self.per < LANES:
            self.groups = 0
        self.span = LANES
        while not self.fits():
            self.span += LANES

    def fits(self):
        last = self.depth - self.span
        self.starts = [min(j * self.per // LANES * LANES, last) for j in range(self.shards)]
        self.offsets = [j * self.per - start for j, start in enumerate(self.starts)]
        return all(offset + self.per <= self.span for offset in self.offsets)


    def rolled(self):
        return (
            self.groups > 0
            and self.per // LANES == 1
            and self.span == 2 * LANES
            and all(o % self.rest == 0 and o + self.rest <= LANES for o in self.offsets)
        )

    def part(self, cells):
        return -(-cells // (8 * self.groups)) * 8

    def packed(self, cells):
        if not self.groups:
            return (cells, self.per)
        return (cells * (self.per // LANES) + self.part(cells), LANES)

    def kept(self, trim):
        return self.cells - 2 * trim * self.height


def pick(values, owner):
    chosen = jnp.int32(values[0])
    for j, value in enumerate(values):
        chosen = jnp.where(owner == j, value, chosen)
    return chosen


def pack(z, ref, value, roll=False):
    cells = value.shape[0]
    if not z.groups:
        ref[...] = value.astype(BF16)
        return
    turn = lambda lanes: lanes
    if roll and z.rolled():
        offset = pick(z.offsets, channel_place())
        turn = lambda lanes: pltpu.roll(lanes, offset, 1)
    full = z.per // LANES
    for g in range(full):
        lanes = turn(value[:, g * LANES : (g + 1) * LANES])
        ref[g * cells : (g + 1) * cells] = lanes.astype(BF16)
    part = z.part(cells)
    rest = [value[g * part : (g + 1) * part, full * LANES :] for g in range(z.groups)]
    short = part - rest[-1].shape[0]
    if short:
        rest[-1] = jnp.concatenate([rest[-1], jnp.zeros((short, z.rest), F32)], axis=0)
    ref[full * cells :] = turn(jnp.concatenate(rest, axis=1)).astype(BF16)


def unpack(z, cells, message, put):
    if not z.groups:
        put(0, 0, message)
        return
    full = z.per // LANES
    for g in range(full):
        put(0, g * LANES, message[g * cells : (g + 1) * cells])
    part = z.part(cells)
    rest = message[full * cells :]
    for g in range(z.groups):
        rows = min(part, cells - g * part)
        put(g * part, full * LANES, rest[:rows, g * z.rest : (g + 1) * z.rest])


def masked_silu(z, state):
    value = silu(state).reshape(z.wide, z.height, z.per)
    at = lax.broadcasted_iota(jnp.int32, value.shape, 0)
    at = at + (lax.axis_index("band") * z.columns - LAYERS)
    value = jnp.where((at >= 0) & (at < z.width), value, 0.0)
    return value.reshape(-1, z.per)


def fetch(sources, targets, sems):
    copies = [
        pltpu.make_async_copy(source, target, sems.at[i])
        for i, (source, target) in enumerate(zip(sources, targets))
    ]
    for copy in copies:
        copy.start()
    for copy in copies:
        copy.wait()


def split_kernel(z, latent_hbm, hint_hbm, *refs):
    outs, (latent_ref, hint_ref, spread, sems) = refs[:-4], refs[-4:]
    fetch((latent_hbm, hint_hbm), (latent_ref, hint_ref), sems)
    latent = latent_ref[...].astype(F32)
    control = (latent + hint_ref[...].astype(F32)).astype(BF16).astype(F32)
    edge = jnp.zeros((2, z.rows, LAYERS, z.per), F32)
    spread[:, :, :LAYERS] = edge
    spread[:, :, LAYERS + z.width :] = edge
    for row in range(z.rows):
        spread[0, row, LAYERS : LAYERS + z.width] = control[row].T
        spread[1, row, LAYERS : LAYERS + z.width] = latent[row].T
    band = lax.axis_index("band")
    for k, out in enumerate(outs):
        start = pl.multiple_of((band ^ k) * z.columns, 8)
        pack(z, out, spread[:, :, pl.ds(start, z.wide)].reshape(-1, z.per))


def in_hbm(array):
    return pltpu.with_memory_space_constraint(array, pltpu.HBM)


def load_kernel(count, *refs):
    fetch(refs[:count], refs[count : 2 * count], refs[2 * count])


def load(*weights):
    count = len(weights)
    return pl.pallas_call(
        functools.partial(load_kernel, count),
        out_shape=[sds(w.shape) for w in weights],
        in_specs=[pl.BlockSpec(memory_space=pltpu.HBM)] * count,
        out_specs=whole(count),
        scratch_shapes=[pltpu.SemaphoreType.DMA((count,))],
        compiler_params=pltpu.CompilerParams(vmem_limit_bytes=1 << 20),
        cost_estimate=pl.CostEstimate(
            flops=0, bytes_accessed=2 * sum(w.size for w in weights), transcendentals=0
        ),
    )(*[in_hbm(w) for w in weights])


def lane_groups(z):
    return [(at, min(LANES, z.per - at)) for at in range(0, z.per, LANES)]


def join_kernel(z, *refs):
    blocks, (*states, act_zero, act_one, image, block_image) = refs[: z.bands], refs[z.bands :]
    acts = (act_zero, act_one)
    band = lax.axis_index("band")
    size = z.rows * z.wide

    def put(row, lane, piece):
        rows, lanes = piece.shape
        group, lane = lane // LANES, lane % LANES
        block_image[group, row : row + rows, lane : lane + lanes] = piece

    for k, block in enumerate(blocks):
        unpack(z, 2 * size, block[...].astype(F32), put)
        for t in range(2):
            for row in range(z.rows):
                to = pl.ds((band ^ k) * z.rows + row, z.wide, stride=z.height)
                at = t * size + row * z.wide
                for g in range(len(lane_groups(z))):
                    image[t, g, to] = block_image[g, at : at + z.wide]
    for t in range(2):
        parts = [image[t, g][:, :n] for g, (_, n) in enumerate(lane_groups(z))]
        value = jnp.concatenate(parts, axis=1)
        states[t][...] = value.astype(BF16)
        pack(z, acts[t], masked_silu(z, value), roll=True)


def place(z, trim, a_ref, at, message, distance):
    first = (1 + trim) * z.height
    owner = channel_place() ^ distance
    offset = pick(z.offsets, owner)
    cells = z.kept(trim)
    if z.rolled():
        main = message[:cells].astype(F32)
        rest = message[cells:].astype(F32)
        part = z.part(cells)
        turned = [rest] + [
            pltpu.roll(rest, LANES - g * z.rest, 1)[: min(part, cells - g * part)]
            for g in range(1, z.groups)
        ]
        rest = jnp.concatenate(turned, axis=0)
        lane = lax.broadcasted_iota(jnp.int32, main.shape, 1)
        low = jnp.where(lane >= offset, main, 0.0)
        high = jnp.where(lane < offset, main, jnp.where(lane < offset + z.rest, rest, 0.0))
        a_ref[first : first + cells, at : at + LANES] = low.astype(BF16)
        a_ref[first : first + cells, at + LANES : at + 2 * LANES] = high.astype(BF16)
    else:
        for known in sorted(set(z.offsets)):

            @pl.when(offset == known)
            def _():
                def put(row, lane, piece):
                    rows, lanes = piece.shape
                    lane = at + known + lane
                    row = row + first
                    a_ref[row : row + rows, lane : lane + lanes] = piece

                unpack(z, cells, message, put)

    return pick(z.starts, owner)


def clear(z, trim, a_ref):
    if z.rolled():
        first = (1 + trim) * z.height
        edge = jnp.zeros((first, a_ref.shape[1]), BF16)
        a_ref[:first] = edge
        a_ref[z.held - first :] = edge
    else:
        a_ref[...] = jnp.zeros(a_ref.shape, BF16)


def accumulate(z, trim, distances, sources, w_ref, a_ref):
    clear(z, trim, a_ref)
    slices = []
    for base, messages in sources:
        for distance, message in zip(distances, messages):
            start = place(z, trim, a_ref, len(slices) * z.span, message, distance)
            slices.append(pl.ds(pl.multiple_of(base + start, LANES), z.span))
    return convolve(z, moves(z, a_ref), taps(z, w_ref, slices))


def up(z, value):
    value = value.reshape(z.wide, z.height, -1)
    row = lax.broadcasted_iota(jnp.int32, value.shape, 1)
    return jnp.where(row == 0, 0.0, pltpu.roll(value, 1, 1)).reshape(z.cells, -1)


def down(z, value):
    value = value.reshape(z.wide, z.height, -1)
    row = lax.broadcasted_iota(jnp.int32, value.shape, 1)
    last = z.height - 1
    return jnp.where(row == last, 0.0, pltpu.roll(value, last, 1)).reshape(z.cells, -1)


def convolve(z, cells, weight):
    moved = jnp.concatenate([cells(j) for j in range(3)], axis=1)
    weights = jnp.concatenate([weight(j) for j in range(3)], axis=1)
    total = lax.dot_general(moved, weights, TRANSPOSED, preferred_element_type=F32)
    full = z.per - z.rest
    parts = []
    if full:
        above, middle, below = [total[:, i * full : (i + 1) * full] for i in range(3)]
        parts.append(middle + up(z, above) + down(z, below))
    if z.rest:
        middle, above, below = [
            total[:, 3 * full + i * z.rest : 3 * full + (i + 1) * z.rest] for i in range(3)
        ]
        parts.append(middle + up(z, above) + down(z, below))
    return jnp.concatenate(parts, axis=1) if len(parts) > 1 else parts[0]


def moves(z, a_ref):
    return lambda j: a_ref[j * z.height : j * z.height + z.cells]


def taps(z, w_ref, slices):
    full = z.per - z.rest

    def rows(j, at):
        rows = [w_ref[i, j, :full, at] for i in range(3) if full]
        if z.rest:
            rows += [w_ref[i, j, full:, at] for i in (1, 0, 2)]
        return jnp.concatenate(rows, axis=0)

    return lambda j: jnp.concatenate([rows(j, at) for at in slices], axis=1)


def send(z, trim, new, act_ref):
    edge = trim * z.height
    act = masked_silu(z, new.astype(F32))[edge : z.cells - edge]
    pack(z, act_ref, act, roll=True)


def bias_of(ref):
    return ref[...].astype(F32).reshape(1, -1)


def block_kernel(z, trim, base, distances, add, end, *refs):
    n = len(distances)
    blocks, refs = refs[:n], refs[n:]
    sums, refs = refs[:add], refs[add:]
    w_ref, *refs = refs
    a_ref = refs.pop()
    sources = [(base, [block[...] for block in blocks])]
    total = accumulate(z, trim, distances, sources, w_ref, a_ref)
    for other in sums:
        total = total + other[...]
    if end:
        end(z, trim, total, *refs)
    else:
        refs[0][...] = total


def close_layer(z, trim, total, state_ref, b_ref, new_ref, act_ref):
    new = (state_ref[...].astype(F32) + total + bias_of(b_ref)).astype(BF16)
    new_ref[...] = new
    send(z, trim + 1, new, act_ref)


def close_control(z, trim, total, state_ref, b_ref, act_ref):
    new = (state_ref[...].astype(F32) + total + bias_of(b_ref)).astype(BF16)
    send(z, trim + 1, new, act_ref)


def close_image(z, trim, total, *refs):
    state_ref, b_ref, *outs, image = refs
    total = state_ref[...].astype(F32) + total + bias_of(b_ref)
    groups = lane_groups(z)
    for g, (lane, n) in enumerate(groups):
        image[g, :, :n] = total[:, lane : lane + n]
    band = lax.axis_index("band")
    for k, out in enumerate(outs):
        rows = []
        for row in range(z.rows):
            first = LAYERS * z.height + (band ^ k) * z.rows + row
            at = pl.ds(first, z.columns, stride=z.height)
            rows.append(
                jnp.concatenate([image[g, at][:, :n] for g, (_, n) in enumerate(groups)], axis=1)
            )
        pack(z, out, jnp.concatenate(rows, axis=0))


def rows_kernel(z, *refs):
    blocks, (out_ref, image, block_image) = refs[:-3], refs[-3:]
    band = lax.axis_index("band")

    def put(row, lane, piece):
        rows, lanes = piece.shape
        block_image[row : row + rows, lane : lane + lanes] = piece

    for k, block in enumerate(blocks):
        start = pl.multiple_of((band ^ k) * z.columns, 8)
        unpack(z, z.rows * z.columns, block[...].astype(F32), put)
        for row in range(z.rows):
            image[row, pl.ds(start, z.columns)] = block_image[
                row * z.columns : (row + 1) * z.columns
            ]
    for row in range(z.rows):
        out_ref[row] = image[row].T.astype(BF16)


def over_bands(blocks):
    moved = [blocks[0]]
    for k, block in enumerate(blocks):
        if k:
            moved.append(exchange(block, "band", k))
    return moved


def gather(cells):
    cores = lax.axis_size("chan")
    near, far = [cells], []
    for k in range(1, cores):
        near.append(exchange(cells, "chan", k))
    chips = []
    for k in range(1, lax.axis_size("section")):
        chips.append(exchange(cells, "section", k))
    for chip in chips:
        for k in range(1, cores):
            far.append(exchange(chip, "chan", k))
    names = (
        tuple(range(cores)),
        tuple(at * cores for at in range(1, len(chips) + 1)),
        tuple(at * cores + k for at in range(1, len(chips) + 1) for k in range(1, cores)),
    )
    return list(zip(names, (near, chips, far)))


def together(received):
    return tuple(sum((list(part) for part in parts), []) for parts in zip(*received))


def late_together(received):
    near, *others = received
    return [near, together(others)]


def per_device(latent, control_hint, cw1, cb1, cw2, cb2, mw1, mb1, mw2, mb2, dw1, db1, dw2, db2):
    z = Sizes(latent)
    kernel = lambda f, *a: functools.partial(f, z, *a)
    groups = len(lane_groups(z))
    single = sds((z.cells, z.per))
    total = sds((z.cells, z.per), F32)
    message = lambda trim: z.packed(z.kept(trim))

    raw = (z.rows, z.per, z.width)
    blocks = pl.pallas_call(
        kernel(split_kernel),
        out_shape=[sds(z.packed(2 * z.rows * z.wide))] * z.bands,
        in_specs=[pl.BlockSpec(memory_space=pltpu.HBM)] * 2,
        out_specs=whole(z.bands),
        scratch_shapes=[pltpu.VMEM(raw, BF16)] * 2
        + [
            pltpu.VMEM((2, z.rows, z.width + 2 * LAYERS, z.per), F32),
            pltpu.SemaphoreType.DMA((2,)),
        ],
        compiler_params=pltpu.CompilerParams(vmem_limit_bytes=4 << 20),
    )(in_hbm(latent.swapaxes(1, 2)), in_hbm(control_hint.swapaxes(1, 2)))
    blocks = over_bands(blocks)
    cw1, mw1, cw2, mw2 = load(cw1, mw1, cw2, mw2)
    *states, control, main = call(
        kernel(join_kernel),
        [single, single, sds(message(0)), sds(message(0))],
        *blocks,
        scratch=[
            pltpu.VMEM((2, groups, z.cells, LANES), F32),
            pltpu.VMEM((groups, 2 * z.rows * z.wide, LANES), F32),
        ],
    )

    def convolution(step, received, w, base, outs, end=None, rest=(), sums=(), extra=()):
        received = [(names, pieces) for names, pieces in received if names]
        for at, (names, pieces) in enumerate(received):
            ends = at == len(received) - 1
            result = call(
                kernel(block_kernel, step, base, names, len(sums), end if ends else None),
                outs if ends else total,
                *pieces,
                *sums,
                w,
                *(rest if ends else ()),
                scratch=(list(extra) if ends else [])
                + [pltpu.VMEM((z.held, len(names) * z.span), BF16)],
                flops=2 * 9 * z.cells * z.per * z.per * len(names),
            )
            sums = (result,)
        return result

    for step, (cw, cb, mw, mb) in enumerate(((cw1, cb1, mw1, mb1), (cw2, cb2, mw2, mb2))):
        outs = [single, sds(message(step + 1))]
        received = gather(control)
        rest = (states[0], cb)
        if step == 0:
            states[0], control = convolution(step, received, cw, 0, outs, close_layer, rest)
        else:
            control = convolution(step, received, cw, 0, outs[1], close_control, rest)
        received = late_together(gather(main))
        rest = (states[1], mb)
        states[1], main = convolution(step, received, mw, 0, outs, close_layer, rest)
    skip = gather(control)
    first = convolution(2, late_together(skip), dw1, z.depth, total)
    outs = [single, sds(message(3))]
    rest = (states[1], db1)
    state, act = convolution(2, gather(main), dw1, 0, outs, close_layer, rest, sums=(first,))
    every = together(skip)
    part = convolution(2, [every], dw2, z.depth, total)
    blocks = convolution(
        3,
        gather(act),
        dw2,
        0,
        [sds(z.packed(z.rows * z.columns))] * z.bands,
        close_image,
        (state, db2),
        sums=(part,),
        extra=[pltpu.VMEM((groups, z.cells, LANES), F32)],
    )
    out = call(
        kernel(rows_kernel),
        sds(raw),
        *over_bands(blocks),
        scratch=[
            pltpu.VMEM((z.rows, z.width, z.per), F32),
            pltpu.VMEM((z.rows * z.columns, z.per), F32),
        ],
    )
    return out.swapaxes(1, 2)


def solution(mesh):
    image = P(("groups", "band"), None, CHANNEL_AXES)
    kernel = P(None, None, CHANNEL_AXES, None)
    bias = P(CHANNEL_AXES)

    return jax.shard_map(
        per_device,
        mesh=mesh,
        in_specs=(image, image) + (kernel, bias) * 6,
        out_specs=image,
        check_vma=False,
    )
```

```python
import functools

import jax
import jax.numpy as jnp
from jax import lax
from jax.experimental import pallas as pl
from jax.experimental.pallas import tpu as pltpu
from jax.sharding import PartitionSpec as P


LAYERS = 4
LANES = 128
CHANNEL_AXES = ("section", "chan")
F32 = jnp.float32
BF16 = jnp.bfloat16
TRANSPOSED = (((1,), (1,)), ((), ()))


def silu(value):
    return value * jax.nn.sigmoid(value)


def exchange(cells, axis, distance):
    count = lax.axis_size(axis)
    return lax.ppermute(cells, axis, [(i, i ^ distance) for i in range(count)])


def channel_place():
    return lax.axis_index("section") * lax.axis_size("chan") + lax.axis_index("chan")


def channel_count():
    return lax.axis_size("section") * lax.axis_size("chan")


def whole(count):
    return [pl.BlockSpec(memory_space=pltpu.VMEM)] * count


def call(kernel, outs, *args, scratch=(), flops=0):
    many = isinstance(outs, (tuple, list))
    moved = sum(a.size * a.dtype.itemsize for a in args)
    moved += sum(o.size * o.dtype.itemsize for o in (outs if many else [outs]))
    return pl.pallas_call(
        kernel,
        out_shape=outs,
        in_specs=whole(len(args)),
        out_specs=whole(len(outs)) if many else whole(1)[0],
        scratch_shapes=list(scratch),
        compiler_params=pltpu.CompilerParams(vmem_limit_bytes=20 << 20),
        cost_estimate=pl.CostEstimate(flops=flops, bytes_accessed=moved, transcendentals=0),
    )(*args)


def sds(shape, dtype=BF16):
    return jax.ShapeDtypeStruct(shape, dtype)


class Sizes:
    def __init__(self, latent):
        self.bands = lax.axis_size("band")
        self.rows, self.width, self.per = latent.shape
        self.columns = self.width // self.bands
        self.wide = self.columns + 2 * LAYERS
        self.height = self.rows * self.bands
        self.cells = self.height * self.wide
        self.held = self.cells + 2 * self.height
        self.shards = channel_count()
        self.depth = self.shards * self.per
        self.rest = self.per % LANES
        self.groups = LANES // self.rest if self.rest and LANES % self.rest == 0 else 0
        if self.per < LANES:
            self.groups = 0
        self.span = LANES
        while not self.fits():
            self.span += LANES

    def fits(self):
        last = self.depth - self.span
        self.starts = [min(j * self.per // LANES * LANES, last) for j in range(self.shards)]
        self.offsets = [j * self.per - start for j, start in enumerate(self.starts)]
        return all(offset + self.per <= self.span for offset in self.offsets)


    def rolled(self):
        return (
            self.groups > 0
            and self.per // LANES == 1
            and self.span == 2 * LANES
            and all(o % self.rest == 0 and o + self.rest <= LANES for o in self.offsets)
        )

    def part(self, cells):
        return -(-cells // (8 * self.groups)) * 8

    def packed(self, cells):
        if not self.groups:
            return (cells, self.per)
        return (cells * (self.per // LANES) + self.part(cells), LANES)

    def kept(self, trim):
        return self.cells - 2 * trim * self.height


def pick(values, owner):
    chosen = jnp.int32(values[0])
    for j, value in enumerate(values):
        chosen = jnp.where(owner == j, value, chosen)
    return chosen


def pack(z, ref, value, roll=False):
    cells = value.shape[0]
    if not z.groups:
        ref[...] = value.astype(BF16)
        return
    turn = lambda lanes: lanes
    if roll and z.rolled():
        offset = pick(z.offsets, channel_place())
        turn = lambda lanes: pltpu.roll(lanes, offset, 1)
    full = z.per // LANES
    for g in range(full):
        lanes = turn(value[:, g * LANES : (g + 1) * LANES])
        ref[g * cells : (g + 1) * cells] = lanes.astype(BF16)
    part = z.part(cells)
    rest = [value[g * part : (g + 1) * part, full * LANES :] for g in range(z.groups)]
    short = part - rest[-1].shape[0]
    if short:
        rest[-1] = jnp.concatenate([rest[-1], jnp.zeros((short, z.rest), F32)], axis=0)
    ref[full * cells :] = turn(jnp.concatenate(rest, axis=1)).astype(BF16)


def unpack(z, cells, message, put):
    if not z.groups:
        put(0, 0, message)
        return
    full = z.per // LANES
    for g in range(full):
        put(0, g * LANES, message[g * cells : (g + 1) * cells])
    part = z.part(cells)
    rest = message[full * cells :]
    for g in range(z.groups):
        rows = min(part, cells - g * part)
        put(g * part, full * LANES, rest[:rows, g * z.rest : (g + 1) * z.rest])


def masked_silu(z, state):
    value = silu(state).reshape(z.wide, z.height, z.per)
    at = lax.broadcasted_iota(jnp.int32, value.shape, 0)
    at = at + (lax.axis_index("band") * z.columns - LAYERS)
    value = jnp.where((at >= 0) & (at < z.width), value, 0.0)
    return value.reshape(-1, z.per)


def fetch(sources, targets, sems):
    copies = [
        pltpu.make_async_copy(source, target, sems.at[i])
        for i, (source, target) in enumerate(zip(sources, targets))
    ]
    for copy in copies:
        copy.start()
    for copy in copies:
        copy.wait()


def split_kernel(z, latent_hbm, hint_hbm, *refs):
    outs, (latent_ref, hint_ref, spread, sems) = refs[:-4], refs[-4:]
    fetch((latent_hbm, hint_hbm), (latent_ref, hint_ref), sems)
    latent = latent_ref[...].astype(F32)
    control = (latent + hint_ref[...].astype(F32)).astype(BF16).astype(F32)
    edge = jnp.zeros((2, z.rows, LAYERS, z.per), F32)
    spread[:, :, :LAYERS] = edge
    spread[:, :, LAYERS + z.width :] = edge
    for row in range(z.rows):
        spread[0, row, LAYERS : LAYERS + z.width] = control[row].T
        spread[1, row, LAYERS : LAYERS + z.width] = latent[row].T
    band = lax.axis_index("band")
    for k, out in enumerate(outs):
        start = pl.multiple_of((band ^ k) * z.columns, 8)
        pack(z, out, spread[:, :, pl.ds(start, z.wide)].reshape(-1, z.per))


def in_hbm(array):
    return pltpu.with_memory_space_constraint(array, pltpu.HBM)


def load_kernel(count, *refs):
    fetch(refs[:count], refs[count : 2 * count], refs[2 * count])


def load(*weights):
    count = len(weights)
    return pl.pallas_call(
        functools.partial(load_kernel, count),
        out_shape=[sds(w.shape) for w in weights],
        in_specs=[pl.BlockSpec(memory_space=pltpu.HBM)] * count,
        out_specs=whole(count),
        scratch_shapes=[pltpu.SemaphoreType.DMA((count,))],
        compiler_params=pltpu.CompilerParams(vmem_limit_bytes=1 << 20),
        cost_estimate=pl.CostEstimate(
            flops=0, bytes_accessed=2 * sum(w.size for w in weights), transcendentals=0
        ),
    )(*[in_hbm(w) for w in weights])


def lane_groups(z):
    return [(at, min(LANES, z.per - at)) for at in range(0, z.per, LANES)]


def join_kernel(z, t, *refs):
    blocks, (state_ref, act_ref, image, block_image) = refs[: z.bands], refs[z.bands :]
    band = lax.axis_index("band")
    size = z.rows * z.wide

    def put(row, lane, piece):
        rows, lanes = piece.shape
        group, lane = lane // LANES, lane % LANES
        if t * size < row + rows and row < (t + 1) * size:
            block_image[group, row : row + rows, lane : lane + lanes] = piece

    for k, block in enumerate(blocks):
        unpack(z, 2 * size, block[...].astype(F32), put)
        for row in range(z.rows):
            to = pl.ds((band ^ k) * z.rows + row, z.wide, stride=z.height)
            at = t * size + row * z.wide
            for g in range(len(lane_groups(z))):
                image[g, to] = block_image[g, at : at + z.wide]
    parts = [image[g][:, :n] for g, (_, n) in enumerate(lane_groups(z))]
    value = jnp.concatenate(parts, axis=1)
    state_ref[...] = value.astype(BF16)
    pack(z, act_ref, masked_silu(z, value), roll=True)


def place(z, trim, a_ref, at, message, distance):
    first = (1 + trim) * z.height
    owner = channel_place() ^ distance
    offset = pick(z.offsets, owner)
    cells = z.kept(trim)
    if z.rolled():
        main = message[:cells].astype(F32)
        rest = message[cells:].astype(F32)
        part = z.part(cells)
        turned = [rest] + [
            pltpu.roll(rest, LANES - g * z.rest, 1)[: min(part, cells - g * part)]
            for g in range(1, z.groups)
        ]
        rest = jnp.concatenate(turned, axis=0)
        lane = lax.broadcasted_iota(jnp.int32, main.shape, 1)
        low = jnp.where(lane >= offset, main, 0.0)
        high = jnp.where(lane < offset, main, jnp.where(lane < offset + z.rest, rest, 0.0))
        a_ref[first : first + cells, at : at + LANES] = low.astype(BF16)
        a_ref[first : first + cells, at + LANES : at + 2 * LANES] = high.astype(BF16)
    else:
        for known in sorted(set(z.offsets)):

            @pl.when(offset == known)
            def _():
                def put(row, lane, piece):
                    rows, lanes = piece.shape
                    lane = at + known + lane
                    row = row + first
                    a_ref[row : row + rows, lane : lane + lanes] = piece

                unpack(z, cells, message, put)

    return pick(z.starts, owner)


def clear(z, trim, a_ref):
    if z.rolled():
        first = (1 + trim) * z.height
        edge = jnp.zeros((first, a_ref.shape[1]), BF16)
        a_ref[:first] = edge
        a_ref[z.held - first :] = edge
    else:
        a_ref[...] = jnp.zeros(a_ref.shape, BF16)


def accumulate(z, trim, distances, sources, w_ref, a_ref):
    clear(z, trim, a_ref)
    slices = []
    for base, messages in sources:
        for distance, message in zip(distances, messages):
            start = place(z, trim, a_ref, len(slices) * z.span, message, distance)
            slices.append(pl.ds(pl.multiple_of(base + start, LANES), z.span))
    return convolve(z, moves(z, a_ref), taps(z, w_ref, slices))


def up(z, value):
    value = value.reshape(z.wide, z.height, -1)
    row = lax.broadcasted_iota(jnp.int32, value.shape, 1)
    return jnp.where(row == 0, 0.0, pltpu.roll(value, 1, 1)).reshape(z.cells, -1)


def down(z, value):
    value = value.reshape(z.wide, z.height, -1)
    row = lax.broadcasted_iota(jnp.int32, value.shape, 1)
    last = z.height - 1
    return jnp.where(row == last, 0.0, pltpu.roll(value, last, 1)).reshape(z.cells, -1)


def convolve(z, cells, weight):
    moved = jnp.concatenate([cells(j) for j in range(3)], axis=1)
    weights = jnp.concatenate([weight(j) for j in range(3)], axis=1)
    total = lax.dot_general(moved, weights, TRANSPOSED, preferred_element_type=F32)
    full = z.per - z.rest
    parts = []
    if full:
        above, middle, below = [total[:, i * full : (i + 1) * full] for i in range(3)]
        parts.append(middle + up(z, above) + down(z, below))
    if z.rest:
        middle, above, below = [
            total[:, 3 * full + i * z.rest : 3 * full + (i + 1) * z.rest] for i in range(3)
        ]
        parts.append(middle + up(z, above) + down(z, below))
    return jnp.concatenate(parts, axis=1) if len(parts) > 1 else parts[0]


def moves(z, a_ref):
    return lambda j: a_ref[j * z.height : j * z.height + z.cells]


def taps(z, w_ref, slices):
    full = z.per - z.rest

    def rows(j, at):
        rows = [w_ref[i, j, :full, at] for i in range(3) if full]
        if z.rest:
            rows += [w_ref[i, j, full:, at] for i in (1, 0, 2)]
        return jnp.concatenate(rows, axis=0)

    return lambda j: jnp.concatenate([rows(j, at) for at in slices], axis=1)


def send(z, trim, new, act_ref):
    edge = trim * z.height
    act = masked_silu(z, new.astype(F32))[edge : z.cells - edge]
    pack(z, act_ref, act, roll=True)


def bias_of(ref):
    return ref[...].astype(F32).reshape(1, -1)


def block_kernel(z, trim, base, distances, add, end, *refs):
    n = len(distances)
    blocks, refs = refs[:n], refs[n:]
    sums, refs = refs[:add], refs[add:]
    w_ref, *refs = refs
    a_ref = refs.pop()
    sources = [(base, [block[...] for block in blocks])]
    total = accumulate(z, trim, distances, sources, w_ref, a_ref)
    for other in sums:
        total = total + other[...]
    if end:
        end(z, trim, total, *refs)
    else:
        refs[0][...] = total


def close_layer(z, trim, total, state_ref, b_ref, new_ref, act_ref):
    new = (state_ref[...].astype(F32) + total + bias_of(b_ref)).astype(BF16)
    new_ref[...] = new
    send(z, trim + 1, new, act_ref)


def close_control(z, trim, total, state_ref, b_ref, act_ref):
    new = (state_ref[...].astype(F32) + total + bias_of(b_ref)).astype(BF16)
    send(z, trim + 1, new, act_ref)


def close_image(z, trim, total, *refs):
    state_ref, b_ref, *outs, image = refs
    total = state_ref[...].astype(F32) + total + bias_of(b_ref)
    groups = lane_groups(z)
    for g, (lane, n) in enumerate(groups):
        image[g, :, :n] = total[:, lane : lane + n]
    band = lax.axis_index("band")
    for k, out in enumerate(outs):
        rows = []
        for row in range(z.rows):
            first = LAYERS * z.height + (band ^ k) * z.rows + row
            at = pl.ds(first, z.columns, stride=z.height)
            rows.append(
                jnp.concatenate([image[g, at][:, :n] for g, (_, n) in enumerate(groups)], axis=1)
            )
        pack(z, out, jnp.concatenate(rows, axis=0))


def rows_kernel(z, *refs):
    blocks, (out_ref, image, block_image) = refs[:-3], refs[-3:]
    band = lax.axis_index("band")

    def put(row, lane, piece):
        rows, lanes = piece.shape
        block_image[row : row + rows, lane : lane + lanes] = piece

    for k, block in enumerate(blocks):
        start = pl.multiple_of((band ^ k) * z.columns, 8)
        unpack(z, z.rows * z.columns, block[...].astype(F32), put)
        for row in range(z.rows):
            image[row, pl.ds(start, z.columns)] = block_image[
                row * z.columns : (row + 1) * z.columns
            ]
    for row in range(z.rows):
        out_ref[row] = image[row].T.astype(BF16)


def over_bands(blocks):
    moved = [blocks[0]]
    for k, block in enumerate(blocks):
        if k:
            moved.append(exchange(block, "band", k))
    return moved


def gather(cells):
    cores = lax.axis_size("chan")
    near, far = [cells], []
    for k in range(1, cores):
        near.append(exchange(cells, "chan", k))
    chips = []
    for k in range(1, lax.axis_size("section")):
        chips.append(exchange(cells, "section", k))
    for chip in chips:
        for k in range(1, cores):
            far.append(exchange(chip, "chan", k))
    names = (
        tuple(range(cores)),
        tuple(at * cores for at in range(1, len(chips) + 1)),
        tuple(at * cores + k for at in range(1, len(chips) + 1) for k in range(1, cores)),
    )
    return list(zip(names, (near, chips, far)))


def together(received):
    return tuple(sum((list(part) for part in parts), []) for parts in zip(*received))


def late_together(received):
    near, *others = received
    return [near, together(others)]


def per_device(latent, control_hint, cw1, cb1, cw2, cb2, mw1, mb1, mw2, mb2, dw1, db1, dw2, db2):
    z = Sizes(latent)
    kernel = lambda f, *a: functools.partial(f, z, *a)
    groups = len(lane_groups(z))
    single = sds((z.cells, z.per))
    total = sds((z.cells, z.per), F32)
    message = lambda trim: z.packed(z.kept(trim))

    raw = (z.rows, z.per, z.width)
    blocks = pl.pallas_call(
        kernel(split_kernel),
        out_shape=[sds(z.packed(2 * z.rows * z.wide))] * z.bands,
        in_specs=[pl.BlockSpec(memory_space=pltpu.HBM)] * 2,
        out_specs=whole(z.bands),
        scratch_shapes=[pltpu.VMEM(raw, BF16)] * 2
        + [
            pltpu.VMEM((2, z.rows, z.width + 2 * LAYERS, z.per), F32),
            pltpu.SemaphoreType.DMA((2,)),
        ],
        compiler_params=pltpu.CompilerParams(vmem_limit_bytes=4 << 20),
    )(in_hbm(latent.swapaxes(1, 2)), in_hbm(control_hint.swapaxes(1, 2)))
    blocks = over_bands(blocks)
    cw1, mw1 = load(cw1, mw1)
    joined = []
    for t in range(2):
        joined.append(
            call(
                kernel(join_kernel, t),
                [single, sds(message(0))],
                *blocks,
                scratch=[
                    pltpu.VMEM((groups, z.cells, LANES), F32),
                    pltpu.VMEM((groups, 2 * z.rows * z.wide, LANES), F32),
                ],
            )
        )
    states = [state for state, _ in joined]
    control, main = [act for _, act in joined]

    def convolution(step, received, w, base, outs, end=None, rest=(), late=(), extra=()):
        received = [(names, pieces) for names, pieces in received if names]
        sums = ()
        for at, (names, pieces) in enumerate(received):
            ends = at == len(received) - 1
            sums += late if ends else ()
            result = call(
                kernel(block_kernel, step, base, names, len(sums), end if ends else None),
                outs if ends else total,
                *pieces,
                *sums,
                w,
                *(rest if ends else ()),
                scratch=(list(extra) if ends else [])
                + [pltpu.VMEM((z.held, len(names) * z.span), BF16)],
                flops=2 * 9 * z.cells * z.per * z.per * len(names),
            )
            sums = (result,)
        return result

    for step, (cw, cb, mw, mb) in enumerate(((cw1, cb1, mw1, mb1), (cw2, cb2, mw2, mb2))):
        outs = [single, sds(message(step + 1))]
        received = gather(control)
        rest = (states[0], cb)
        if step == 0:
            states[0], control = convolution(step, received, cw, 0, outs, close_layer, rest)
        else:
            control = convolution(step, received, cw, 0, outs[1], close_control, rest)
        received = gather(main)
        rest = (states[1], mb)
        states[1], main = convolution(step, received, mw, 0, outs, close_layer, rest)
    skip = gather(control)
    first = convolution(2, late_together(skip), dw1, z.depth, total)
    outs = [single, sds(message(3))]
    rest = (states[1], db1)
    state, act = convolution(2, gather(main), dw1, 0, outs, close_layer, rest, late=(first,))
    every = together(skip)
    part = convolution(2, [every], dw2, z.depth, total)
    blocks = convolution(
        3,
        gather(act),
        dw2,
        0,
        [sds(z.packed(z.rows * z.columns))] * z.bands,
        close_image,
        (state, db2),
        late=(part,),
        extra=[pltpu.VMEM((groups, z.cells, LANES), F32)],
    )
    out = call(
        kernel(rows_kernel),
        sds(raw),
        *over_bands(blocks),
        scratch=[
            pltpu.VMEM((z.rows, z.width, z.per), F32),
            pltpu.VMEM((z.rows * z.columns, z.per), F32),
        ],
    )
    return out.swapaxes(1, 2)


def solution(mesh):
    image = P(("groups", "band"), None, CHANNEL_AXES)
    kernel = P(None, None, CHANNEL_AXES, None)
    bias = P(CHANNEL_AXES)

    return jax.shard_map(
        per_device,
        mesh=mesh,
        in_specs=(image, image) + (kernel, bias) * 6,
        out_specs=image,
        check_vma=False,
    )
```

```python
import functools

import jax
import jax.numpy as jnp
from jax import lax
from jax.experimental import pallas as pl
from jax.experimental.pallas import tpu as pltpu
from jax.sharding import PartitionSpec as P


LAYERS = 4
LANES = 128
CHANNEL_AXES = ("section", "chan")
F32 = jnp.float32
BF16 = jnp.bfloat16
TRANSPOSED = (((1,), (1,)), ((), ()))


def silu(value):
    return value * jax.nn.sigmoid(value)


def exchange(cells, axis, distance):
    count = lax.axis_size(axis)
    return lax.ppermute(cells, axis, [(i, i ^ distance) for i in range(count)])


def channel_place():
    return lax.axis_index("section") * lax.axis_size("chan") + lax.axis_index("chan")


def channel_count():
    return lax.axis_size("section") * lax.axis_size("chan")


def whole(count):
    return [pl.BlockSpec(memory_space=pltpu.VMEM)] * count


def call(kernel, outs, *args, scratch=(), flops=0):
    many = isinstance(outs, (tuple, list))
    moved = sum(a.size * a.dtype.itemsize for a in args)
    moved += sum(o.size * o.dtype.itemsize for o in (outs if many else [outs]))
    return pl.pallas_call(
        kernel,
        out_shape=outs,
        in_specs=whole(len(args)),
        out_specs=whole(len(outs)) if many else whole(1)[0],
        scratch_shapes=list(scratch),
        compiler_params=pltpu.CompilerParams(vmem_limit_bytes=20 << 20),
        cost_estimate=pl.CostEstimate(flops=flops, bytes_accessed=moved, transcendentals=0),
    )(*args)


def sds(shape, dtype=BF16):
    return jax.ShapeDtypeStruct(shape, dtype)


class Sizes:
    def __init__(self, latent):
        self.bands = lax.axis_size("band")
        self.rows, self.width, self.per = latent.shape
        self.columns = self.width // self.bands
        self.wide = self.columns + 2 * LAYERS
        self.height = self.rows * self.bands
        self.cells = self.height * self.wide
        self.shards = channel_count()
        self.depth = self.shards * self.per
        self.rest = self.per % LANES
        self.groups = LANES // self.rest if self.rest and LANES % self.rest == 0 else 0
        if self.per < LANES:
            self.groups = 0
        self.span = LANES
        while not self.fits():
            self.span += LANES

    def fits(self):
        last = self.depth - self.span
        self.starts = [min(j * self.per // LANES * LANES, last) for j in range(self.shards)]
        self.offsets = [j * self.per - start for j, start in enumerate(self.starts)]
        return all(offset + self.per <= self.span for offset in self.offsets)


    def rolled(self):
        return (
            self.groups > 0
            and self.per // LANES == 1
            and self.span == 2 * LANES
            and all(o % self.rest == 0 and o + self.rest <= LANES for o in self.offsets)
        )

    def part(self, cells):
        return -(-cells // (8 * self.groups)) * 8

    def packed(self, cells):
        if not self.groups:
            return (cells, self.per)
        return (cells * (self.per // LANES) + self.part(cells), LANES)

    def kept(self, trim):
        return self.cells - 2 * trim * self.height


def pick(values, owner):
    chosen = jnp.int32(values[0])
    for j, value in enumerate(values):
        chosen = jnp.where(owner == j, value, chosen)
    return chosen


def pack(z, ref, value, roll=False):
    cells = value.shape[0]
    if not z.groups:
        ref[...] = value.astype(BF16)
        return
    turn = lambda lanes: lanes
    if roll and z.rolled():
        offset = pick(z.offsets, channel_place())
        turn = lambda lanes: pltpu.roll(lanes, offset, 1)
    full = z.per // LANES
    for g in range(full):
        lanes = turn(value[:, g * LANES : (g + 1) * LANES])
        ref[g * cells : (g + 1) * cells] = lanes.astype(BF16)
    part = z.part(cells)
    rest = [value[g * part : (g + 1) * part, full * LANES :] for g in range(z.groups)]
    short = part - rest[-1].shape[0]
    if short:
        rest[-1] = jnp.concatenate([rest[-1], jnp.zeros((short, z.rest), F32)], axis=0)
    ref[full * cells :] = turn(jnp.concatenate(rest, axis=1)).astype(BF16)


def unpack(z, cells, message, put):
    if not z.groups:
        put(0, 0, message)
        return
    full = z.per // LANES
    for g in range(full):
        put(0, g * LANES, message[g * cells : (g + 1) * cells])
    part = z.part(cells)
    rest = message[full * cells :]
    for g in range(z.groups):
        rows = min(part, cells - g * part)
        put(g * part, full * LANES, rest[:rows, g * z.rest : (g + 1) * z.rest])


def masked_silu(z, trim, state):
    value = silu(state).reshape(-1, z.height, z.per)
    at = lax.broadcasted_iota(jnp.int32, value.shape, 0)
    at = at + (lax.axis_index("band") * z.columns - LAYERS + trim)
    value = jnp.where((at >= 0) & (at < z.width), value, 0.0)
    return value.reshape(-1, z.per)


def fetch(sources, targets, sems):
    copies = [
        pltpu.make_async_copy(source, target, sems.at[i])
        for i, (source, target) in enumerate(zip(sources, targets))
    ]
    for copy in copies:
        copy.start()
    for copy in copies:
        copy.wait()


def split_kernel(z, latent_hbm, hint_hbm, *refs):
    outs, (latent_ref, hint_ref, spread, sems) = refs[:-4], refs[-4:]
    fetch((latent_hbm, hint_hbm), (latent_ref, hint_ref), sems)
    latent = latent_ref[...].astype(F32)
    control = (latent + hint_ref[...].astype(F32)).astype(BF16).astype(F32)
    edge = jnp.zeros((2, z.rows, LAYERS, z.per), F32)
    spread[:, :, :LAYERS] = edge
    spread[:, :, LAYERS + z.width :] = edge
    for row in range(z.rows):
        spread[0, row, LAYERS : LAYERS + z.width] = control[row].T
        spread[1, row, LAYERS : LAYERS + z.width] = latent[row].T
    band = lax.axis_index("band")
    for k, out in enumerate(outs):
        start = pl.multiple_of((band ^ k) * z.columns, 8)
        pack(z, out, spread[:, :, pl.ds(start, z.wide)].reshape(-1, z.per))


def in_hbm(array):
    return pltpu.with_memory_space_constraint(array, pltpu.HBM)


def load_kernel(count, *refs):
    fetch(refs[:count], refs[count : 2 * count], refs[2 * count])


def load(*weights):
    count = len(weights)
    return pl.pallas_call(
        functools.partial(load_kernel, count),
        out_shape=[sds(w.shape) for w in weights],
        in_specs=[pl.BlockSpec(memory_space=pltpu.HBM)] * count,
        out_specs=whole(count),
        scratch_shapes=[pltpu.SemaphoreType.DMA((count,))],
        compiler_params=pltpu.CompilerParams(vmem_limit_bytes=1 << 20),
        cost_estimate=pl.CostEstimate(
            flops=0, bytes_accessed=2 * sum(w.size for w in weights), transcendentals=0
        ),
    )(*[in_hbm(w) for w in weights])


def lane_groups(z):
    return [(at, min(LANES, z.per - at)) for at in range(0, z.per, LANES)]


def join_kernel(z, t, *refs):
    blocks, (state_ref, act_ref, image, block_image) = refs[: z.bands], refs[z.bands :]
    band = lax.axis_index("band")
    size = z.rows * z.wide

    def put(row, lane, piece):
        rows, lanes = piece.shape
        group, lane = lane // LANES, lane % LANES
        if t * size < row + rows and row < (t + 1) * size:
            block_image[group, row : row + rows, lane : lane + lanes] = piece

    for k, block in enumerate(blocks):
        unpack(z, 2 * size, block[...].astype(F32), put)
        for row in range(z.rows):
            to = pl.ds((band ^ k) * z.rows + row, z.wide, stride=z.height)
            at = t * size + row * z.wide
            for g in range(len(lane_groups(z))):
                image[g, to] = block_image[g, at : at + z.wide]
    parts = [image[g][:, :n] for g, (_, n) in enumerate(lane_groups(z))]
    value = jnp.concatenate(parts, axis=1)
    state_ref[...] = value.astype(BF16)
    pack(z, act_ref, masked_silu(z, 0, value), roll=True)


def place(z, trim, a_ref, at, message, distance):
    owner = channel_place() ^ distance
    offset = pick(z.offsets, owner)
    cells = z.kept(trim)
    if z.rolled():
        main = message[:cells].astype(F32)
        rest = message[cells:].astype(F32)
        part = z.part(cells)
        turned = [rest] + [
            pltpu.roll(rest, LANES - g * z.rest, 1)[: min(part, cells - g * part)]
            for g in range(1, z.groups)
        ]
        rest = jnp.concatenate(turned, axis=0)
        lane = lax.broadcasted_iota(jnp.int32, main.shape, 1)
        low = jnp.where(lane >= offset, main, 0.0)
        high = jnp.where(lane < offset, main, jnp.where(lane < offset + z.rest, rest, 0.0))
        a_ref[:, at : at + LANES] = low.astype(BF16)
        a_ref[:, at + LANES : at + 2 * LANES] = high.astype(BF16)
    else:
        for known in sorted(set(z.offsets)):

            @pl.when(offset == known)
            def _():
                def put(row, lane, piece):
                    rows, lanes = piece.shape
                    lane = at + known + lane
                    a_ref[row : row + rows, lane : lane + lanes] = piece

                unpack(z, cells, message, put)

    return pick(z.starts, owner)


def accumulate(z, trim, drop, distances, sources, w_ref, a_ref):
    if not z.rolled():
        a_ref[...] = jnp.zeros(a_ref.shape, BF16)
    slices = []
    for base, messages in sources:
        for distance, message in zip(distances, messages):
            start = place(z, trim, a_ref, len(slices) * z.span, message, distance)
            slices.append(pl.ds(pl.multiple_of(base + start, LANES), z.span))
    return convolve(z, moves(z, trim, drop, a_ref), taps(z, w_ref, slices))


def up(z, value):
    cells = value.shape[0]
    value = value.reshape(cells // z.height, z.height, -1)
    row = lax.broadcasted_iota(jnp.int32, value.shape, 1)
    return jnp.where(row == 0, 0.0, pltpu.roll(value, 1, 1)).reshape(cells, -1)


def down(z, value):
    cells = value.shape[0]
    value = value.reshape(cells // z.height, z.height, -1)
    row = lax.broadcasted_iota(jnp.int32, value.shape, 1)
    last = z.height - 1
    return jnp.where(row == last, 0.0, pltpu.roll(value, last, 1)).reshape(cells, -1)


def convolve(z, cells, weight):
    moved = jnp.concatenate([cells(j) for j in range(3)], axis=1)
    weights = jnp.concatenate([weight(j) for j in range(3)], axis=1)
    total = lax.dot_general(moved, weights, TRANSPOSED, preferred_element_type=F32)
    full = z.per - z.rest
    parts = []
    if full:
        above, middle, below = [total[:, i * full : (i + 1) * full] for i in range(3)]
        parts.append(middle + up(z, above) + down(z, below))
    if z.rest:
        middle, above, below = [
            total[:, 3 * full + i * z.rest : 3 * full + (i + 1) * z.rest] for i in range(3)
        ]
        parts.append(middle + up(z, above) + down(z, below))
    return jnp.concatenate(parts, axis=1) if len(parts) > 1 else parts[0]


def moves(z, trim, drop, a_ref):
    cells = z.kept(trim + 1 + drop)
    return lambda j: a_ref[(j + drop) * z.height : (j + drop) * z.height + cells]


def taps(z, w_ref, slices):
    full = z.per - z.rest

    def rows(j, at):
        rows = [w_ref[i, j, :full, at] for i in range(3) if full]
        if z.rest:
            rows += [w_ref[i, j, full:, at] for i in (1, 0, 2)]
        return jnp.concatenate(rows, axis=0)

    return lambda j: jnp.concatenate([rows(j, at) for at in slices], axis=1)


def send(z, trim, new, act_ref):
    pack(z, act_ref, masked_silu(z, trim, new.astype(F32)), roll=True)


def inner(z, trim, state_ref):
    return state_ref[z.height : z.height + z.kept(trim + 1)].astype(F32)


def bias_of(ref):
    return ref[...].astype(F32).reshape(1, -1)


def block_kernel(z, trim, drop, base, distances, add, end, *refs):
    n = len(distances)
    blocks, refs = refs[:n], refs[n:]
    sums, refs = refs[:add], refs[add:]
    w_ref, *refs = refs
    a_ref = refs.pop()
    sources = [(base, [block[...] for block in blocks])]
    total = accumulate(z, trim, drop, distances, sources, w_ref, a_ref)
    for other in sums:
        total = total + other[...]
    if end:
        end(z, trim, total, *refs)
    else:
        refs[0][...] = total


def close_layer(z, trim, total, state_ref, b_ref, new_ref, act_ref):
    new = (inner(z, trim, state_ref) + total + bias_of(b_ref)).astype(BF16)
    new_ref[...] = new
    send(z, trim + 1, new, act_ref)


def close_control(z, trim, total, state_ref, b_ref, act_ref):
    new = (inner(z, trim, state_ref) + total + bias_of(b_ref)).astype(BF16)
    send(z, trim + 1, new, act_ref)


def close_image(z, trim, total, *refs):
    state_ref, b_ref, *outs, image = refs
    total = inner(z, trim, state_ref) + total + bias_of(b_ref)
    groups = lane_groups(z)
    for g, (lane, n) in enumerate(groups):
        image[g, :, :n] = total[:, lane : lane + n]
    band = lax.axis_index("band")
    for k, out in enumerate(outs):
        rows = []
        for row in range(z.rows):
            first = (band ^ k) * z.rows + row
            at = pl.ds(first, z.columns, stride=z.height)
            rows.append(
                jnp.concatenate([image[g, at][:, :n] for g, (_, n) in enumerate(groups)], axis=1)
            )
        pack(z, out, jnp.concatenate(rows, axis=0))


def rows_kernel(z, *refs):
    blocks, (out_ref, image, block_image) = refs[:-3], refs[-3:]
    band = lax.axis_index("band")

    def put(row, lane, piece):
        rows, lanes = piece.shape
        block_image[row : row + rows, lane : lane + lanes] = piece

    for k, block in enumerate(blocks):
        start = pl.multiple_of((band ^ k) * z.columns, 8)
        unpack(z, z.rows * z.columns, block[...].astype(F32), put)
        for row in range(z.rows):
            image[row, pl.ds(start, z.columns)] = block_image[
                row * z.columns : (row + 1) * z.columns
            ]
    for row in range(z.rows):
        out_ref[row] = image[row].T.astype(BF16)


def over_bands(blocks):
    moved = [blocks[0]]
    for k, block in enumerate(blocks):
        if k:
            moved.append(exchange(block, "band", k))
    return moved


def gather(cells):
    cores = lax.axis_size("chan")
    near, far = [cells], []
    for k in range(1, cores):
        near.append(exchange(cells, "chan", k))
    chips = []
    for k in range(1, lax.axis_size("section")):
        chips.append(exchange(cells, "section", k))
    for chip in chips:
        for k in range(1, cores):
            far.append(exchange(chip, "chan", k))
    names = (
        tuple(range(cores)),
        tuple(at * cores for at in range(1, len(chips) + 1)),
        tuple(at * cores + k for at in range(1, len(chips) + 1) for k in range(1, cores)),
    )
    return list(zip(names, (near, chips, far)))


def together(received):
    return tuple(sum((list(part) for part in parts), []) for parts in zip(*received))


def late_together(received):
    near, *others = received
    return [near, together(others)]


def per_device(latent, control_hint, cw1, cb1, cw2, cb2, mw1, mb1, mw2, mb2, dw1, db1, dw2, db2):
    z = Sizes(latent)
    kernel = lambda f, *a: functools.partial(f, z, *a)
    groups = len(lane_groups(z))
    state_of = lambda trim: sds((z.kept(trim), z.per))
    message = lambda trim: z.packed(z.kept(trim))

    raw = (z.rows, z.per, z.width)
    blocks = pl.pallas_call(
        kernel(split_kernel),
        out_shape=[sds(z.packed(2 * z.rows * z.wide))] * z.bands,
        in_specs=[pl.BlockSpec(memory_space=pltpu.HBM)] * 2,
        out_specs=whole(z.bands),
        scratch_shapes=[pltpu.VMEM(raw, BF16)] * 2
        + [
            pltpu.VMEM((2, z.rows, z.width + 2 * LAYERS, z.per), F32),
            pltpu.SemaphoreType.DMA((2,)),
        ],
        compiler_params=pltpu.CompilerParams(vmem_limit_bytes=4 << 20),
    )(in_hbm(latent.swapaxes(1, 2)), in_hbm(control_hint.swapaxes(1, 2)))
    blocks = over_bands(blocks)
    cw1, mw1, mw2 = load(cw1, mw1, mw2)
    joined = []
    for t in range(2):
        joined.append(
            call(
                kernel(join_kernel, t),
                [state_of(0), sds(message(0))],
                *blocks,
                scratch=[
                    pltpu.VMEM((groups, z.cells, LANES), F32),
                    pltpu.VMEM((groups, 2 * z.rows * z.wide, LANES), F32),
                ],
            )
        )
    states = [state for state, _ in joined]
    control, main = [act for _, act in joined]

    def convolution(
        step, received, w, base, outs=None, end=None, rest=(), late=(), extra=(), drop=0
    ):
        received = [(names, pieces) for names, pieces in received if names]
        sums = ()
        total = sds((z.kept(step + 1 + drop), z.per), F32)
        for at, (names, pieces) in enumerate(received):
            ends = at == len(received) - 1
            sums += late if ends else ()
            result = call(
                kernel(block_kernel, step, drop, base, names, len(sums), end if ends else None),
                outs if ends and end else total,
                *pieces,
                *sums,
                w,
                *(rest if ends else ()),
                scratch=(list(extra) if ends else [])
                + [pltpu.VMEM((z.kept(step), len(names) * z.span), BF16)],
                flops=2 * 9 * z.cells * z.per * z.per * len(names),
            )
            sums = (result,)
        return result

    for step, (cw, cb, mw, mb) in enumerate(((cw1, cb1, mw1, mb1), (cw2, cb2, mw2, mb2))):
        outs = [state_of(step + 1), sds(message(step + 1))]
        received = gather(control)
        rest = (states[0], cb)
        if step == 0:
            states[0], control = convolution(step, received, cw, 0, outs, close_layer, rest)
        else:
            control = convolution(step, received, cw, 0, outs[1], close_control, rest)
        received = late_together(gather(main))
        rest = (states[1], mb)
        states[1], main = convolution(step, received, mw, 0, outs, close_layer, rest)
    skip = gather(control)
    first = convolution(2, late_together(skip), dw1, z.depth)
    outs = [state_of(3), sds(message(3))]
    rest = (states[1], db1)
    state, act = convolution(2, gather(main), dw1, 0, outs, close_layer, rest, late=(first,))
    every = together(skip)
    part = convolution(2, [every], dw2, z.depth, drop=1)
    blocks = convolution(
        3,
        gather(act),
        dw2,
        0,
        [sds(z.packed(z.rows * z.columns))] * z.bands,
        close_image,
        (state, db2),
        late=(part,),
        extra=[pltpu.VMEM((groups, z.kept(LAYERS), LANES), F32)],
    )
    out = call(
        kernel(rows_kernel),
        sds(raw),
        *over_bands(blocks),
        scratch=[
            pltpu.VMEM((z.rows, z.width, z.per), F32),
            pltpu.VMEM((z.rows * z.columns, z.per), F32),
        ],
    )
    return out.swapaxes(1, 2)


def solution(mesh):
    image = P(("groups", "band"), None, CHANNEL_AXES)
    kernel = P(None, None, CHANNEL_AXES, None)
    bias = P(CHANNEL_AXES)

    return jax.shard_map(
        per_device,
        mesh=mesh,
        in_specs=(image, image) + (kernel, bias) * 6,
        out_specs=image,
        check_vma=False,
    )
```

```python
import functools

import jax
import jax.numpy as jnp
from jax import lax
from jax.experimental import pallas as pl
from jax.experimental.pallas import tpu as pltpu
from jax.sharding import PartitionSpec as P


LAYERS = 4
LANES = 128
CHANNEL_AXES = ("section", "chan")
F32 = jnp.float32
BF16 = jnp.bfloat16
TRANSPOSED = (((1,), (1,)), ((), ()))


def silu(value):
    return value * jax.nn.sigmoid(value)


def exchange(cells, axis, distance):
    count = lax.axis_size(axis)
    return lax.ppermute(cells, axis, [(i, i ^ distance) for i in range(count)])


def channel_place():
    return lax.axis_index("section") * lax.axis_size("chan") + lax.axis_index("chan")


def channel_count():
    return lax.axis_size("section") * lax.axis_size("chan")


def whole(count):
    return [pl.BlockSpec(memory_space=pltpu.VMEM)] * count


def call(kernel, outs, *args, scratch=(), flops=0):
    many = isinstance(outs, (tuple, list))
    moved = sum(a.size * a.dtype.itemsize for a in args)
    moved += sum(o.size * o.dtype.itemsize for o in (outs if many else [outs]))
    return pl.pallas_call(
        kernel,
        out_shape=outs,
        in_specs=whole(len(args)),
        out_specs=whole(len(outs)) if many else whole(1)[0],
        scratch_shapes=list(scratch),
        compiler_params=pltpu.CompilerParams(vmem_limit_bytes=20 << 20),
        cost_estimate=pl.CostEstimate(flops=flops, bytes_accessed=moved, transcendentals=0),
    )(*args)


def sds(shape, dtype=BF16):
    return jax.ShapeDtypeStruct(shape, dtype)


class Sizes:
    def __init__(self, latent):
        self.bands = lax.axis_size("band")
        self.rows, self.width, self.per = latent.shape
        self.columns = self.width // self.bands
        self.wide = self.columns + 2 * LAYERS
        self.height = self.rows * self.bands
        self.cells = self.height * self.wide
        self.shards = channel_count()
        self.depth = self.shards * self.per
        self.rest = self.per % LANES
        self.groups = LANES // self.rest if self.rest and LANES % self.rest == 0 else 0
        if self.per < LANES:
            self.groups = 0
        self.span = LANES
        while not self.fits():
            self.span += LANES

    def fits(self):
        last = self.depth - self.span
        self.starts = [min(j * self.per // LANES * LANES, last) for j in range(self.shards)]
        self.offsets = [j * self.per - start for j, start in enumerate(self.starts)]
        return all(offset + self.per <= self.span for offset in self.offsets)


    def rolled(self):
        return (
            self.groups > 0
            and self.per // LANES == 1
            and self.span == 2 * LANES
            and all(o % self.rest == 0 and o + self.rest <= LANES for o in self.offsets)
        )

    def part(self, cells):
        return -(-cells // (8 * self.groups)) * 8

    def packed(self, cells):
        if not self.groups:
            return (cells, self.per)
        return (cells * (self.per // LANES) + self.part(cells), LANES)

    def kept(self, trim):
        return self.cells - 2 * trim * self.height


def pick(values, owner):
    chosen = jnp.int32(values[0])
    for j, value in enumerate(values):
        chosen = jnp.where(owner == j, value, chosen)
    return chosen


def pack(z, ref, value, roll=False):
    cells = value.shape[0]
    if not z.groups:
        ref[...] = value.astype(BF16)
        return
    turn = lambda lanes: lanes
    if roll and z.rolled():
        offset = pick(z.offsets, channel_place())
        turn = lambda lanes: pltpu.roll(lanes, offset, 1)
    full = z.per // LANES
    for g in range(full):
        lanes = turn(value[:, g * LANES : (g + 1) * LANES])
        ref[g * cells : (g + 1) * cells] = lanes.astype(BF16)
    part = z.part(cells)
    rest = [value[g * part : (g + 1) * part, full * LANES :] for g in range(z.groups)]
    short = part - rest[-1].shape[0]
    if short:
        rest[-1] = jnp.concatenate([rest[-1], jnp.zeros((short, z.rest), F32)], axis=0)
    ref[full * cells :] = turn(jnp.concatenate(rest, axis=1)).astype(BF16)


def unpack(z, cells, message, put):
    if not z.groups:
        put(0, 0, message)
        return
    full = z.per // LANES
    for g in range(full):
        put(0, g * LANES, message[g * cells : (g + 1) * cells])
    part = z.part(cells)
    rest = message[full * cells :]
    for g in range(z.groups):
        rows = min(part, cells - g * part)
        put(g * part, full * LANES, rest[:rows, g * z.rest : (g + 1) * z.rest])


def masked_silu(z, trim, state):
    value = silu(state).reshape(-1, z.height, z.per)
    at = lax.broadcasted_iota(jnp.int32, value.shape, 0)
    at = at + (lax.axis_index("band") * z.columns - LAYERS + trim)
    value = jnp.where((at >= 0) & (at < z.width), value, 0.0)
    return value.reshape(-1, z.per)


def fetch(sources, targets, sems):
    copies = [
        pltpu.make_async_copy(source, target, sems.at[i])
        for i, (source, target) in enumerate(zip(sources, targets))
    ]
    for copy in copies:
        copy.start()
    for copy in copies:
        copy.wait()


def split_kernel(z, latent_hbm, hint_hbm, *refs):
    outs, (latent_ref, hint_ref, spread, sems) = refs[:-4], refs[-4:]
    fetch((latent_hbm, hint_hbm), (latent_ref, hint_ref), sems)
    latent = latent_ref[...].astype(F32)
    control = (latent + hint_ref[...].astype(F32)).astype(BF16).astype(F32)
    edge = jnp.zeros((2, z.rows, LAYERS, z.per), F32)
    spread[:, :, :LAYERS] = edge
    spread[:, :, LAYERS + z.width :] = edge
    for row in range(z.rows):
        spread[0, row, LAYERS : LAYERS + z.width] = control[row].T
        spread[1, row, LAYERS : LAYERS + z.width] = latent[row].T
    band = lax.axis_index("band")
    for k, out in enumerate(outs):
        start = pl.multiple_of((band ^ k) * z.columns, 8)
        pack(z, out, spread[:, :, pl.ds(start, z.wide)].reshape(-1, z.per))


def in_hbm(array):
    return pltpu.with_memory_space_constraint(array, pltpu.HBM)


def load_kernel(count, *refs):
    fetch(refs[:count], refs[count : 2 * count], refs[2 * count])


def load(*weights):
    count = len(weights)
    return pl.pallas_call(
        functools.partial(load_kernel, count),
        out_shape=[sds(w.shape) for w in weights],
        in_specs=[pl.BlockSpec(memory_space=pltpu.HBM)] * count,
        out_specs=whole(count),
        scratch_shapes=[pltpu.SemaphoreType.DMA((count,))],
        compiler_params=pltpu.CompilerParams(vmem_limit_bytes=1 << 20),
        cost_estimate=pl.CostEstimate(
            flops=0, bytes_accessed=2 * sum(w.size for w in weights), transcendentals=0
        ),
    )(*[in_hbm(w) for w in weights])


def lane_groups(z):
    return [(at, min(LANES, z.per - at)) for at in range(0, z.per, LANES)]


def join_kernel(z, t, *refs):
    blocks, (state_ref, act_ref, image, block_image) = refs[: z.bands], refs[z.bands :]
    band = lax.axis_index("band")
    size = z.rows * z.wide

    def put(row, lane, piece):
        rows, lanes = piece.shape
        group, lane = lane // LANES, lane % LANES
        if t * size < row + rows and row < (t + 1) * size:
            block_image[group, row : row + rows, lane : lane + lanes] = piece

    for k, block in enumerate(blocks):
        unpack(z, 2 * size, block[...].astype(F32), put)
        for row in range(z.rows):
            to = pl.ds((band ^ k) * z.rows + row, z.wide, stride=z.height)
            at = t * size + row * z.wide
            for g in range(len(lane_groups(z))):
                image[g, to] = block_image[g, at : at + z.wide]
    parts = [image[g][:, :n] for g, (_, n) in enumerate(lane_groups(z))]
    value = jnp.concatenate(parts, axis=1)
    state_ref[...] = value.astype(BF16)
    pack(z, act_ref, masked_silu(z, 0, value), roll=True)


def place(z, trim, a_ref, at, message, distance):
    owner = channel_place() ^ distance
    offset = pick(z.offsets, owner)
    cells = z.kept(trim)
    if z.rolled():
        main = message[:cells].astype(F32)
        rest = message[cells:].astype(F32)
        part = z.part(cells)
        turned = [rest] + [
            pltpu.roll(rest, LANES - g * z.rest, 1)[: min(part, cells - g * part)]
            for g in range(1, z.groups)
        ]
        rest = jnp.concatenate(turned, axis=0)
        lane = lax.broadcasted_iota(jnp.int32, main.shape, 1)
        low = jnp.where(lane >= offset, main, 0.0)
        high = jnp.where(lane < offset, main, jnp.where(lane < offset + z.rest, rest, 0.0))
        a_ref[:, at : at + LANES] = low.astype(BF16)
        a_ref[:, at + LANES : at + 2 * LANES] = high.astype(BF16)
    else:
        for known in sorted(set(z.offsets)):

            @pl.when(offset == known)
            def _():
                def put(row, lane, piece):
                    rows, lanes = piece.shape
                    lane = at + known + lane
                    a_ref[row : row + rows, lane : lane + lanes] = piece

                unpack(z, cells, message, put)

    return pick(z.starts, owner)


def accumulate(z, trim, drop, distances, sources, w_ref, a_ref):
    if not z.rolled():
        a_ref[...] = jnp.zeros(a_ref.shape, BF16)
    slices = []
    for base, messages in sources:
        for distance, message in zip(distances, messages):
            start = place(z, trim, a_ref, len(slices) * z.span, message, distance)
            slices.append(pl.ds(pl.multiple_of(base + start, LANES), z.span))
    return convolve(z, moves(z, trim, drop, a_ref), taps(z, w_ref, slices))


def up(z, value):
    cells = value.shape[0]
    value = value.reshape(cells // z.height, z.height, -1)
    row = lax.broadcasted_iota(jnp.int32, value.shape, 1)
    return jnp.where(row == 0, 0.0, pltpu.roll(value, 1, 1)).reshape(cells, -1)


def down(z, value):
    cells = value.shape[0]
    value = value.reshape(cells // z.height, z.height, -1)
    row = lax.broadcasted_iota(jnp.int32, value.shape, 1)
    last = z.height - 1
    return jnp.where(row == last, 0.0, pltpu.roll(value, last, 1)).reshape(cells, -1)


def convolve(z, cells, weight):
    moved = jnp.concatenate([cells(j) for j in range(3)], axis=1)
    weights = jnp.concatenate([weight(j) for j in range(3)], axis=1)
    total = lax.dot_general(moved, weights, TRANSPOSED, preferred_element_type=F32)
    full = z.per - z.rest
    parts = []
    if full:
        above, middle, below = [total[:, i * full : (i + 1) * full] for i in range(3)]
        parts.append(middle + up(z, above) + down(z, below))
    if z.rest:
        middle, above, below = [
            total[:, 3 * full + i * z.rest : 3 * full + (i + 1) * z.rest] for i in range(3)
        ]
        parts.append(middle + up(z, above) + down(z, below))
    return jnp.concatenate(parts, axis=1) if len(parts) > 1 else parts[0]


def moves(z, trim, drop, a_ref):
    cells = z.kept(trim + 1 + drop)
    return lambda j: a_ref[(j + drop) * z.height : (j + drop) * z.height + cells]


def taps(z, w_ref, slices):
    full = z.per - z.rest

    def rows(j, at):
        rows = [w_ref[i, j, :full, at] for i in range(3) if full]
        if z.rest:
            rows += [w_ref[i, j, full:, at] for i in (1, 0, 2)]
        return jnp.concatenate(rows, axis=0)

    return lambda j: jnp.concatenate([rows(j, at) for at in slices], axis=1)


def send(z, trim, new, act_ref):
    pack(z, act_ref, masked_silu(z, trim, new.astype(F32)), roll=True)


def inner(z, trim, state_ref):
    return state_ref[z.height : z.height + z.kept(trim + 1)].astype(F32)


def bias_of(ref):
    return ref[...].astype(F32).reshape(1, -1)


def block_kernel(z, trim, drop, base, distances, add, end, *refs):
    n = len(distances)
    blocks, refs = refs[:n], refs[n:]
    sums, refs = refs[:add], refs[add:]
    w_ref, *refs = refs
    a_ref = refs.pop()
    sources = [(base, [block[...] for block in blocks])]
    total = accumulate(z, trim, drop, distances, sources, w_ref, a_ref)
    for other in sums:
        total = total + other[...]
    if end:
        end(z, trim, total, *refs)
    else:
        refs[0][...] = total


def close_layer(z, trim, total, state_ref, b_ref, new_ref, act_ref):
    new = (inner(z, trim, state_ref) + total + bias_of(b_ref)).astype(BF16)
    new_ref[...] = new
    send(z, trim + 1, new, act_ref)


def close_control(z, trim, total, state_ref, b_ref, act_ref):
    new = (inner(z, trim, state_ref) + total + bias_of(b_ref)).astype(BF16)
    send(z, trim + 1, new, act_ref)


def close_image(z, trim, total, *refs):
    state_ref, b_ref, *outs, image = refs
    total = inner(z, trim, state_ref) + total + bias_of(b_ref)
    groups = lane_groups(z)
    for g, (lane, n) in enumerate(groups):
        image[g, :, :n] = total[:, lane : lane + n]
    band = lax.axis_index("band")
    for k, out in enumerate(outs):
        rows = []
        for row in range(z.rows):
            first = (band ^ k) * z.rows + row
            at = pl.ds(first, z.columns, stride=z.height)
            rows.append(
                jnp.concatenate([image[g, at][:, :n] for g, (_, n) in enumerate(groups)], axis=1)
            )
        pack(z, out, jnp.concatenate(rows, axis=0))


def rows_kernel(z, *refs):
    blocks, (out_hbm, image, block_image, out_ref, sems) = refs[:-5], refs[-5:]
    band = lax.axis_index("band")

    def put(row, lane, piece):
        rows, lanes = piece.shape
        block_image[row : row + rows, lane : lane + lanes] = piece

    for k, block in enumerate(blocks):
        start = pl.multiple_of((band ^ k) * z.columns, 8)
        unpack(z, z.rows * z.columns, block[...].astype(F32), put)
        for row in range(z.rows):
            image[row, pl.ds(start, z.columns)] = block_image[
                row * z.columns : (row + 1) * z.columns
            ]
    copies = []
    for row in range(z.rows):
        out_ref[row] = image[row].T.astype(BF16)
        copies.append(pltpu.make_async_copy(out_ref.at[row], out_hbm.at[row], sems.at[row]))
        copies[-1].start()
    for copy in copies:
        copy.wait()


def over_bands(blocks):
    moved = [blocks[0]]
    for k, block in enumerate(blocks):
        if k:
            moved.append(exchange(block, "band", k))
    return moved


def gather(cells):
    cores = lax.axis_size("chan")
    near, far = [cells], []
    for k in range(1, cores):
        near.append(exchange(cells, "chan", k))
    chips = []
    for k in range(1, lax.axis_size("section")):
        chips.append(exchange(cells, "section", k))
    for chip in chips:
        for k in range(1, cores):
            far.append(exchange(chip, "chan", k))
    names = (
        tuple(range(cores)),
        tuple(at * cores for at in range(1, len(chips) + 1)),
        tuple(at * cores + k for at in range(1, len(chips) + 1) for k in range(1, cores)),
    )
    return list(zip(names, (near, chips, far)))


def together(received):
    return tuple(sum((list(part) for part in parts), []) for parts in zip(*received))


def late_together(received):
    near, *others = received
    return [near, together(others)]


def per_device(latent, control_hint, cw1, cb1, cw2, cb2, mw1, mb1, mw2, mb2, dw1, db1, dw2, db2):
    z = Sizes(latent)
    kernel = lambda f, *a: functools.partial(f, z, *a)
    groups = len(lane_groups(z))
    state_of = lambda trim: sds((z.kept(trim), z.per))
    message = lambda trim: z.packed(z.kept(trim))

    raw = (z.rows, z.per, z.width)
    blocks = pl.pallas_call(
        kernel(split_kernel),
        out_shape=[sds(z.packed(2 * z.rows * z.wide))] * z.bands,
        in_specs=[pl.BlockSpec(memory_space=pltpu.HBM)] * 2,
        out_specs=whole(z.bands),
        scratch_shapes=[pltpu.VMEM(raw, BF16)] * 2
        + [
            pltpu.VMEM((2, z.rows, z.width + 2 * LAYERS, z.per), F32),
            pltpu.SemaphoreType.DMA((2,)),
        ],
        compiler_params=pltpu.CompilerParams(vmem_limit_bytes=4 << 20),
    )(in_hbm(latent.swapaxes(1, 2)), in_hbm(control_hint.swapaxes(1, 2)))
    blocks = over_bands(blocks)
    cw1, mw1, mw2 = load(cw1, mw1, mw2)
    joined = []
    for t in range(2):
        joined.append(
            call(
                kernel(join_kernel, t),
                [state_of(0), sds(message(0))],
                *blocks,
                scratch=[
                    pltpu.VMEM((groups, z.cells, LANES), F32),
                    pltpu.VMEM((groups, 2 * z.rows * z.wide, LANES), F32),
                ],
            )
        )
    states = [state for state, _ in joined]
    control, main = [act for _, act in joined]

    def convolution(
        step, received, w, base, outs=None, end=None, rest=(), late=(), extra=(), drop=0
    ):
        received = [(names, pieces) for names, pieces in received if names]
        sums = ()
        total = sds((z.kept(step + 1 + drop), z.per), F32)
        for at, (names, pieces) in enumerate(received):
            ends = at == len(received) - 1
            sums += late if ends else ()
            result = call(
                kernel(block_kernel, step, drop, base, names, len(sums), end if ends else None),
                outs if ends and end else total,
                *pieces,
                *sums,
                w,
                *(rest if ends else ()),
                scratch=(list(extra) if ends else [])
                + [pltpu.VMEM((z.kept(step), len(names) * z.span), BF16)],
                flops=2 * 9 * z.cells * z.per * z.per * len(names),
            )
            sums = (result,)
        return result

    for step, (cw, cb, mw, mb) in enumerate(((cw1, cb1, mw1, mb1), (cw2, cb2, mw2, mb2))):
        outs = [state_of(step + 1), sds(message(step + 1))]
        received = gather(control)
        rest = (states[0], cb)
        if step == 0:
            states[0], control = convolution(step, received, cw, 0, outs, close_layer, rest)
        else:
            control = convolution(step, received, cw, 0, outs[1], close_control, rest)
        received = late_together(gather(main))
        rest = (states[1], mb)
        states[1], main = convolution(step, received, mw, 0, outs, close_layer, rest)
    skip = gather(control)
    first = convolution(2, late_together(skip), dw1, z.depth)
    outs = [state_of(3), sds(message(3))]
    rest = (states[1], db1)
    state, act = convolution(2, gather(main), dw1, 0, outs, close_layer, rest, late=(first,))
    every = together(skip)
    part = convolution(2, [every], dw2, z.depth, drop=1)
    blocks = convolution(
        3,
        gather(act),
        dw2,
        0,
        [sds(z.packed(z.rows * z.columns))] * z.bands,
        close_image,
        (state, db2),
        late=(part,),
        extra=[pltpu.VMEM((groups, z.kept(LAYERS), LANES), F32)],
    )
    blocks = over_bands(blocks)
    out = pl.pallas_call(
        kernel(rows_kernel),
        out_shape=sds(raw),
        in_specs=whole(z.bands),
        out_specs=pl.BlockSpec(memory_space=pltpu.HBM),
        scratch_shapes=[
            pltpu.VMEM((z.rows, z.width, z.per), F32),
            pltpu.VMEM((z.rows * z.columns, z.per), F32),
            pltpu.VMEM(raw, BF16),
            pltpu.SemaphoreType.DMA((z.rows,)),
        ],
        compiler_params=pltpu.CompilerParams(vmem_limit_bytes=4 << 20),
    )(*blocks)
    return out.swapaxes(1, 2)


def solution(mesh):
    image = P(("groups", "band"), None, CHANNEL_AXES)
    kernel = P(None, None, CHANNEL_AXES, None)
    bias = P(CHANNEL_AXES)

    return jax.shard_map(
        per_device,
        mesh=mesh,
        in_specs=(image, image) + (kernel, bias) * 6,
        out_specs=image,
        check_vma=False,
    )
```
